32 devices in a mesh: ctx: 16 (over z, y, core), fsdp: 2 (over x).
Axes of the slice: x: 2, y: 2, z: 4, core: 2. Of those that a mesh axis runs over, the one named last changes fastest.
Arguments:
- hidden_in: bfloat16 [2, 2048, 1024], P('fsdp', 'ctx'), may hold values from -6 to 6
- block_order: int32 [2, 32], P('fsdp'), may hold values from 0 to 31, as said below
- segment_ids: int32 [2, 2048], P('fsdp'), may hold values from 0 to 5, never falling along the last dimension, each value on 1 to 1024 neighbouring positions
- cotangent: bfloat16 [2, 2048, 1024], P('fsdp', 'ctx'), may hold values from -6 to 6
- attn_gain: bfloat16 [1024], P('fsdp'), may hold values from 0.5 to 1.5
- query_key_value_weight: bfloat16 [1024, 2048], P('fsdp'), may hold values from -0.1875 to 0.1875
- w_out: bfloat16 [1024, 1024], P('fsdp'), may hold values from -0.75 to 0.75
- ffn_gain: bfloat16 [1024], P('fsdp'), may hold values from 0.5 to 1.5
- w_router: bfloat16 [1024, 32], P('fsdp'), may hold values from -0.09375 to 0.09375
- routes: int32 [2, 2048, 8], P('fsdp', 'ctx'), may hold values from 0 to 31, all different within a row; in each aligned block of 128 rows (0 to 127, 128 to 255, ..., all dimensions but the last counted through in order) at most 48 rows name the same one
- expert_in: bfloat16 [32, 1024, 1024], P('fsdp', 'ctx'), may hold values from -0.1875 to 0.1875
- expert_out: bfloat16 [32, 512, 1024], P('fsdp', 'ctx'), may hold values from -1 to 1
Outputs:
- hidden_out: bfloat16 [2, 2048, 1024], P('fsdp', 'ctx')
- grad_in: float32 [2, 2048, 1024], P('fsdp', 'ctx')
- grad_attn_gain: float32 [1024], P('fsdp')
- grad_w_qkv: float32 [1024, 2048], P('fsdp')
- grad_w_out: float32 [1024, 1024], P('fsdp')
- grad_ffn_gain: float32 [1024], P('fsdp')
- grad_router: float32 [1024, 32], P('fsdp')
- grad_expert_in: float32 [32, 1024, 1024], P('fsdp', 'ctx')
- grad_expert_out: float32 [32, 512, 1024], P('fsdp', 'ctx')
The draws below stay inside these ranges and needn't reach their ends.
Inputs may be any that keep to these rules, and one draw needn't show every extreme that they name: `routes`: in the rows of one device no expert is named by more than 48 rows; some expert is named by exactly 48 rows on some devices. `segment_ids`: document numbers never fall along positions; a document holds 1 to 1024 positions, one exactly 1024. `block_order`: each row names every number of 0 to 31 once; storage blocks 2 k and 2 k + 1 hold position blocks p and 31 - p for some p < 16.
All inputs are finite; a program needn't handle non-finite values.
Results may differ from the reference program's by a relative error of at most 0.018.
Values may be sent and summed in bfloat16 or wider, within the bound.
No kernel may reach another device: no remote copies, remote signals or barrier semaphores. Data moves between devices by JAX's collectives and lax.ppermute only.
A program may use at most 192 MiB of HBM per device.

```python
import math
import jax
import jax.numpy as jnp
import numpy as np
from jax import lax

MODEL_WIDTH = 1024
QUERY_HEADS = 16
KEY_VALUE_HEADS = 8
HEAD_SIZE = 64
E = 32
TOPK = 8
F = 512
TOK_DEV = 128
PACKED_TOKENS = 2048
SEQS = 2
BLOCKS = 32
MOST = 48
CAP = 576
N_CTX = 16


def draw_block_order(key, part):
    seeds = jax.random.split(key, SEQS)

    def deal(seed_key):
        lower = jax.random.permutation(seed_key, BLOCKS // 2).astype(jnp.int32)
        upper = BLOCKS - 1 - lower
        return jnp.stack([lower, upper], axis=1).reshape(-1)
    return jax.vmap(deal)(seeds).astype(jnp.int32)


def level_of(key, dims, cuts, least, largest):
    gain = 1.0
    for dim, blocks in cuts:
        steps = jax.random.uniform(jax.random.fold_in(jax.random.fold_in(key, 6), dim), (blocks,), jnp.float32, least / len(cuts), largest / len(cuts))
        gain = gain * jnp.repeat(jnp.exp(steps), dims[dim] // blocks).reshape((-1,) + (1,) * (len(dims) - 1 - dim))
    return gain


def length_profile(count, total, limit, slope):
    loads = [(1 << 20) // math.isqrt(rank ** slope) + 1 for rank in range(2, count + 1)]
    spare, counts = total - limit - (count - 1), [1] * (count - 1)
    while spare > 0:
        free = [i for i in range(count - 1) if counts[i] < limit]
        mass, left = sum([loads[i] for i in free]), spare
        for i in free:
            extra = min(limit - counts[i], max(1, left * loads[i] // mass), spare)
            counts[i] = counts[i] + extra
            spare = spare - extra
    return np.array([limit] + counts)


def uneven_parts(key, number_of, total, reach, slope):
    if number_of == 2:
        one = jax.random.randint(key, (), max(1, total - reach), min(reach, total - 1) + 1)
        return jnp.stack([one, total - one])
    sizes = jnp.asarray(length_profile(number_of, total, reach, slope), jnp.int32)
    twos = (number_of - 1) // 2
    donor, sink = sizes[1:1 + 2 * twos:2], sizes[2:2 + 2 * twos:2]
    margin = jnp.minimum(donor - 1, reach - sink)
    shifted = jax.random.randint(jax.random.fold_in(key, 1), (twos,), 0, 1 << 20) % (margin + 1)
    sizes = sizes.at[1:1 + 2 * twos:2].set(donor - shifted).at[2:2 + 2 * twos:2].set(sink + shifted)
    return sizes[jax.random.permutation(jax.random.fold_in(key, 2), number_of)]


def assign_block(key, own, number, rows, count, top, most, skew):
    ranking = jax.random.permutation(key, count)
    packed, common = portions_of(count, rows * top, most, skew, True), portions_of(count, rows * top, most, skew, False)
    places = jnp.arange(count)

    def named(lengths, rotation):
        used = int((lengths > 0).sum())
        fixed = max(1, used // 4)
        shifted = fixed + (places - fixed + rotation * (used - fixed)) % max(1, count - fixed)
        return jnp.zeros((count,), jnp.int32).at[ranking[jnp.where(places < fixed, places, shifted)]].set(jnp.asarray(lengths, jnp.int32))

    lengths = jnp.where(number % 4 == 0, named(packed, number // 4), named(common, number - number // 4 - 1))
    mixed = jax.random.permutation(jax.random.fold_in(own, 3), count)
    source_of, receiver = mixed[0:count // 2 * 2:2], mixed[1:count // 2 * 2:2]
    room = jnp.minimum(lengths[source_of] - 1, most - lengths[receiver]) // 2
    room = jnp.where((source_of == ranking[0]) | (receiver == ranking[0]) | (lengths[receiver] == 0), 0, jnp.maximum(room, 0))
    shifted = jax.random.randint(jax.random.fold_in(own, 4), (count // 2,), 0, 1 << 20) % (room + 1)
    lengths = lengths.at[source_of].add(-shifted).at[receiver].add(shifted)
    items = jnp.searchsorted(jnp.cumsum(lengths), jnp.arange(rows * top), side="right").astype(jnp.int32)
    table = items.reshape(top, rows).T
    table = table[jax.random.permutation(jax.random.fold_in(own, 1), rows)]
    rotation = jax.random.randint(jax.random.fold_in(own, 2), (rows, 1), 0, top)
    return jnp.take_along_axis(table, (jnp.arange(top)[None, :] + rotation) % top, axis=1)


def portions_of(amount, total, bound, slope, full):
    loads = [(1 << 20) // math.isqrt(rank ** slope) + 1 for rank in range(1, amount + 1)]
    largest = bound if full else min(bound, max(-(-total // amount), total * loads[0] // sum(loads)))
    least = 1 if total - largest >= amount - 1 else 0
    counts, surplus = [largest] + [least] * (amount - 1), total - largest - least * (amount - 1)
    while surplus > 0:
        free = [i for i in range(1, amount) if counts[i] < largest] or [i for i in range(1, amount) if counts[i] < bound]
        mass, remaining = sum([loads[i] for i in free]), surplus
        for i in free:
            more = min(bound - counts[i], max(1, remaining * loads[i] // mass), surplus)
            counts[i] = counts[i] + more
            surplus = surplus - more
    return np.array(counts)


def gaussian(key, dims, spread, bound, cuts=(), held_as=jnp.bfloat16):
    array = jax.random.normal(key, dims, jnp.float32) * spread
    if len(cuts) > 0:
        array = level_of(key, dims, cuts, -0.22, 0.18) * array
    return jnp.clip(array, min=-bound, max=bound).astype(held_as)


def setup_inputs(seed: int = 0) -> dict:
    streams_of = jax.random.split(jax.random.key(seed), 13)
    hidden_in = gaussian(streams_of[0], (SEQS, PACKED_TOKENS, MODEL_WIDTH), 1.0, 6.0, ((0, 2), (1, 16)))
    block_order = draw_block_order(jax.random.fold_in(streams_of[12], 71), 0)
    segment_ids = jax.vmap(lambda own: jnp.searchsorted(jnp.cumsum(uneven_parts(own, 4 + PACKED_TOKENS // 1024, PACKED_TOKENS, PACKED_TOKENS // 2, 2)), jnp.arange(PACKED_TOKENS), side="right"))(jax.random.split(streams_of[2], SEQS)).reshape((SEQS, PACKED_TOKENS)).astype(jnp.int32)
    cotangent = gaussian(streams_of[3], (SEQS, PACKED_TOKENS, MODEL_WIDTH), 1.0, 6.0, ((0, 2), (1, 16)))
    attn_gain = jnp.clip(1.0 + 0.1 * jax.random.normal(streams_of[4], (MODEL_WIDTH,), jnp.float32), 0.5, 1.5).astype(jnp.bfloat16)
    query_key_value_weight = gaussian(streams_of[5], (MODEL_WIDTH, (QUERY_HEADS + 2 * KEY_VALUE_HEADS) * HEAD_SIZE), MODEL_WIDTH ** -0.5, 0.1875, ((0, 2),))
    w_out = gaussian(streams_of[6], (QUERY_HEADS * HEAD_SIZE, MODEL_WIDTH), (QUERY_HEADS * HEAD_SIZE // 16) ** -0.5, 0.75, ((0, 2),))
    ffn_gain = jnp.clip(1.0 + 0.1 * jax.random.normal(streams_of[7], (MODEL_WIDTH,), jnp.float32), 0.5, 1.5).astype(jnp.bfloat16)
    w_router = gaussian(streams_of[8], (MODEL_WIDTH, E), (4 * MODEL_WIDTH) ** -0.5, 0.09375, ((0, 2),))
    routes_keys = jax.random.split(jax.random.fold_in(streams_of[9], 1), SEQS * PACKED_TOKENS // TOK_DEV)
    routes_turns = jax.random.permutation(jax.random.fold_in(streams_of[9], 3), SEQS * PACKED_TOKENS // TOK_DEV)
    routes = jax.vmap(lambda own, number: assign_block(jax.random.fold_in(streams_of[9], 2), own, number, TOK_DEV, E, TOPK, MOST, 1))(routes_keys, routes_turns).reshape((SEQS, PACKED_TOKENS, TOPK))
    expert_in = gaussian(streams_of[10], (E, MODEL_WIDTH, 2 * F), MODEL_WIDTH ** -0.5, 0.1875, ((0, 2), (1, 16)))
    expert_out = gaussian(streams_of[11], (E, F, MODEL_WIDTH), (F // 16) ** -0.5, 1.0, ((0, 2), (1, 16)))
    return dict(hidden_in=hidden_in, block_order=block_order, segment_ids=segment_ids, cotangent=cotangent, attn_gain=attn_gain, query_key_value_weight=query_key_value_weight, w_out=w_out, ffn_gain=ffn_gain, w_router=w_router, routes=routes, expert_in=expert_in, expert_out=expert_out)


@jax.custom_vjp
def lower_limit(v):
    return lax.optimization_barrier(v.astype(jnp.bfloat16)).astype(jnp.float32)

@jax.custom_vjp
def low_back(v):
    return v

def low_keep(v):
    return (lower_limit(v), None)

def low_pass(kept, grad):
    return (grad,)

def back_keep(v):
    return (v, None)

def back_low(kept, grad):
    return (lower_limit(grad),)
lower_limit.defvjp(low_keep, low_pass)
low_back.defvjp(back_keep, back_low)
EPSILON = 1e-06
THETA = 10000.0
MASK_FILL_VALUE = -1e+30
HIGHEST = lax.Precision.HIGHEST

def product(left, right):
    return jnp.dot(left, right, precision=HIGHEST)

def rms_scale(value_rows):
    return lax.rsqrt(lax.optimization_barrier(jnp.mean(value_rows * value_rows, axis=-1, keepdims=True)) + EPSILON)

def rotate(value_rows):
    middle = value_rows.shape[-1] // 2
    return jnp.concatenate([-value_rows[..., middle:], value_rows[..., :middle]], axis=-1)

def rope_tables(position):
    steps = jnp.arange(HEAD_SIZE // 2, dtype=jnp.float32)
    frequency = jnp.power(THETA, -2.0 * steps / HEAD_SIZE)
    angle = position.astype(jnp.float32)[:, None] * frequency[None, :]
    angle = jnp.concatenate([angle, angle], axis=-1)
    return (jnp.cos(angle), jnp.sin(angle))

def sequence_forward(inputs, gain_one, qkv_weight, out_weight, gain_two, router_weight, expert_up, expert_down, position, document, route):
    query_group = QUERY_HEADS // KEY_VALUE_HEADS
    query_total_width = QUERY_HEADS * HEAD_SIZE
    key_total_width = KEY_VALUE_HEADS * HEAD_SIZE
    scale = 1.0 / math.sqrt(HEAD_SIZE)
    h_one = lower_limit(inputs * rms_scale(inputs) * gain_one)
    projected_rows = low_back(product(h_one, qkv_weight))
    cosine, sine = rope_tables(position)
    query_matrix = projected_rows[:, :query_total_width].reshape(PACKED_TOKENS, QUERY_HEADS, HEAD_SIZE)
    key_rows = projected_rows[:, query_total_width:query_total_width + key_total_width].reshape(PACKED_TOKENS, KEY_VALUE_HEADS, HEAD_SIZE)
    value_rows = lower_limit(projected_rows[:, query_total_width + key_total_width:]).reshape(PACKED_TOKENS, KEY_VALUE_HEADS, HEAD_SIZE)
    query_matrix = lower_limit(query_matrix * cosine[:, None, :] + rotate(query_matrix) * sine[:, None, :])
    key_rows = lower_limit(key_rows * cosine[:, None, :] + rotate(key_rows) * sine[:, None, :])
    grouped_queries = query_matrix.reshape(PACKED_TOKENS, KEY_VALUE_HEADS, query_group, HEAD_SIZE)
    query_block = min(512, PACKED_TOKENS)

    def attend(start):
        block_queries = lax.dynamic_slice_in_dim(grouped_queries, start, query_block, 0)
        block_position = lax.dynamic_slice_in_dim(position, start, query_block, 0)
        block_document = lax.dynamic_slice_in_dim(document, start, query_block, 0)
        scores = low_back(jnp.einsum('qhgd,khd->hgqk', block_queries, key_rows, precision=HIGHEST) * scale)
        allowed = (block_document[:, None] == document[None, :]) & (position[None, :] <= block_position[:, None])
        scores = jnp.where(allowed[None, None], scores, MASK_FILL_VALUE)
        probs = lower_limit(jax.nn.softmax(scores, axis=-1))
        return jnp.einsum('hgqk,khd->qhgd', probs, value_rows, precision=HIGHEST)
    starts = jnp.arange(PACKED_TOKENS // query_block, dtype=jnp.int32) * query_block
    attended = lax.map(jax.checkpoint(attend), starts).reshape(PACKED_TOKENS, query_total_width)
    attended = low_back(lower_limit(attended))
    middle_state = inputs + low_back(product(attended, out_weight))
    h_two = lower_limit(middle_state * rms_scale(middle_state) * gain_two)
    logits = product(h_two, router_weight)
    gates = jax.nn.softmax(jnp.take_along_axis(logits, route, axis=1), axis=-1)
    flat = route.reshape(-1)
    onehot = (flat[:, None] == jnp.arange(E, dtype=jnp.int32)[None, :]).astype(jnp.int32)
    slot = lax.optimization_barrier(jnp.sum((jnp.cumsum(onehot, axis=0) - onehot) * onehot, axis=1))
    kept = slot < CAP
    target = jnp.where(kept, flat * CAP + slot, E * CAP)
    token = jnp.arange(PACKED_TOKENS * TOPK, dtype=jnp.int32) // TOPK
    copies = low_back(h_two[token])
    buffer = jnp.zeros((E * CAP, MODEL_WIDTH), jnp.float32).at[target].set(copies, mode='drop').reshape(E, CAP, MODEL_WIDTH)
    before = low_back(jnp.einsum('ecd,edf->ecf', buffer, expert_up, precision=HIGHEST))
    activation = lower_limit(jax.nn.silu(before[..., :F]) * before[..., F:])
    results = low_back(lower_limit(jnp.einsum('ecf,efd->ecd', activation, expert_down, precision=HIGHEST))).reshape(E * CAP, MODEL_WIDTH)
    returned = results[jnp.minimum(target, E * CAP - 1)] * kept[:, None].astype(jnp.float32)
    mixture = lax.optimization_barrier(jnp.sum(gates[..., None] * returned.reshape(PACKED_TOKENS, TOPK, MODEL_WIDTH), axis=1))
    return middle_state + mixture

def reference(hidden_in, block_order, segment_ids, cotangent, attn_gain, query_key_value_weight, w_out, ffn_gain, w_router, routes, expert_in, expert_out):
    half_block = PACKED_TOKENS // (2 * N_CTX)
    offsets = jnp.arange(half_block, dtype=jnp.int32)
    positions = [(block_order[sequence][:, None] * half_block + offsets[None, :]).reshape(-1) for sequence in range(SEQS)]

    def forward(inputs, gain_one, qkv_weight, out_weight, gain_two, router_weight, expert_up, expert_down):
        outputs = []
        for sequence in range(SEQS):
            position = positions[sequence]
            document = segment_ids[sequence][position]
            outputs.append(sequence_forward(inputs[sequence], gain_one, qkv_weight, out_weight, gain_two, router_weight, expert_up, expert_down, position, document, routes[sequence]))
        return jnp.stack(outputs)
    result, pullback = jax.vjp(forward, hidden_in.astype(jnp.float32), attn_gain.astype(jnp.float32), query_key_value_weight.astype(jnp.float32), w_out.astype(jnp.float32), ffn_gain.astype(jnp.float32), w_router.astype(jnp.float32), expert_in.astype(jnp.float32), expert_out.astype(jnp.float32))
    grads = pullback(cotangent.astype(jnp.float32))
    return (result.astype(jnp.bfloat16), grads[0], grads[1], grads[2], grads[3], grads[4], grads[5], grads[6], grads[7])
```

```python
import math

import jax
import jax.numpy as jnp
from jax import lax
from jax.experimental import pallas as pl
from jax.experimental.pallas import tpu as pltpu
from jax.sharding import Mesh
from jax.sharding import PartitionSpec as P

QUERY_HEADS = 16
KEY_VALUE_HEADS = 8
HEAD_SIZE = 64
E = 32
TOPK = 8
F = 512
MOST = 48


EPSILON = 1e-06
THETA = 10000.0
MASK_FILL_VALUE = -1e30
HIGHEST = lax.Precision.HIGHEST


def carried_in(value, axis, combine, identity):
    length, mine = (lax.axis_size(axis), lax.axis_index(axis))
    everything = lax.all_gather(value, axis)
    start = jnp.broadcast_to(jnp.asarray(identity, value.dtype), value.shape)

    def turn(k, before):
        reached = k < mine
        new = combine(before, everything[k])
        return jnp.where(reached, new, before)

    return lax.fori_loop(0, length, turn, start)


def rms_scale(value_rows):
    return lax.rsqrt(jnp.mean(value_rows * value_rows, axis=-1, keepdims=True) + EPSILON)


def rotate(value_rows):
    middle = value_rows.shape[-1] // 2
    return jnp.concatenate([-value_rows[..., middle:], value_rows[..., :middle]], axis=-1)


def rotate_back(value_rows):
    middle = value_rows.shape[-1] // 2
    return jnp.concatenate([value_rows[..., middle:], -value_rows[..., :middle]], axis=-1)


def rope_tables(position):
    steps = jnp.arange(HEAD_SIZE // 2, dtype=jnp.float32)
    frequency = jnp.power(THETA, -2.0 * steps / HEAD_SIZE)
    angle = position.astype(jnp.float32)[:, None] * frequency[None, :]
    angle = jnp.concatenate([angle, angle], axis=-1)
    return (jnp.cos(angle), jnp.sin(angle))


def contract_rows(left, right):
    return lax.dot_general(
        left, right, (((0,), (0,)), ((), ())), preferred_element_type=jnp.float32
    )


def contract_columns(left, right):
    return lax.dot_general(
        left, right, (((1,), (1,)), ((), ())), preferred_element_type=jnp.float32
    )


def own_rows(total, rank, count):
    share = total.shape[0] // count
    return lax.dynamic_slice_in_dim(total, rank * share, share, 0)


def general_shards(
    hidden_in,
    block_order,
    segment_ids,
    cotangent,
    attn_gain,
    query_key_value_weight,
    w_out,
    ffn_gain,
    w_router,
    routes,
    expert_in,
    expert_out,
):
    count_of_rows = hidden_in.shape[1]
    width = hidden_in.shape[2]
    ctx_count = lax.axis_size("ctx")
    fsdp_count = lax.axis_size("fsdp")
    sequence_length = count_of_rows * ctx_count
    half_block = count_of_rows // 2
    capacity = sequence_length * TOPK * 9 // (8 * E)
    query_total_width = QUERY_HEADS * HEAD_SIZE
    key_total_width = KEY_VALUE_HEADS * HEAD_SIZE
    query_group = QUERY_HEADS // KEY_VALUE_HEADS
    scale = 1.0 / math.sqrt(HEAD_SIZE)
    key_block_rows = min(1024, sequence_length)
    block_count = sequence_length // key_block_rows
    pair_count = count_of_rows * TOPK
    gain_one, qkv_full, out_full, gain_two, router_full = (
        lax.all_gather(attn_gain, "fsdp", axis=0, tiled=True),
        lax.all_gather(query_key_value_weight, "fsdp", axis=0, tiled=True),
        lax.all_gather(w_out, "fsdp", axis=0, tiled=True),
        lax.all_gather(ffn_gain, "fsdp", axis=0, tiled=True),
        lax.all_gather(w_router, "fsdp", axis=0, tiled=True),
    )
    up_full, down_full = (
        lax.all_gather(expert_in, "ctx", axis=1, tiled=True),
        lax.all_gather(expert_out, "ctx", axis=1, tiled=True),
    )
    key_position = (
        block_order[0][:, None] * half_block + jnp.arange(half_block, dtype=jnp.int32)[None, :]
    ).reshape(-1)
    key_document = segment_ids[0][key_position]
    first_row = lax.axis_index("ctx") * count_of_rows
    query_position = lax.dynamic_slice_in_dim(key_position, first_row, count_of_rows, 0)
    query_document = lax.dynamic_slice_in_dim(key_document, first_row, count_of_rows, 0)
    inputs = hidden_in[0].astype(jnp.float32)
    grad_out = cotangent[0].astype(jnp.float32)
    scale_one = rms_scale(inputs)
    norm_one = inputs * scale_one
    gain_one_f = gain_one.astype(jnp.float32)
    h_one = (norm_one * gain_one_f).astype(jnp.bfloat16)
    projected_rows = jnp.dot(h_one, qkv_full, preferred_element_type=jnp.float32)
    cosine, sine = rope_tables(query_position)
    query_raw = projected_rows[:, :query_total_width].reshape(count_of_rows, QUERY_HEADS, HEAD_SIZE)
    unrotated_key = projected_rows[
        :, query_total_width : query_total_width + key_total_width
    ].reshape(count_of_rows, KEY_VALUE_HEADS, HEAD_SIZE)
    query_matrix = (query_raw * cosine[:, None, :] + rotate(query_raw) * sine[:, None, :]).astype(
        jnp.bfloat16
    )
    key_rows = (
        unrotated_key * cosine[:, None, :] + rotate(unrotated_key) * sine[:, None, :]
    ).astype(jnp.bfloat16)
    value_rows = projected_rows[:, query_total_width + key_total_width :].astype(jnp.bfloat16)
    key_value_local = jnp.concatenate(
        [key_rows.reshape(count_of_rows, key_total_width), value_rows], axis=1
    )
    key_value_all = lax.all_gather(key_value_local, "ctx", axis=0, tiled=True)
    grouped_queries = query_matrix.reshape(count_of_rows, KEY_VALUE_HEADS, query_group, HEAD_SIZE)
    block_number = jnp.arange(block_count, dtype=jnp.int32)

    def block_keys(source, index):
        current_rows = lax.dynamic_slice_in_dim(source, index * key_block_rows, key_block_rows, 0)
        block_key_rows = current_rows[:, :key_total_width].reshape(
            key_block_rows, KEY_VALUE_HEADS, HEAD_SIZE
        )
        block_value_rows = current_rows[:, key_total_width:].reshape(
            key_block_rows, KEY_VALUE_HEADS, HEAD_SIZE
        )
        block_position = lax.dynamic_slice_in_dim(
            key_position, index * key_block_rows, key_block_rows, 0
        )
        block_document = lax.dynamic_slice_in_dim(
            key_document, index * key_block_rows, key_block_rows, 0
        )
        allowed = (query_document[:, None] == block_document[None, :]) & (
            block_position[None, :] <= query_position[:, None]
        )
        return (block_key_rows, block_value_rows, allowed)

    def scores_of(block_key_rows, allowed):
        scores = (
            jnp.einsum(
                "qhgd,khd->hgqk",
                grouped_queries,
                block_key_rows,
                preferred_element_type=jnp.float32,
            )
            * scale
        )
        return jnp.where(allowed[None, None], scores, MASK_FILL_VALUE)

    def max_sum(carry, index):
        top, total = carry
        block_key_rows, block_value_rows, allowed = block_keys(key_value_all, index)
        scores = scores_of(block_key_rows, allowed)
        new_top = jnp.maximum(top, jnp.max(scores, axis=-1))
        weights = jnp.where(allowed[None, None], jnp.exp(scores - new_top[..., None]), 0.0)
        total = total * jnp.exp(top - new_top) + jnp.sum(weights, axis=-1)
        return ((new_top, total), None)

    upper_start = jnp.full(
        (KEY_VALUE_HEADS, query_group, count_of_rows), MASK_FILL_VALUE, jnp.float32
    )
    overall_start = jnp.zeros((KEY_VALUE_HEADS, query_group, count_of_rows), jnp.float32)
    (top, total), unused = lax.scan(max_sum, (upper_start, overall_start), block_number)
    log_total = top + jnp.log(total)

    def weighted_values(accum, index):
        block_key_rows, block_value_rows, allowed = block_keys(key_value_all, index)
        scores = scores_of(block_key_rows, allowed)
        probs = jnp.where(allowed[None, None], jnp.exp(scores - log_total[..., None]), 0.0).astype(
            jnp.bfloat16
        )
        return (
            accum
            + jnp.einsum(
                "hgqk,khd->qhgd", probs, block_value_rows, preferred_element_type=jnp.float32
            ),
            None,
        )

    attended_f, unused = lax.scan(
        weighted_values,
        jnp.zeros((count_of_rows, KEY_VALUE_HEADS, query_group, HEAD_SIZE), jnp.float32),
        block_number,
    )
    attended = attended_f.reshape(count_of_rows, query_total_width).astype(jnp.bfloat16)
    middle_state = inputs + jnp.dot(attended, out_full, preferred_element_type=jnp.float32)
    scale_two = rms_scale(middle_state)
    norm_two = middle_state * scale_two
    gain_two_f = gain_two.astype(jnp.float32)
    h_two = (norm_two * gain_two_f).astype(jnp.bfloat16)
    logits = jnp.dot(h_two, router_full, preferred_element_type=jnp.float32)
    route = routes[0]
    gates = jax.nn.softmax(jnp.take_along_axis(logits, route, axis=1), axis=-1)
    flat = route.reshape(-1)
    onehot = (flat[:, None] == jnp.arange(E, dtype=jnp.int32)[None, :]).astype(jnp.int32)
    rank = jnp.sum((jnp.cumsum(onehot, axis=0) - onehot) * onehot, axis=1)
    counts = jnp.sum(onehot, axis=0)

    def add_counts(earlier, later):
        return earlier + later

    offsets = carried_in(counts, "ctx", add_counts, jnp.zeros((E,), jnp.int32))
    slot = jnp.sum(onehot * offsets[None, :], axis=1) + rank
    kept = slot < capacity
    target = jnp.where(kept, flat * MOST + rank, E * MOST)
    safe_target = jnp.minimum(target, E * MOST - 1)
    keep_float = kept.astype(jnp.float32)[:, None]
    token = jnp.arange(pair_count, dtype=jnp.int32) // TOPK
    send_rows = (
        jnp.zeros((E * MOST, width), jnp.bfloat16)
        .at[target]
        .set(h_two[token], mode="drop")
        .reshape(E, MOST, width)
    )
    received = lax.all_to_all(send_rows, "fsdp", split_axis=0, concat_axis=1, tiled=True)
    before = jnp.einsum("erd,edf->erf", received, up_full, preferred_element_type=jnp.float32)
    gate_pre = before[..., :F]
    up_pre = before[..., F:]
    sigma = jax.nn.sigmoid(gate_pre)
    activation = (gate_pre * sigma * up_pre).astype(jnp.bfloat16)
    expert_result = jnp.einsum(
        "erf,efd->erd", activation, down_full, preferred_element_type=jnp.float32
    ).astype(jnp.bfloat16)
    returned = lax.all_to_all(
        expert_result, "fsdp", split_axis=1, concat_axis=0, tiled=True
    ).reshape(E * MOST, width)
    pair_result = (returned[safe_target].astype(jnp.float32) * keep_float).reshape(
        count_of_rows, TOPK, width
    )
    mixture = jnp.sum(gates[..., None] * pair_result, axis=1)
    hidden_out = (middle_state + mixture).astype(jnp.bfloat16)
    grad_pair = (
        (gates[..., None] * grad_out[:, None, :]).reshape(pair_count, width) * keep_float
    ).astype(jnp.bfloat16)
    grad_gates = jnp.sum(grad_out[:, None, :] * pair_result, axis=-1)
    grad_chosen = gates * (grad_gates - jnp.sum(gates * grad_gates, axis=-1, keepdims=True))
    chosen_table = (route[..., None] == jnp.arange(E, dtype=jnp.int32)[None, None, :]).astype(
        jnp.float32
    )
    grad_logits = jnp.sum(grad_chosen[..., None] * chosen_table, axis=1)
    grad_router_part = lax.dot_general(
        h_two.astype(jnp.float32), grad_logits, (((0,), (0,)), ((), ())), precision=HIGHEST
    )
    grad_h_two = lax.dot_general(
        grad_logits, router_full.astype(jnp.float32), (((1,), (1,)), ((), ())), precision=HIGHEST
    )
    send_grads = (
        jnp.zeros((E * MOST, width), jnp.bfloat16)
        .at[target]
        .set(grad_pair, mode="drop")
        .reshape(E, MOST, width)
    )
    grad_received = lax.all_to_all(send_grads, "fsdp", split_axis=0, concat_axis=1, tiled=True)
    grad_activation = jnp.einsum(
        "erd,efd->erf", grad_received, down_full, preferred_element_type=jnp.float32
    )
    grad_down = jnp.einsum(
        "erf,erd->efd", activation, grad_received, preferred_element_type=jnp.float32
    )
    grad_gate = grad_activation * up_pre * sigma * (1.0 + gate_pre * (1.0 - sigma))
    grad_up = grad_activation * gate_pre * sigma
    grad_pre = jnp.concatenate([grad_gate, grad_up], axis=-1).astype(jnp.bfloat16)
    grad_up_weight = jnp.einsum(
        "erd,erf->edf", received, grad_pre, preferred_element_type=jnp.float32
    )
    grad_copy = jnp.einsum(
        "erf,edf->erd", grad_pre, up_full, preferred_element_type=jnp.float32
    ).astype(jnp.bfloat16)
    grad_returned = lax.all_to_all(
        grad_copy, "fsdp", split_axis=1, concat_axis=0, tiled=True
    ).reshape(E * MOST, width)
    grad_h_two = grad_h_two + jnp.sum(
        (grad_returned[safe_target].astype(jnp.float32) * keep_float).reshape(
            count_of_rows, TOPK, width
        ),
        axis=1,
    )
    grad_expert_in, grad_expert_out = (
        lax.psum_scatter(
            grad_up_weight.astype(jnp.bfloat16), "ctx", scatter_dimension=1, tiled=True
        ).astype(jnp.float32),
        lax.psum_scatter(
            grad_down.astype(jnp.bfloat16), "ctx", scatter_dimension=1, tiled=True
        ).astype(jnp.float32),
    )
    grad_gain_two = jnp.sum(grad_h_two * norm_two, axis=0)
    scaled_two = grad_h_two * gain_two_f
    grad_mid = grad_out + scale_two * (
        scaled_two - norm_two * jnp.mean(scaled_two * norm_two, axis=-1, keepdims=True)
    )
    grad_branch = grad_mid.astype(jnp.bfloat16)
    grad_out_weight = contract_rows(attended, grad_branch)
    attended_gradient = contract_columns(grad_branch, out_full).astype(jnp.bfloat16)
    grouped_gradient = attended_gradient.reshape(
        count_of_rows, KEY_VALUE_HEADS, query_group, HEAD_SIZE
    )
    delta = jnp.transpose(
        jnp.sum(grouped_gradient.astype(jnp.float32) * attended_f, axis=-1), (1, 2, 0)
    )

    def block_gradients(query_accum, index):
        block_key_rows, block_value_rows, allowed = block_keys(key_value_all, index)
        scores = scores_of(block_key_rows, allowed)
        probs = jnp.where(allowed[None, None], jnp.exp(scores - log_total[..., None]), 0.0)
        grad_probs = jnp.einsum(
            "qhgd,khd->hgqk", grouped_gradient, block_value_rows, preferred_element_type=jnp.float32
        )
        grad_scores = (probs * (grad_probs - delta[..., None])).astype(jnp.bfloat16)
        query_accum = query_accum + jnp.einsum(
            "hgqk,khd->qhgd", grad_scores, block_key_rows, preferred_element_type=jnp.float32
        )
        grad_keys = (
            jnp.einsum(
                "hgqk,qhgd->khd", grad_scores, grouped_queries, preferred_element_type=jnp.float32
            )
            * scale
        )
        grad_values = jnp.einsum(
            "hgqk,qhgd->khd",
            probs.astype(jnp.bfloat16),
            grouped_gradient,
            preferred_element_type=jnp.float32,
        )
        joined = jnp.concatenate(
            [
                grad_keys.reshape(key_block_rows, key_total_width),
                grad_values.reshape(key_block_rows, key_total_width),
            ],
            axis=1,
        )
        return (query_accum, joined)

    grad_queries, grad_blocks = lax.scan(
        block_gradients,
        jnp.zeros((count_of_rows, KEY_VALUE_HEADS, query_group, HEAD_SIZE), jnp.float32),
        block_number,
    )
    key_value_gradient = lax.psum_scatter(
        grad_blocks.reshape(sequence_length, 2 * key_total_width).astype(jnp.bfloat16),
        "ctx",
        scatter_dimension=0,
        tiled=True,
    ).astype(jnp.float32)
    grad_queries = (grad_queries * scale).reshape(count_of_rows, QUERY_HEADS, HEAD_SIZE)
    local_key_gradient = key_value_gradient[:, :key_total_width].reshape(
        count_of_rows, KEY_VALUE_HEADS, HEAD_SIZE
    )
    grad_values_mine = key_value_gradient[:, key_total_width:]
    grad_query_pre = grad_queries * cosine[:, None, :] + rotate_back(
        grad_queries * sine[:, None, :]
    )
    grad_key_pre = local_key_gradient * cosine[:, None, :] + rotate_back(
        local_key_gradient * sine[:, None, :]
    )
    grad_projected = jnp.concatenate(
        [
            grad_query_pre.reshape(count_of_rows, query_total_width),
            grad_key_pre.reshape(count_of_rows, key_total_width),
            grad_values_mine,
        ],
        axis=1,
    ).astype(jnp.bfloat16)
    grad_qkv_weight = contract_rows(h_one, grad_projected)
    grad_h_one = contract_columns(grad_projected, qkv_full)
    grad_gain_one = jnp.sum(grad_h_one * norm_one, axis=0)
    scaled_one = grad_h_one * gain_one_f
    grad_inputs = grad_mid + scale_one * (
        scaled_one - norm_one * jnp.mean(scaled_one * norm_one, axis=-1, keepdims=True)
    )
    total_one, total_qkv, total_out, total_two, total_router = lax.psum(
        (grad_gain_one, grad_qkv_weight, grad_out_weight, grad_gain_two, grad_router_part),
        ("ctx", "fsdp"),
    )
    fsdp_rank = lax.axis_index("fsdp")
    share_one = own_rows(total_one, fsdp_rank, fsdp_count)
    share_qkv = own_rows(total_qkv, fsdp_rank, fsdp_count)
    share_out = own_rows(total_out, fsdp_rank, fsdp_count)
    share_two = own_rows(total_two, fsdp_rank, fsdp_count)
    share_router = own_rows(total_router, fsdp_rank, fsdp_count)
    return (
        hidden_out[None],
        grad_inputs[None],
        share_one,
        share_qkv,
        share_out,
        share_two,
        share_router,
        grad_expert_in,
        grad_expert_out,
    )


def general_solution(mesh):
    placed = (
        P("fsdp", "ctx", None),
        P("fsdp", None),
        P("fsdp", None),
        P("fsdp", "ctx", None),
        P("fsdp"),
        P("fsdp", None),
        P("fsdp", None),
        P("fsdp"),
        P("fsdp", None),
        P("fsdp", "ctx", None),
        P("fsdp", "ctx", None),
        P("fsdp", "ctx", None),
    )
    return jax.shard_map(
        general_shards,
        mesh=mesh,
        in_specs=placed,
        out_specs=(
            P("fsdp", "ctx", None),
            P("fsdp", "ctx", None),
            P("fsdp"),
            P("fsdp", None),
            P("fsdp", None),
            P("fsdp"),
            P("fsdp", None),
            P("fsdp", "ctx", None),
            P("fsdp", "ctx", None),
        ),
        check_vma=False,
    )


CTX = ("a", "b", "c", "d")
HALF = ("b", "c", "d", "f")
EVERY = ("a", "b", "c", "d", "f")
QUERY_BLOCK = 256
EXTRA = 128


def swap(value, axis):
    return lax.ppermute(value, axis, [(0, 1), (1, 0)])


def in_order(mine, other, axis, dim):
    first = lax.axis_index(axis) == 0
    return jnp.where(
        first, jnp.concatenate([mine, other], dim), jnp.concatenate([other, mine], dim)
    )


def join(value, axis, dim=0):
    return in_order(value, swap(value, axis), axis, dim)


def gather_ctx(parts, orders):
    held = [part[(None,) * 4] for part in parts]
    for step in range(4):
        others = [swap(held[i], orders[i][step]) for i in range(len(held))]
        held = [
            in_order(held[i], others[i], orders[i][step], CTX.index(orders[i][step]))
            for i in range(len(held))
        ]
    return [value.reshape((16,) + value.shape[4:]) for value in held]


def sum_everywhere(value):
    for axis in ("d", "f", "c", "b", "a"):
        value = value + swap(value, axis)
    return value


def exact_parts(value):
    high = lax.reduce_precision(value, 8, 7)
    rest = value - high
    middle = lax.reduce_precision(rest, 8, 7)
    return [part.astype(jnp.bfloat16) for part in (high, middle, rest - middle)]


def lane_of(shape):
    return lax.broadcasted_iota(jnp.int32, shape, 1)


def attention_forward(
    place, first_key, h_low, h_high, weight, cosine, sine, start,
    query_out, key_out, value_out, mixed_out, attended_out, value_t,
):
    rows = h_low.shape[0]
    block = QUERY_BLOCK
    pieces = block // 64

    def project(chunk, carry):
        storage = [
            pl.ds(pl.multiple_of(place[chunk * pieces + n] * 64, 64), 64) for n in range(pieces)
        ]
        low = jnp.concatenate([h_low[one, :] for one in storage], 0)
        high = jnp.concatenate([h_high[one, :] for one in storage], 0)
        here = pl.ds(pl.multiple_of(chunk * block, block), block)
        both = jnp.dot(low, weight[:512, :], preferred_element_type=jnp.float32) + jnp.dot(
            high, weight[512:, :], preferred_element_type=jnp.float32
        )
        pair = both[:, :128]
        values = both[:, 128:].astype(jnp.bfloat16)
        lane = lane_of((block, 128))
        turned = jnp.where(
            lane % 64 < 32, -pltpu.roll(pair, 96, 1), pltpu.roll(pair, 32, 1)
        )
        pair = pair * cosine[here, :] + turned * sine[here, :]
        pair = pair.astype(jnp.bfloat16).astype(jnp.float32)
        key_out[here, :] = jnp.where(lane >= 64, pair, 0.0).astype(jnp.bfloat16)
        query_out[here, :] = jnp.where(
            lane >= 64, pltpu.roll(pair, 64, 1) * (1.0 / math.sqrt(HEAD_SIZE)), 0.0
        ).astype(jnp.bfloat16)
        value_out[here, :] = values
        turned_values = jnp.transpose(values.astype(jnp.float32))
        ones = lax.broadcasted_iota(jnp.int32, (128, block), 0) == 64
        value_t[:, here] = jnp.where(ones, 1.0, turned_values).astype(jnp.bfloat16)
        return carry

    lax.fori_loop(0, rows // block, project, 0)

    def attend(number, carry):
        here = pl.ds(pl.multiple_of(number * block, block), block)
        queries = query_out[here, :]
        begin = start[:, here]
        query_at = lax.broadcasted_iota(jnp.int32, (block, block), 1) + number * block

        def turn(key_number, state):
            top, total = state
            there = pl.ds(pl.multiple_of(key_number * block, block), block)
            scores = lax.dot_general(
                key_out[there, :], queries, (((1,), (1,)), ((), ())),
                preferred_element_type=jnp.float32,
            )
            key_at = lax.broadcasted_iota(jnp.int32, (block, block), 0) + key_number * block
            allowed = (key_at >= begin) & (key_at <= query_at)
            scores = jnp.where(allowed, scores, MASK_FILL_VALUE)
            new_top = jnp.maximum(top, jnp.max(scores, axis=0, keepdims=True))
            weights = jnp.exp(scores - new_top).astype(jnp.bfloat16)
            total = total * jnp.exp(top - new_top) + jnp.dot(
                value_t[:, there], weights, preferred_element_type=jnp.float32
            )
            return new_top, total

        top, total = lax.fori_loop(
            first_key[number],
            number + 1,
            turn,
            (
                jnp.full((1, block), MASK_FILL_VALUE, jnp.float32),
                jnp.zeros((128, block), jnp.float32),
            ),
        )
        weight_sum = total[64:65, :]
        mixed = total * (1.0 / weight_sum)
        log_total = top + jnp.log(weight_sum)
        mixed_out[:64, here] = mixed[:64, :]
        mixed_out[64:72, here] = jnp.broadcast_to(log_total, (8, block))
        upright = jnp.transpose(mixed)[:, :64].astype(jnp.bfloat16)
        for n in range(pieces):
            rows_there = pl.ds(pl.multiple_of(place[number * pieces + n] * 64, 64), 64)
            attended_out[rows_there, :] = upright[n * 64 : (n + 1) * 64, :]
        return carry

    lax.fori_loop(0, rows // block, attend, 0)


def attention_backward(
    place, first_key, query, key, value, mixed, grad, cosine, sine, start,
    pair_out, value_out, key_t, pair_sum, value_sum,
):
    rows = query.shape[0]
    block = QUERY_BLOCK
    pieces = block // 64
    scale = 1.0 / math.sqrt(HEAD_SIZE)

    def prepare(chunk, carry):
        here = pl.ds(pl.multiple_of(chunk * block, block), block)
        turned = jnp.transpose(key[here, :].astype(jnp.float32))
        key_t[:, here] = turned[64:, :].astype(jnp.bfloat16)
        pair_sum[here, :] = jnp.zeros((block, 128), jnp.float32)
        value_sum[here, :] = jnp.zeros((block, 64), jnp.float32)
        return carry

    lax.fori_loop(0, rows // block, prepare, 0)

    def storage(number):
        return [
            pl.ds(pl.multiple_of(place[number * pieces + n] * 64, 64), 64) for n in range(pieces)
        ]

    def attend(number, carry):
        here = pl.ds(pl.multiple_of(number * block, block), block)
        queries = query[here, :]
        incoming = jnp.concatenate([grad[one, :] for one in storage(number)], 0)
        padded = jnp.concatenate([incoming, jnp.zeros((block, 64), jnp.bfloat16)], 1)
        incoming_t = jnp.transpose(padded.astype(jnp.float32))[:64, :]
        log_total = mixed[64:65, here]
        delta = jnp.sum(incoming_t * mixed[:64, here], axis=0, keepdims=True)
        begin = start[:, here]
        query_at = lax.broadcasted_iota(jnp.int32, (block, block), 1) + number * block

        def turn(key_number, total):
            there = pl.ds(pl.multiple_of(key_number * block, block), block)
            scores = lax.dot_general(
                key[there, :], queries, (((1,), (1,)), ((), ())),
                preferred_element_type=jnp.float32,
            )
            key_at = lax.broadcasted_iota(jnp.int32, (block, block), 0) + key_number * block
            allowed = (key_at >= begin) & (key_at <= query_at)
            probs = jnp.where(allowed, jnp.exp(scores - log_total), 0.0)
            grad_probs = lax.dot_general(
                value[there, :], padded, (((1,), (1,)), ((), ())),
                preferred_element_type=jnp.float32,
            )
            grad_scores = (probs * (grad_probs - delta)).astype(jnp.bfloat16)
            value_sum[there, :] += jnp.dot(
                probs.astype(jnp.bfloat16), incoming, preferred_element_type=jnp.float32
            )
            pair_sum[there, :] += jnp.dot(
                grad_scores, queries, preferred_element_type=jnp.float32
            )
            return total + jnp.dot(
                key_t[:, there], grad_scores, preferred_element_type=jnp.float32
            )

        total = lax.fori_loop(
            first_key[number], number + 1, turn, jnp.zeros((64, block), jnp.float32)
        )
        tall = jnp.concatenate([total * scale, jnp.zeros((64, block), jnp.float32)], 0)
        pair_sum[here, :] += jnp.transpose(tall)
        return carry

    lax.fori_loop(0, rows // block, attend, 0)

    def finish(number, carry):
        here = pl.ds(pl.multiple_of(number * block, block), block)
        pair = pair_sum[here, :]
        lane = lane_of((block, 128))
        across = pair * sine[here, :]
        turned = jnp.where(
            lane % 64 < 32, pltpu.roll(across, 96, 1), -pltpu.roll(across, 32, 1)
        )
        pair = pair * cosine[here, :] + turned
        values = value_sum[here, :]
        for n, one in enumerate(storage(number)):
            pair_out[one, :] = pair[n * 64 : (n + 1) * 64, :]
            value_out[one, :] = values[n * 64 : (n + 1) * 64, :]
        return carry

    lax.fori_loop(0, rows // block, finish, 0)


def whole_call(kernel, scalars, outs, scratch, vmem):
    def run(*operands):
        spec = pl.BlockSpec(memory_space=pltpu.VMEM)
        return pl.pallas_call(
            kernel,
            out_shape=outs,
            grid_spec=pltpu.PrefetchScalarGridSpec(
                num_scalar_prefetch=scalars,
                grid=(),
                in_specs=[spec] * (len(operands) - scalars),
                out_specs=[spec] * len(outs),
                scratch_shapes=scratch,
            ),
            compiler_params=pltpu.CompilerParams(vmem_limit_bytes=vmem),
        )(*operands)

    return run


def fast_shards(
    hidden_in, block_order, segment_ids, cotangent, attn_gain, query_key_value_weight,
    w_out, ffn_gain, w_router, routes, expert_in, expert_out,
):
    bf16, f32 = jnp.bfloat16, jnp.float32
    rows = hidden_in.shape[1]
    width = hidden_in.shape[2]
    length = rows * 16
    capacity = length * TOPK * 9 // (8 * E)
    ia, ib, ic, idd, jf = (lax.axis_index(name) for name in EVERY)
    mine = ia * 8 + ib * 4 + ic * 2 + idd
    expert = jf * 16 + mine
    low_half = jf == 0

    gain_one_f = join(attn_gain, "f").astype(f32)
    inputs = hidden_in[0].astype(f32)
    grad_out = cotangent[0].astype(f32)
    scale_one = rms_scale(inputs)
    norm_one = inputs * scale_one
    h_one = (norm_one * gain_one_f).astype(bf16)
    h_low, h_high = gather_ctx(
        [h_one[:, :512], h_one[:, 512:]], [("a", "b", "c", "d"), ("c", "a", "b", "d")]
    )
    h_low = h_low.reshape(length, 512)
    h_high = h_high.reshape(length, 512)

    split_rows = query_key_value_weight.shape[0]
    q_part = query_key_value_weight[:, :1024].reshape(split_rows, 16, 64)
    k_part = query_key_value_weight[:, 1024:1536].reshape(split_rows, 8, 1, 64)
    v_part = query_key_value_weight[:, 1536:].reshape(split_rows, 8, 1, 64)
    kv_part = jnp.concatenate([k_part, v_part], 2).reshape(split_rows, 16, 64)
    by_head = jnp.concatenate([q_part, kv_part], 2).reshape(split_rows, 2048)
    my_slice = lax.dynamic_slice_in_dim(by_head, (mine // 2) * 256, 256, 1)
    my_weight = join(my_slice, "f")
    head_weight = jnp.concatenate(
        [
            jnp.where(idd == 0, my_weight[:, :64], my_weight[:, 128:192]),
            my_weight[:, 64:128],
            my_weight[:, 192:],
            jnp.zeros((width, 64), bf16),
        ],
        1,
    )
    out_full = join(w_out, "f")
    gain_two_f = join(ffn_gain, "f").astype(f32)
    router_full = join(w_router, "f")
    by_head_full = join(by_head, "f")

    up_weight = lax.all_to_all(expert_in, CTX, split_axis=0, concat_axis=0, tiled=True).reshape(
        width, 2 * F
    )
    down_weight = lax.all_to_all(
        expert_out, CTX, split_axis=0, concat_axis=0, tiled=True
    ).reshape(F, width)

    order = block_order[0]
    place = jnp.sum(
        jnp.where(order[None, :] == jnp.arange(32, dtype=jnp.int32)[:, None],
                  jnp.arange(32, dtype=jnp.int32)[None, :], 0),
        axis=1,
    )
    document = segment_ids[0]
    start = jnp.sum((document[:, None] < document[None, :]).astype(jnp.int32), axis=0)
    first_key = start[::QUERY_BLOCK] // QUERY_BLOCK
    start = start[None, :]
    steps = jnp.arange(HEAD_SIZE // 2, dtype=f32)
    frequency = jnp.power(THETA, -2.0 * steps / HEAD_SIZE)
    coarse = (jnp.arange(length // 64, dtype=f32) * 64.0)[:, None] * frequency[None, :]
    fine = jnp.arange(64, dtype=f32)[:, None] * frequency[None, :]
    cos_a, sin_a = (jnp.cos(coarse)[:, None, :], jnp.sin(coarse)[:, None, :])
    cos_b, sin_b = (jnp.cos(fine)[None], jnp.sin(fine)[None])
    cosine = jnp.tile((cos_a * cos_b - sin_a * sin_b).reshape(length, 32), (1, 4))
    sine = jnp.tile((sin_a * cos_b + cos_a * sin_b).reshape(length, 32), (1, 4))

    query, key, value, mixed, attended_head = whole_call(
        attention_forward,
        2,
        [
            jax.ShapeDtypeStruct((length, 128), bf16),
            jax.ShapeDtypeStruct((length, 128), bf16),
            jax.ShapeDtypeStruct((length, 128), bf16),
            jax.ShapeDtypeStruct((72, length), f32),
            jax.ShapeDtypeStruct((length, 64), bf16),
        ],
        [pltpu.VMEM((128, length), bf16)],
        32 << 20,
    )(place, first_key, h_low, h_high, head_weight, cosine, sine, start)

    def to_tokens(value_heads):
        got = lax.all_to_all(
            value_heads.reshape(16, rows, -1), CTX, split_axis=0, concat_axis=0, tiled=True
        )
        return got

    attended = to_tokens(attended_head).transpose(1, 0, 2).reshape(rows, 1024)
    middle_state = inputs + jnp.dot(attended, out_full, preferred_element_type=f32)
    scale_two = rms_scale(middle_state)
    norm_two = middle_state * scale_two
    h_two = (norm_two * gain_two_f).astype(bf16)
    logits = jnp.dot(h_two, router_full, preferred_element_type=f32)
    route = routes[0]
    named = jnp.any(route[:, :, None] == jnp.arange(E, dtype=jnp.int32)[None, None, :], axis=1)
    top = jnp.max(jnp.where(named, logits, MASK_FILL_VALUE), axis=-1, keepdims=True)
    weights = jnp.where(named, jnp.exp(logits - top), 0.0)
    gates = weights / jnp.sum(weights, axis=-1, keepdims=True)

    named_b = named.astype(bf16)
    earlier = (
        jnp.arange(rows)[:, None] > jnp.arange(rows)[None, :]
    ).astype(bf16)
    rank = jnp.dot(earlier, named_b, preferred_element_type=f32)
    row_of = jnp.where(named, rank, -1.0)
    row_pair = jnp.stack([row_of, swap(row_of, "a")])
    half = row_pair.reshape(2, rows, 2, 2, 8)
    half = jnp.where(ia == 0, half[:, :, :, 0], half[:, :, :, 1])
    half = half.transpose(0, 3, 2, 1).reshape(2, 16, 1, rows)
    pick = (half == jnp.arange(MOST, dtype=f32)[None, None, :, None]).astype(bf16)

    def send_rows(choice, tokens):
        built = lax.dot_general(
            choice, tokens, (((2,), (0,)), ((), ())), preferred_element_type=f32
        ).astype(bf16)
        return lax.all_to_all(built, HALF, split_axis=0, concat_axis=0, tiled=True)

    def take_rows(choice, sent):
        got = lax.all_to_all(sent, HALF, split_axis=0, concat_axis=0, tiled=True)
        return lax.dot_general(
            choice, got, (((0, 1), (0, 1)), ((), ())), preferred_element_type=f32
        )

    extended = jnp.concatenate(
        [h_two] + exact_parts(gates) + [jnp.zeros((rows, EXTRA - 3 * E), bf16)], 1
    )
    other_extended = swap(extended, "a")
    rows_mine = send_rows(pick[0], extended)
    rows_other = send_rows(pick[1], other_extended)
    received = in_order(rows_mine[None], rows_other[None], "a", 0).reshape(
        32 * MOST, width + EXTRA
    )

    columns = row_of.T.reshape(2, 16, rows).transpose(1, 0, 2).reshape(32, rows)
    their_row = lax.all_to_all(columns, EVERY, split_axis=0, concat_axis=0, tiled=True)
    their_count = jnp.sum((their_row >= 0).astype(f32), axis=1).reshape(16, 2)
    before_me = (jnp.arange(16)[:, None] > jnp.arange(16)[None, :]).astype(f32)
    offset = jnp.dot(before_me, their_count, precision=HIGHEST).reshape(32, 1)
    their_count = their_count.reshape(32, 1)
    row_number = jnp.arange(MOST, dtype=f32)[None, :]
    kept = (row_number < their_count) & (row_number + offset < capacity)
    kept = kept.astype(f32).reshape(32 * MOST, 1)
    their_pick = (their_row[:, None, :] == row_number[:, :, None]).astype(bf16)
    all_cotangent = lax.all_gather(cotangent[0], EVERY, axis=0, tiled=True).reshape(
        32, rows, width
    )
    grad_rows = jnp.einsum(
        "srt,stc->src", their_pick, all_cotangent, preferred_element_type=f32
    ).astype(bf16).reshape(32 * MOST, width)

    x_rows = received[:, :width]
    lane = jnp.arange(EXTRA, dtype=jnp.int32)[None, :]
    my_lane = ((lane % E) == expert) & (lane < 3 * E)
    gate_rows = jnp.sum(
        jnp.where(my_lane, received[:, width:].astype(f32), 0.0), axis=1, keepdims=True
    )
    before = jnp.dot(x_rows, up_weight, preferred_element_type=f32)
    gate_pre = before[:, :F]
    up_pre = before[:, F:]
    sigma = jax.nn.sigmoid(gate_pre)
    activation = (gate_pre * sigma * up_pre).astype(bf16)
    result = jnp.dot(activation, down_weight, preferred_element_type=f32).astype(bf16)
    result_f = result.astype(f32) * kept
    grad_pair = (gate_rows * grad_rows.astype(f32) * kept).astype(bf16)
    grad_gate_rows = jnp.sum(grad_rows.astype(f32) * result_f, axis=1, keepdims=True)
    grad_activation = contract_columns(grad_pair, down_weight)
    grad_down = contract_rows(activation, grad_pair)
    grad_gate = grad_activation * up_pre * sigma * (1.0 + gate_pre * (1.0 - sigma))
    grad_up = grad_activation * gate_pre * sigma
    grad_pre = jnp.concatenate([grad_gate, grad_up], axis=-1).astype(bf16)
    grad_copy = contract_columns(grad_pre, up_weight).astype(bf16)
    grad_up_weight = contract_rows(x_rows, grad_pre)
    gate_parts = exact_parts(grad_gate_rows)
    extra = jnp.zeros((32 * MOST, EXTRA), bf16)
    for number, part in enumerate(gate_parts):
        extra = jnp.where(lane == expert + number * E, part, extra)
    grad_copy = jnp.concatenate([grad_copy, extra], 1).reshape(2, 16, MOST, width + EXTRA)
    gated_result = (gate_rows * result_f).astype(bf16).reshape(2, 16, MOST, width)

    def give_back(by_half):
        here = jnp.where(ia == 0, by_half[0], by_half[1])
        there = jnp.where(ia == 0, by_half[1], by_half[0])
        away = take_rows(pick[1], there).astype(bf16)
        home = take_rows(pick[0], here)
        return home + swap(away, "a").astype(f32)

    back = give_back(grad_copy)
    mixture = give_back(gated_result)
    hidden_out = (middle_state + mixture).astype(bf16)
    gate_grads = sum(
        back[:, width + n * E : width + (n + 1) * E] for n in range(3)
    )
    grad_logits = gates * (gate_grads - jnp.sum(gates * gate_grads, axis=-1, keepdims=True))
    grad_h_two = back[:, :width] + lax.dot_general(
        grad_logits, router_full.astype(f32), (((1,), (1,)), ((), ())), precision=HIGHEST
    )
    grad_router_part = lax.dot_general(
        grad_logits, h_two.astype(f32), (((0,), (0,)), ((), ())), precision=HIGHEST
    )
    grad_gain_two = jnp.sum(grad_h_two * norm_two, axis=0, keepdims=True)
    scaled_two = grad_h_two * gain_two_f
    grad_mid = grad_out + scale_two * (
        scaled_two - norm_two * jnp.mean(scaled_two * norm_two, axis=-1, keepdims=True)
    )
    grad_branch = grad_mid.astype(bf16)
    attended_gradient = contract_columns(grad_branch, out_full).astype(bf16)
    grad_heads = to_tokens(
        attended_gradient.reshape(rows, 16, 64).transpose(1, 0, 2)
    ).reshape(length, 64)

    all_branch = lax.all_gather(grad_branch, CTX, axis=0, tiled=True)
    out_part = contract_rows(attended_head, all_branch)
    out_part = (out_part + swap(out_part, "f")).astype(bf16)
    out_all = gather_ctx(
        [out_part[:, :512], out_part[:, 512:]], [("a", "b", "c", "d"), ("c", "a", "b", "d")]
    )
    out_all = jnp.concatenate(out_all, 2).reshape(2, 512, width)
    share_out = jnp.where(low_half, out_all[0], out_all[1]).astype(f32)

    small = sum_everywhere(
        jnp.concatenate([grad_router_part, jnp.broadcast_to(grad_gain_two, (8, width))], 0)
    )
    small = jnp.where(low_half, small[:, :512], small[:, 512:])
    share_router = small[:E].T
    share_two = small[E]

    pair_grad, value_grad = whole_call(
        attention_backward,
        2,
        [jax.ShapeDtypeStruct((length, 128), f32), jax.ShapeDtypeStruct((length, 64), f32)],
        [
            pltpu.VMEM((64, length), bf16),
            pltpu.VMEM((length, 128), f32),
            pltpu.VMEM((length, 64), f32),
        ],
        32 << 20,
    )(place, first_key, query, key, value, mixed, grad_heads, cosine, sine, start)
    key_grad = pair_grad[:, 64:]
    sent = jnp.where(idd == 0, value_grad, key_grad)
    stays = jnp.where(idd == 0, key_grad, value_grad)
    grad_columns = jnp.concatenate([pair_grad[:, :64], stays + swap(sent, "d")], 1).astype(bf16)

    low_part = contract_rows(h_low, grad_columns)
    high_part = contract_rows(h_high, grad_columns)
    columns_grad = jnp.where(low_half, low_part, high_part) + swap(
        jnp.where(low_half, high_part, low_part), "f"
    )
    columns_grad = columns_grad.astype(bf16)
    qkv_all = gather_ctx(
        [columns_grad[:256], columns_grad[256:]], [("a", "b", "c", "d"), ("c", "a", "b", "d")]
    )
    qkv_all = jnp.concatenate(qkv_all, 1).transpose(1, 0, 2).astype(f32)
    kv_all = qkv_all[:, :, 64:].reshape(512, 8, 2, 64)
    share_qkv = jnp.concatenate(
        [
            qkv_all[:, :, :64].reshape(512, 1024),
            kv_all[:, :, 0].reshape(512, 512),
            kv_all[:, :, 1].reshape(512, 512),
        ],
        1,
    )

    grad_projected = to_tokens(grad_columns)
    grad_projected = grad_projected.transpose(1, 0, 2).reshape(rows, 2048)
    grad_h_one = contract_columns(grad_projected, by_head_full)
    grad_gain_one = sum_everywhere(jnp.sum(grad_h_one * norm_one, axis=0))
    share_one = jnp.where(low_half, grad_gain_one[:512], grad_gain_one[512:])
    scaled_one = grad_h_one * gain_one_f
    grad_inputs = grad_mid + scale_one * (
        scaled_one - norm_one * jnp.mean(scaled_one * norm_one, axis=-1, keepdims=True)
    )

    grad_expert_in = lax.all_to_all(
        grad_up_weight.astype(bf16).reshape(16, 64, 2 * F), CTX,
        split_axis=0, concat_axis=0, tiled=True,
    ).astype(f32)
    grad_expert_out = lax.all_to_all(
        grad_down.astype(bf16).reshape(16, 32, width), CTX,
        split_axis=0, concat_axis=0, tiled=True,
    ).astype(f32)
    return (
        hidden_out[None],
        grad_inputs[None],
        share_one,
        share_qkv,
        share_out,
        share_two,
        share_router,
        grad_expert_in,
        grad_expert_out,
    )


def fast_solution(mesh):
    fine = Mesh(mesh.devices.reshape(2, 2, 2, 2, 2), EVERY)
    placed = (
        P("f", CTX, None),
        P("f", None),
        P("f", None),
        P("f", CTX, None),
        P("f"),
        P("f", None),
        P("f", None),
        P("f"),
        P("f", None),
        P("f", CTX, None),
        P("f", CTX, None),
        P("f", CTX, None),
    )
    return jax.shard_map(
        fast_shards,
        mesh=fine,
        in_specs=placed,
        out_specs=(
            P("f", CTX, None),
            P("f", CTX, None),
            P("f"),
            P("f", None),
            P("f", None),
            P("f"),
            P("f", None),
            P("f", CTX, None),
            P("f", CTX, None),
        ),
        check_vma=False,
    )


def solution(mesh):
    if mesh.shape["ctx"] == QUERY_HEADS and mesh.shape["fsdp"] * mesh.shape["ctx"] == E:
        return fast_solution(mesh)
    return general_solution(mesh)
```

```python
import math

import jax
import jax.numpy as jnp
from jax import lax
from jax.experimental import pallas as pl
from jax.experimental.pallas import tpu as pltpu
from jax.sharding import Mesh
from jax.sharding import PartitionSpec as P

QUERY_HEADS = 16
KEY_VALUE_HEADS = 8
HEAD_SIZE = 64
E = 32
TOPK = 8
F = 512
MOST = 48


EPSILON = 1e-06
THETA = 10000.0
MASK_FILL_VALUE = -1e30
HIGHEST = lax.Precision.HIGHEST


def carried_in(value, axis, combine, identity):
    length, mine = (lax.axis_size(axis), lax.axis_index(axis))
    everything = lax.all_gather(value, axis)
    start = jnp.broadcast_to(jnp.asarray(identity, value.dtype), value.shape)

    def turn(k, before):
        reached = k < mine
        new = combine(before, everything[k])
        return jnp.where(reached, new, before)

    return lax.fori_loop(0, length, turn, start)


def rms_scale(value_rows):
    return lax.rsqrt(jnp.mean(value_rows * value_rows, axis=-1, keepdims=True) + EPSILON)


def rotate(value_rows):
    middle = value_rows.shape[-1] // 2
    return jnp.concatenate([-value_rows[..., middle:], value_rows[..., :middle]], axis=-1)


def rotate_back(value_rows):
    middle = value_rows.shape[-1] // 2
    return jnp.concatenate([value_rows[..., middle:], -value_rows[..., :middle]], axis=-1)


def rope_tables(position):
    steps = jnp.arange(HEAD_SIZE // 2, dtype=jnp.float32)
    frequency = jnp.power(THETA, -2.0 * steps / HEAD_SIZE)
    angle = position.astype(jnp.float32)[:, None] * frequency[None, :]
    angle = jnp.concatenate([angle, angle], axis=-1)
    return (jnp.cos(angle), jnp.sin(angle))


def contract_rows(left, right):
    return lax.dot_general(
        left, right, (((0,), (0,)), ((), ())), preferred_element_type=jnp.float32
    )


def contract_columns(left, right):
    return lax.dot_general(
        left, right, (((1,), (1,)), ((), ())), preferred_element_type=jnp.float32
    )


def own_rows(total, rank, count):
    share = total.shape[0] // count
    return lax.dynamic_slice_in_dim(total, rank * share, share, 0)


def general_shards(
    hidden_in,
    block_order,
    segment_ids,
    cotangent,
    attn_gain,
    query_key_value_weight,
    w_out,
    ffn_gain,
    w_router,
    routes,
    expert_in,
    expert_out,
):
    count_of_rows = hidden_in.shape[1]
    width = hidden_in.shape[2]
    ctx_count = lax.axis_size("ctx")
    fsdp_count = lax.axis_size("fsdp")
    sequence_length = count_of_rows * ctx_count
    half_block = count_of_rows // 2
    capacity = sequence_length * TOPK * 9 // (8 * E)
    query_total_width = QUERY_HEADS * HEAD_SIZE
    key_total_width = KEY_VALUE_HEADS * HEAD_SIZE
    query_group = QUERY_HEADS // KEY_VALUE_HEADS
    scale = 1.0 / math.sqrt(HEAD_SIZE)
    key_block_rows = min(1024, sequence_length)
    block_count = sequence_length // key_block_rows
    pair_count = count_of_rows * TOPK
    gain_one, qkv_full, out_full, gain_two, router_full = (
        lax.all_gather(attn_gain, "fsdp", axis=0, tiled=True),
        lax.all_gather(query_key_value_weight, "fsdp", axis=0, tiled=True),
        lax.all_gather(w_out, "fsdp", axis=0, tiled=True),
        lax.all_gather(ffn_gain, "fsdp", axis=0, tiled=True),
        lax.all_gather(w_router, "fsdp", axis=0, tiled=True),
    )
    up_full, down_full = (
        lax.all_gather(expert_in, "ctx", axis=1, tiled=True),
        lax.all_gather(expert_out, "ctx", axis=1, tiled=True),
    )
    key_position = (
        block_order[0][:, None] * half_block + jnp.arange(half_block, dtype=jnp.int32)[None, :]
    ).reshape(-1)
    key_document = segment_ids[0][key_position]
    first_row = lax.axis_index("ctx") * count_of_rows
    query_position = lax.dynamic_slice_in_dim(key_position, first_row, count_of_rows, 0)
    query_document = lax.dynamic_slice_in_dim(key_document, first_row, count_of_rows, 0)
    inputs = hidden_in[0].astype(jnp.float32)
    grad_out = cotangent[0].astype(jnp.float32)
    scale_one = rms_scale(inputs)
    norm_one = inputs * scale_one
    gain_one_f = gain_one.astype(jnp.float32)
    h_one = (norm_one * gain_one_f).astype(jnp.bfloat16)
    projected_rows = jnp.dot(h_one, qkv_full, preferred_element_type=jnp.float32)
    cosine, sine = rope_tables(query_position)
    query_raw = projected_rows[:, :query_total_width].reshape(count_of_rows, QUERY_HEADS, HEAD_SIZE)
    unrotated_key = projected_rows[
        :, query_total_width : query_total_width + key_total_width
    ].reshape(count_of_rows, KEY_VALUE_HEADS, HEAD_SIZE)
    query_matrix = (query_raw * cosine[:, None, :] + rotate(query_raw) * sine[:, None, :]).astype(
        jnp.bfloat16
    )
    key_rows = (
        unrotated_key * cosine[:, None, :] + rotate(unrotated_key) * sine[:, None, :]
    ).astype(jnp.bfloat16)
    value_rows = projected_rows[:, query_total_width + key_total_width :].astype(jnp.bfloat16)
    key_value_local = jnp.concatenate(
        [key_rows.reshape(count_of_rows, key_total_width), value_rows], axis=1
    )
    key_value_all = lax.all_gather(key_value_local, "ctx", axis=0, tiled=True)
    grouped_queries = query_matrix.reshape(count_of_rows, KEY_VALUE_HEADS, query_group, HEAD_SIZE)
    block_number = jnp.arange(block_count, dtype=jnp.int32)

    def block_keys(source, index):
        current_rows = lax.dynamic_slice_in_dim(source, index * key_block_rows, key_block_rows, 0)
        block_key_rows = current_rows[:, :key_total_width].reshape(
            key_block_rows, KEY_VALUE_HEADS, HEAD_SIZE
        )
        block_value_rows = current_rows[:, key_total_width:].reshape(
            key_block_rows, KEY_VALUE_HEADS, HEAD_SIZE
        )
        block_position = lax.dynamic_slice_in_dim(
            key_position, index * key_block_rows, key_block_rows, 0
        )
        block_document = lax.dynamic_slice_in_dim(
            key_document, index * key_block_rows, key_block_rows, 0
        )
        allowed = (query_document[:, None] == block_document[None, :]) & (
            block_position[None, :] <= query_position[:, None]
        )
        return (block_key_rows, block_value_rows, allowed)

    def scores_of(block_key_rows, allowed):
        scores = (
            jnp.einsum(
                "qhgd,khd->hgqk",
                grouped_queries,
                block_key_rows,
                preferred_element_type=jnp.float32,
            )
            * scale
        )
        return jnp.where(allowed[None, None], scores, MASK_FILL_VALUE)

    def max_sum(carry, index):
        top, total = carry
        block_key_rows, block_value_rows, allowed = block_keys(key_value_all, index)
        scores = scores_of(block_key_rows, allowed)
        new_top = jnp.maximum(top, jnp.max(scores, axis=-1))
        weights = jnp.where(allowed[None, None], jnp.exp(scores - new_top[..., None]), 0.0)
        total = total * jnp.exp(top - new_top) + jnp.sum(weights, axis=-1)
        return ((new_top, total), None)

    upper_start = jnp.full(
        (KEY_VALUE_HEADS, query_group, count_of_rows), MASK_FILL_VALUE, jnp.float32
    )
    overall_start = jnp.zeros((KEY_VALUE_HEADS, query_group, count_of_rows), jnp.float32)
    (top, total), unused = lax.scan(max_sum, (upper_start, overall_start), block_number)
    log_total = top + jnp.log(total)

    def weighted_values(accum, index):
        block_key_rows, block_value_rows, allowed = block_keys(key_value_all, index)
        scores = scores_of(block_key_rows, allowed)
        probs = jnp.where(allowed[None, None], jnp.exp(scores - log_total[..., None]), 0.0).astype(
            jnp.bfloat16
        )
        return (
            accum
            + jnp.einsum(
                "hgqk,khd->qhgd", probs, block_value_rows, preferred_element_type=jnp.float32
            ),
            None,
        )

    attended_f, unused = lax.scan(
        weighted_values,
        jnp.zeros((count_of_rows, KEY_VALUE_HEADS, query_group, HEAD_SIZE), jnp.float32),
        block_number,
    )
    attended = attended_f.reshape(count_of_rows, query_total_width).astype(jnp.bfloat16)
    middle_state = inputs + jnp.dot(attended, out_full, preferred_element_type=jnp.float32)
    scale_two = rms_scale(middle_state)
    norm_two = middle_state * scale_two
    gain_two_f = gain_two.astype(jnp.float32)
    h_two = (norm_two * gain_two_f).astype(jnp.bfloat16)
    logits = jnp.dot(h_two, router_full, preferred_element_type=jnp.float32)
    route = routes[0]
    gates = jax.nn.softmax(jnp.take_along_axis(logits, route, axis=1), axis=-1)
    flat = route.reshape(-1)
    onehot = (flat[:, None] == jnp.arange(E, dtype=jnp.int32)[None, :]).astype(jnp.int32)
    rank = jnp.sum((jnp.cumsum(onehot, axis=0) - onehot) * onehot, axis=1)
    counts = jnp.sum(onehot, axis=0)

    def add_counts(earlier, later):
        return earlier + later

    offsets = carried_in(counts, "ctx", add_counts, jnp.zeros((E,), jnp.int32))
    slot = jnp.sum(onehot * offsets[None, :], axis=1) + rank
    kept = slot < capacity
    target = jnp.where(kept, flat * MOST + rank, E * MOST)
    safe_target = jnp.minimum(target, E * MOST - 1)
    keep_float = kept.astype(jnp.float32)[:, None]
    token = jnp.arange(pair_count, dtype=jnp.int32) // TOPK
    send_rows = (
        jnp.zeros((E * MOST, width), jnp.bfloat16)
        .at[target]
        .set(h_two[token], mode="drop")
        .reshape(E, MOST, width)
    )
    received = lax.all_to_all(send_rows, "fsdp", split_axis=0, concat_axis=1, tiled=True)
    before = jnp.einsum("erd,edf->erf", received, up_full, preferred_element_type=jnp.float32)
    gate_pre = before[..., :F]
    up_pre = before[..., F:]
    sigma = jax.nn.sigmoid(gate_pre)
    activation = (gate_pre * sigma * up_pre).astype(jnp.bfloat16)
    expert_result = jnp.einsum(
        "erf,efd->erd", activation, down_full, preferred_element_type=jnp.float32
    ).astype(jnp.bfloat16)
    returned = lax.all_to_all(
        expert_result, "fsdp", split_axis=1, concat_axis=0, tiled=True
    ).reshape(E * MOST, width)
    pair_result = (returned[safe_target].astype(jnp.float32) * keep_float).reshape(
        count_of_rows, TOPK, width
    )
    mixture = jnp.sum(gates[..., None] * pair_result, axis=1)
    hidden_out = (middle_state + mixture).astype(jnp.bfloat16)
    grad_pair = (
        (gates[..., None] * grad_out[:, None, :]).reshape(pair_count, width) * keep_float
    ).astype(jnp.bfloat16)
    grad_gates = jnp.sum(grad_out[:, None, :] * pair_result, axis=-1)
    grad_chosen = gates * (grad_gates - jnp.sum(gates * grad_gates, axis=-1, keepdims=True))
    chosen_table = (route[..., None] == jnp.arange(E, dtype=jnp.int32)[None, None, :]).astype(
        jnp.float32
    )
    grad_logits = jnp.sum(grad_chosen[..., None] * chosen_table, axis=1)
    grad_router_part = lax.dot_general(
        h_two.astype(jnp.float32), grad_logits, (((0,), (0,)), ((), ())), precision=HIGHEST
    )
    grad_h_two = lax.dot_general(
        grad_logits, router_full.astype(jnp.float32), (((1,), (1,)), ((), ())), precision=HIGHEST
    )
    send_grads = (
        jnp.zeros((E * MOST, width), jnp.bfloat16)
        .at[target]
        .set(grad_pair, mode="drop")
        .reshape(E, MOST, width)
    )
    grad_received = lax.all_to_all(send_grads, "fsdp", split_axis=0, concat_axis=1, tiled=True)
    grad_activation = jnp.einsum(
        "erd,efd->erf", grad_received, down_full, preferred_element_type=jnp.float32
    )
    grad_down = jnp.einsum(
        "erf,erd->efd", activation, grad_received, preferred_element_type=jnp.float32
    )
    grad_gate = grad_activation * up_pre * sigma * (1.0 + gate_pre * (1.0 - sigma))
    grad_up = grad_activation * gate_pre * sigma
    grad_pre = jnp.concatenate([grad_gate, grad_up], axis=-1).astype(jnp.bfloat16)
    grad_up_weight = jnp.einsum(
        "erd,erf->edf", received, grad_pre, preferred_element_type=jnp.float32
    )
    grad_copy = jnp.einsum(
        "erf,edf->erd", grad_pre, up_full, preferred_element_type=jnp.float32
    ).astype(jnp.bfloat16)
    grad_returned = lax.all_to_all(
        grad_copy, "fsdp", split_axis=1, concat_axis=0, tiled=True
    ).reshape(E * MOST, width)
    grad_h_two = grad_h_two + jnp.sum(
        (grad_returned[safe_target].astype(jnp.float32) * keep_float).reshape(
            count_of_rows, TOPK, width
        ),
        axis=1,
    )
    grad_expert_in, grad_expert_out = (
        lax.psum_scatter(
            grad_up_weight.astype(jnp.bfloat16), "ctx", scatter_dimension=1, tiled=True
        ).astype(jnp.float32),
        lax.psum_scatter(
            grad_down.astype(jnp.bfloat16), "ctx", scatter_dimension=1, tiled=True
        ).astype(jnp.float32),
    )
    grad_gain_two = jnp.sum(grad_h_two * norm_two, axis=0)
    scaled_two = grad_h_two * gain_two_f
    grad_mid = grad_out + scale_two * (
        scaled_two - norm_two * jnp.mean(scaled_two * norm_two, axis=-1, keepdims=True)
    )
    grad_branch = grad_mid.astype(jnp.bfloat16)
    grad_out_weight = contract_rows(attended, grad_branch)
    attended_gradient = contract_columns(grad_branch, out_full).astype(jnp.bfloat16)
    grouped_gradient = attended_gradient.reshape(
        count_of_rows, KEY_VALUE_HEADS, query_group, HEAD_SIZE
    )
    delta = jnp.transpose(
        jnp.sum(grouped_gradient.astype(jnp.float32) * attended_f, axis=-1), (1, 2, 0)
    )

    def block_gradients(query_accum, index):
        block_key_rows, block_value_rows, allowed = block_keys(key_value_all, index)
        scores = scores_of(block_key_rows, allowed)
        probs = jnp.where(allowed[None, None], jnp.exp(scores - log_total[..., None]), 0.0)
        grad_probs = jnp.einsum(
            "qhgd,khd->hgqk", grouped_gradient, block_value_rows, preferred_element_type=jnp.float32
        )
        grad_scores = (probs * (grad_probs - delta[..., None])).astype(jnp.bfloat16)
        query_accum = query_accum + jnp.einsum(
            "hgqk,khd->qhgd", grad_scores, block_key_rows, preferred_element_type=jnp.float32
        )
        grad_keys = (
            jnp.einsum(
                "hgqk,qhgd->khd", grad_scores, grouped_queries, preferred_element_type=jnp.float32
            )
            * scale
        )
        grad_values = jnp.einsum(
            "hgqk,qhgd->khd",
            probs.astype(jnp.bfloat16),
            grouped_gradient,
            preferred_element_type=jnp.float32,
        )
        joined = jnp.concatenate(
            [
                grad_keys.reshape(key_block_rows, key_total_width),
                grad_values.reshape(key_block_rows, key_total_width),
            ],
            axis=1,
        )
        return (query_accum, joined)

    grad_queries, grad_blocks = lax.scan(
        block_gradients,
        jnp.zeros((count_of_rows, KEY_VALUE_HEADS, query_group, HEAD_SIZE), jnp.float32),
        block_number,
    )
    key_value_gradient = lax.psum_scatter(
        grad_blocks.reshape(sequence_length, 2 * key_total_width).astype(jnp.bfloat16),
        "ctx",
        scatter_dimension=0,
        tiled=True,
    ).astype(jnp.float32)
    grad_queries = (grad_queries * scale).reshape(count_of_rows, QUERY_HEADS, HEAD_SIZE)
    local_key_gradient = key_value_gradient[:, :key_total_width].reshape(
        count_of_rows, KEY_VALUE_HEADS, HEAD_SIZE
    )
    grad_values_mine = key_value_gradient[:, key_total_width:]
    grad_query_pre = grad_queries * cosine[:, None, :] + rotate_back(
        grad_queries * sine[:, None, :]
    )
    grad_key_pre = local_key_gradient * cosine[:, None, :] + rotate_back(
        local_key_gradient * sine[:, None, :]
    )
    grad_projected = jnp.concatenate(
        [
            grad_query_pre.reshape(count_of_rows, query_total_width),
            grad_key_pre.reshape(count_of_rows, key_total_width),
            grad_values_mine,
        ],
        axis=1,
    ).astype(jnp.bfloat16)
    grad_qkv_weight = contract_rows(h_one, grad_projected)
    grad_h_one = contract_columns(grad_projected, qkv_full)
    grad_gain_one = jnp.sum(grad_h_one * norm_one, axis=0)
    scaled_one = grad_h_one * gain_one_f
    grad_inputs = grad_mid + scale_one * (
        scaled_one - norm_one * jnp.mean(scaled_one * norm_one, axis=-1, keepdims=True)
    )
    total_one, total_qkv, total_out, total_two, total_router = lax.psum(
        (grad_gain_one, grad_qkv_weight, grad_out_weight, grad_gain_two, grad_router_part),
        ("ctx", "fsdp"),
    )
    fsdp_rank = lax.axis_index("fsdp")
    share_one = own_rows(total_one, fsdp_rank, fsdp_count)
    share_qkv = own_rows(total_qkv, fsdp_rank, fsdp_count)
    share_out = own_rows(total_out, fsdp_rank, fsdp_count)
    share_two = own_rows(total_two, fsdp_rank, fsdp_count)
    share_router = own_rows(total_router, fsdp_rank, fsdp_count)
    return (
        hidden_out[None],
        grad_inputs[None],
        share_one,
        share_qkv,
        share_out,
        share_two,
        share_router,
        grad_expert_in,
        grad_expert_out,
    )


def general_solution(mesh):
    placed = (
        P("fsdp", "ctx", None),
        P("fsdp", None),
        P("fsdp", None),
        P("fsdp", "ctx", None),
        P("fsdp"),
        P("fsdp", None),
        P("fsdp", None),
        P("fsdp"),
        P("fsdp", None),
        P("fsdp", "ctx", None),
        P("fsdp", "ctx", None),
        P("fsdp", "ctx", None),
    )
    return jax.shard_map(
        general_shards,
        mesh=mesh,
        in_specs=placed,
        out_specs=(
            P("fsdp", "ctx", None),
            P("fsdp", "ctx", None),
            P("fsdp"),
            P("fsdp", None),
            P("fsdp", None),
            P("fsdp"),
            P("fsdp", None),
            P("fsdp", "ctx", None),
            P("fsdp", "ctx", None),
        ),
        check_vma=False,
    )


CTX = ("a", "b", "c", "d")
HALF = ("b", "c", "d", "f")
EVERY = ("a", "b", "c", "d", "f")
QUERY_BLOCK = 256
EXTRA = 128


def swap(value, axis):
    return lax.ppermute(value, axis, [(0, 1), (1, 0)])


def in_order(mine, other, axis, dim):
    first = lax.axis_index(axis) == 0
    return jnp.where(
        first, jnp.concatenate([mine, other], dim), jnp.concatenate([other, mine], dim)
    )


def join(value, axis, dim=0):
    return in_order(value, swap(value, axis), axis, dim)


def spread(value):
    return value[(None,) * 4]


def gather_step(held, axis):
    return in_order(held, swap(held, axis), axis, CTX.index(axis))


def share_swap(value):
    half = value.shape[0] // 2
    part = swap(jnp.where(lax.axis_index("d") == 0, value[:half], value[half:]), "f")
    return part


def share_join(value, part):
    return in_order(value, join(part, "d"), "f", 0)


def sum_everywhere(value):
    for axis in ("d", "f", "c", "b", "a"):
        value = value + swap(value, axis)
    return value


def together(*values):
    return lax.optimization_barrier(values)


def two_parts(value):
    high = lax.reduce_precision(value, 8, 7)
    return [high.astype(jnp.bfloat16), (value - high).astype(jnp.bfloat16)]


def angles(number, fine, coarse):
    cos_b, sin_b = fine[0], fine[1]
    cos_a = coarse[0, pl.ds(number, 1), :]
    sin_a = coarse[1, pl.ds(number, 1), :]
    return cos_a * cos_b - sin_a * sin_b, sin_a * cos_b + cos_a * sin_b


def block_angles(chunk, pieces, fine, coarse):
    pairs = [angles(chunk * pieces + n, fine, coarse) for n in range(pieces)]
    return (
        jnp.concatenate([one[0] for one in pairs], 0),
        jnp.concatenate([one[1] for one in pairs], 0),
    )


def lane_of(shape):
    return lax.broadcasted_iota(jnp.int32, shape, 1)


def attention_forward(
    place, h_place, first_key, low_own, high_own, low_next, high_next, weight, fine, coarse,
    start, query_out, key_out, value_out, mixed_out, attended_out, value_t,
):
    rows = query_out.shape[0]
    block = QUERY_BLOCK
    pieces = block // 64

    def project(chunk, carry):
        def rows_of(own, following):
            found = []
            for n in range(pieces):
                spot = h_place[chunk * pieces + n]
                at = pl.ds(pl.multiple_of((spot % 16) * 64, 64), 64)
                found.append(jnp.where(spot < 16, own[at, :], following[at, :]))
            return jnp.concatenate(found, 0)

        low = rows_of(low_own, low_next)
        high = rows_of(high_own, high_next)
        here = pl.ds(pl.multiple_of(chunk * block, block), block)
        both = jnp.dot(low, weight[:512, :], preferred_element_type=jnp.float32) + jnp.dot(
            high, weight[512:, :], preferred_element_type=jnp.float32
        )
        pair = both[:, :128]
        values = both[:, 128:].astype(jnp.bfloat16)
        lane = lane_of((block, 128))
        turned = jnp.where(
            lane % 64 < 32, -pltpu.roll(pair, 96, 1), pltpu.roll(pair, 32, 1)
        )
        cosine, sine = block_angles(chunk, pieces, fine, coarse)
        pair = pair * cosine + turned * sine
        pair = pair.astype(jnp.bfloat16).astype(jnp.float32)
        key_out[here, :] = jnp.where(lane >= 64, pair, 0.0).astype(jnp.bfloat16)
        query_out[here, :] = jnp.where(
            lane >= 64, pltpu.roll(pair, 64, 1) * (1.0 / math.sqrt(HEAD_SIZE)), 0.0
        ).astype(jnp.bfloat16)
        value_out[here, :] = values
        turned_values = jnp.transpose(values.astype(jnp.float32))
        ones = lax.broadcasted_iota(jnp.int32, (128, block), 0) == 64
        value_t[:, here] = jnp.where(ones, 1.0, turned_values).astype(jnp.bfloat16)
        return carry

    lax.fori_loop(0, rows // block, project, 0)

    def attend(number, carry):
        here = pl.ds(pl.multiple_of(number * block, block), block)
        queries = query_out[here, :]
        begin = start[:, here]
        query_at = lax.broadcasted_iota(jnp.int32, (block, block), 1) + number * block

        def turn(key_number, state):
            top, total = state
            there = pl.ds(pl.multiple_of(key_number * block, block), block)
            scores = lax.dot_general(
                key_out[there, :], queries, (((1,), (1,)), ((), ())),
                preferred_element_type=jnp.float32,
            )
            key_at = lax.broadcasted_iota(jnp.int32, (block, block), 0) + key_number * block
            allowed = (key_at >= begin) & (key_at <= query_at)
            scores = jnp.where(allowed, scores, MASK_FILL_VALUE)
            new_top = jnp.maximum(top, jnp.max(scores, axis=0, keepdims=True))
            weights = jnp.exp(scores - new_top).astype(jnp.bfloat16)
            total = total * jnp.exp(top - new_top) + jnp.dot(
                value_t[:, there], weights, preferred_element_type=jnp.float32
            )
            return new_top, total

        top, total = lax.fori_loop(
            first_key[number],
            number + 1,
            turn,
            (
                jnp.full((1, block), MASK_FILL_VALUE, jnp.float32),
                jnp.zeros((128, block), jnp.float32),
            ),
        )
        weight_sum = total[64:65, :]
        mixed = total * (1.0 / weight_sum)
        log_total = top + jnp.log(weight_sum)
        mixed_out[:64, here] = mixed[:64, :]
        mixed_out[64:72, here] = jnp.broadcast_to(log_total, (8, block))
        upright = jnp.transpose(mixed)[:, :64].astype(jnp.bfloat16)
        for n in range(pieces):
            rows_there = pl.ds(pl.multiple_of(place[number * pieces + n] * 64, 64), 64)
            attended_out[rows_there, :] = upright[n * 64 : (n + 1) * 64, :]
        return carry

    lax.fori_loop(0, rows // block, attend, 0)


def attention_backward(
    place, first_key, core, query, key, value, mixed, grad, fine, coarse, start,
    keep_out, send_out, key_t, pair_sum, value_sum,
):
    rows = query.shape[0]
    block = QUERY_BLOCK
    pieces = block // 64
    scale = 1.0 / math.sqrt(HEAD_SIZE)

    def prepare(chunk, carry):
        here = pl.ds(pl.multiple_of(chunk * block, block), block)
        turned = jnp.transpose(key[here, :].astype(jnp.float32))
        key_t[:, here] = turned[64:, :].astype(jnp.bfloat16)
        pair_sum[here, :] = jnp.zeros((block, 128), jnp.float32)
        value_sum[here, :] = jnp.zeros((block, 128), jnp.float32)
        return carry

    lax.fori_loop(0, rows // block, prepare, 0)

    def storage(number):
        return [
            pl.ds(pl.multiple_of(place[number * pieces + n] * 64, 64), 64) for n in range(pieces)
        ]

    def attend(number, carry):
        here = pl.ds(pl.multiple_of(number * block, block), block)
        queries = query[here, :]
        incoming = jnp.concatenate([grad[one, :] for one in storage(number)], 0)
        nothing = jnp.zeros((block, 64), jnp.bfloat16)
        padded = jnp.concatenate([incoming, nothing], 1)
        upper = jnp.concatenate([nothing, incoming], 1)
        incoming_t = jnp.transpose(padded.astype(jnp.float32))[:64, :]
        log_total = mixed[64:65, here]
        delta = jnp.sum(incoming_t * mixed[:64, here], axis=0, keepdims=True)
        begin = start[:, here]
        query_at = lax.broadcasted_iota(jnp.int32, (block, block), 1) + number * block

        def turn(key_number, total):
            there = pl.ds(pl.multiple_of(key_number * block, block), block)
            scores = lax.dot_general(
                key[there, :], queries, (((1,), (1,)), ((), ())),
                preferred_element_type=jnp.float32,
            )
            key_at = lax.broadcasted_iota(jnp.int32, (block, block), 0) + key_number * block
            allowed = (key_at >= begin) & (key_at <= query_at)
            probs = jnp.where(allowed, jnp.exp(scores - log_total), 0.0)
            grad_probs = lax.dot_general(
                value[there, :], padded, (((1,), (1,)), ((), ())),
                preferred_element_type=jnp.float32,
            )
            grad_scores = (probs * (grad_probs - delta)).astype(jnp.bfloat16)
            value_sum[there, :] += jnp.dot(
                probs.astype(jnp.bfloat16), upper, preferred_element_type=jnp.float32
            )
            pair_sum[there, :] += jnp.dot(
                grad_scores, queries, preferred_element_type=jnp.float32
            )
            return total + jnp.dot(
                key_t[:, there], grad_scores, preferred_element_type=jnp.float32
            )

        total = lax.fori_loop(
            first_key[number], number + 1, turn, jnp.zeros((64, block), jnp.float32)
        )
        tall = jnp.concatenate([total * scale, jnp.zeros((64, block), jnp.float32)], 0)
        pair_sum[here, :] += jnp.transpose(tall)
        return carry

    lax.fori_loop(0, rows // block, attend, 0)

    def finish(number, carry):
        here = pl.ds(pl.multiple_of(number * block, block), block)
        pair = pair_sum[here, :]
        lane = lane_of((block, 128))
        cosine, sine = block_angles(number, pieces, fine, coarse)
        across = pair * sine
        turned = jnp.where(
            lane % 64 < 32, pltpu.roll(across, 96, 1), -pltpu.roll(across, 32, 1)
        )
        pair = pair * cosine + turned
        values = value_sum[here, :]
        keys_stay = core[0] == 0
        keep = jnp.where((lane < 64) | keys_stay, pair, values)
        send = jnp.where(lane < 64, 0.0, jnp.where(keys_stay, values, pair)).astype(jnp.bfloat16)
        for n, one in enumerate(storage(number)):
            keep_out[one, :] = keep[n * 64 : (n + 1) * 64, :]
            send_out[one, :] = send[n * 64 : (n + 1) * 64, :]
        return carry

    lax.fori_loop(0, rows // block, finish, 0)


def expert_rows(
    where, rows, grad, up_weight, down_weight,
    copy_out, result_out, activation_out, pair_out, pre_out,
):
    f32, bf16 = jnp.float32, jnp.bfloat16
    width = grad.shape[3]
    count = rows.shape[0]
    expert = where[0]
    extra = rows[:, width:].astype(f32)
    lane = lane_of((count, EXTRA))
    gate = jnp.sum(
        jnp.where((lane == expert) | (lane == expert + E), extra, 0.0), axis=1, keepdims=True
    )
    before = jnp.dot(rows[:, :width], up_weight[...], preferred_element_type=f32)
    gate_pre = before[:, :F]
    up_pre = before[:, F:]
    sigma = jax.nn.sigmoid(gate_pre)
    swish = gate_pre * sigma
    activation = (swish * up_pre).astype(bf16)
    activation_out[...] = activation
    result = jnp.dot(activation, down_weight[...], preferred_element_type=f32).astype(bf16)
    result = result.astype(f32)
    grads = grad[...].reshape(count, width).astype(f32)
    grad_gate = jnp.sum(grads * result, axis=1, keepdims=True)
    result_out[...] = (gate * result).astype(bf16)
    pair = (gate * grads).astype(bf16)
    pair_out[...] = pair
    grad_activation = lax.dot_general(
        pair, down_weight[...], (((1,), (1,)), ((), ())), preferred_element_type=f32
    )
    pre_out[:, :F] = (
        grad_activation * up_pre * sigma * (1.0 + gate_pre * (1.0 - sigma))
    ).astype(bf16)
    pre_out[:, F:] = (grad_activation * swish).astype(bf16)
    copy_out[:, :width] = lax.dot_general(
        pre_out[...], up_weight[...], (((1,), (1,)), ((), ())), preferred_element_type=f32
    ).astype(bf16)
    high = grad_gate.astype(bf16).astype(f32)
    copy_out[:, width:] = jnp.where(
        lane == expert, high, jnp.where(lane == expert + E, grad_gate - high, 0.0)
    ).astype(bf16)


def expert_call(half, where, rows, grads, up_weight, down_weight):
    count, full = rows.shape
    width = grads.shape[3]
    steps = 2
    block = count // steps
    bf16 = jnp.bfloat16
    row_spec = lambda columns: pl.BlockSpec((block, columns), lambda i, w: (i, 0))
    whole = lambda a: pl.BlockSpec(a.shape, lambda i, w: (0, 0), pipeline_mode=pl.Buffered(1))
    columns = (full, width, F, width, 2 * F)
    return pl.pallas_call(
        expert_rows,
        out_shape=[jax.ShapeDtypeStruct((count, n), bf16) for n in columns],
        grid_spec=pltpu.PrefetchScalarGridSpec(
            num_scalar_prefetch=1,
            grid=(steps,),
            in_specs=[
                row_spec(full),
                pl.BlockSpec((16 // steps, 1, MOST, width), lambda i, w: (i, half, 0, 0)),
                whole(up_weight),
                whole(down_weight),
            ],
            out_specs=[row_spec(n) for n in columns],
        ),
        compiler_params=pltpu.CompilerParams(vmem_limit_bytes=48 << 20),
    )(where, rows, grads, up_weight, down_weight)


def assemble(first, second, qkv_out, out_out, gain_out):
    f32 = jnp.float32
    for pair in range(8):
        for source, rows, at in ((first, 384, 0), (second, 128, 384)):
            left = source[2 * pair, :rows, :].astype(f32)
            right = source[2 * pair + 1, :rows, :].astype(f32)
            here = slice(at, at + rows)
            qkv_out[here, pair * 128 : (pair + 1) * 128] = jnp.concatenate(
                [left[:, :64], right[:, :64]], 1
            )
            qkv_out[here, 1024 + pair * 64 : 1024 + (pair + 1) * 64] = left[:, 64:]
            qkv_out[here, 1536 + pair * 64 : 1536 + (pair + 1) * 64] = right[:, 64:]
    total = jnp.zeros((16, 128), f32)
    for device in range(16):
        bits = [(device >> n) & 1 for n in range(4)]
        at = bits[0] * 256 + bits[1] * 128 + bits[2] * 64 + bits[3] * 32
        for part in range(8):
            out_out[at : at + 32, part * 128 : (part + 1) * 128] = second[
                device, 128 + part * 32 : 160 + part * 32, :
            ].astype(f32)
        total = total + second[device, 384:400, :].astype(f32)
    gain_out[...] = total[:8, :] + total[8:, :]


def whole_call(kernel, scalars, outs, scratch, vmem):
    def run(*operands):
        spec = pl.BlockSpec(memory_space=pltpu.VMEM)
        return pl.pallas_call(
            kernel,
            out_shape=outs,
            grid_spec=pltpu.PrefetchScalarGridSpec(
                num_scalar_prefetch=scalars,
                grid=(),
                in_specs=[spec] * (len(operands) - scalars),
                out_specs=[spec] * len(outs),
                scratch_shapes=scratch,
            ),
            compiler_params=pltpu.CompilerParams(vmem_limit_bytes=vmem),
        )(*operands)

    return run


def fast_shards(
    hidden_in, block_order, segment_ids, cotangent, attn_gain, query_key_value_weight,
    w_out, ffn_gain, w_router, routes, expert_in, expert_out,
):
    bf16, f32 = jnp.bfloat16, jnp.float32
    rows = hidden_in.shape[1]
    width = hidden_in.shape[2]
    length = rows * 16
    capacity = length * TOPK * 9 // (8 * E)
    ia, ib, ic, idd, jf = (lax.axis_index(name) for name in EVERY)
    mine = ia * 8 + ib * 4 + ic * 2 + idd
    expert = jf * 16 + mine
    low_half = jf == 0

    inputs = hidden_in[0].astype(f32)
    scale_one = rms_scale(inputs)
    norm_one = inputs * scale_one
    gain_one_f = join(attn_gain, "f").astype(f32)
    h_one = (norm_one * gain_one_f).astype(bf16)

    (
        h_one, block_order, segment_ids, query_key_value_weight, w_out, ffn_gain, w_router,
        routes, cotangent,
    ) = together(
        h_one, block_order, segment_ids, query_key_value_weight, w_out, ffn_gain, w_router,
        routes, cotangent,
    )
    both = gather_step(spread(h_one), "a")

    def columns_of(start, number, low_first):
        pair = lax.dynamic_slice_in_dim(query_key_value_weight, start + number * 128, 128, 1)
        return jnp.where(low_first, pair[:, :64], pair[:, 64:])

    my_columns = jnp.concatenate(
        [
            columns_of(0, mine // 2, idd == 0),
            columns_of(1024, mine // 4, ic == 0),
            columns_of(1536, mine // 4, ic == 0),
            jnp.zeros((512, 64), bf16),
        ],
        1,
    )
    other_columns = swap(my_columns, "f")

    route = routes[0]
    named = jnp.any(route[:, :, None] == jnp.arange(E, dtype=jnp.int32)[None, None, :], axis=1)
    counts = spread(jnp.sum(named.astype(f32), axis=0, keepdims=True))
    named_b = named.astype(bf16)
    earlier = (jnp.arange(rows)[:, None] > jnp.arange(rows)[None, :]).astype(bf16)
    rank = jnp.dot(earlier, named_b, preferred_element_type=f32)
    row_of = jnp.where(named, rank, -1.0)
    counts = gather_step(counts, "a")
    expert_weights = jnp.concatenate([expert_in, expert_out], 1)
    both, row_of, cotangent, counts, expert_weights = together(
        both, row_of, cotangent, counts, expert_weights
    )
    low = gather_step(both[..., :512], "b")
    high = gather_step(both[..., 512:], "c")
    other_row_of = swap(row_of, "a")
    other_cotangent = swap(cotangent[0], "a")
    counts = gather_step(counts, "c")

    def picks(rows_of):
        half = rows_of.reshape(rows, 2, 2, 8)
        half = jnp.where(ia == 0, half[:, :, 0], half[:, :, 1])
        half = half.transpose(2, 1, 0).reshape(16, 1, rows)
        return (half == jnp.arange(MOST, dtype=f32)[None, :, None]).astype(bf16)

    def build_rows(choice, tokens):
        return lax.dot_general(
            choice, tokens, (((2,), (0,)), ((), ())), preferred_element_type=f32
        ).astype(bf16)

    def exchange(sent):
        return lax.all_to_all(sent, HALF, split_axis=0, concat_axis=0, tiled=True)

    low, high, other_columns, counts = together(low, high, other_columns, counts)
    low = gather_step(low, "c")
    high = gather_step(high, "b")
    counts = gather_step(counts, "b")
    out_part = share_swap(w_out)
    other_gain_two = swap(ffn_gain, "f")
    other_router = swap(w_router, "f")
    low, high, other_cotangent, other_row_of, counts, expert_weights, out_part = together(
        low, high, other_cotangent, other_row_of, counts, expert_weights, out_part
    )
    low_own = low.reshape(length // 2, 512)
    high_own = high.reshape(length // 2, 512)
    low_next = swap(low_own, "d")
    high_next = swap(high_own, "d")
    expert_weights = lax.all_to_all(
        expert_weights, CTX, split_axis=0, concat_axis=0, tiled=True
    )
    counts = gather_step(counts, "d")
    head_weight = in_order(my_columns, other_columns, "f", 0)

    order = block_order[0]
    blocks = order.shape[0]
    place = jnp.sum(
        jnp.where(order[None, :] == jnp.arange(blocks, dtype=jnp.int32)[:, None],
                  jnp.arange(blocks, dtype=jnp.int32)[None, :], 0),
        axis=1,
    )
    document = segment_ids[0]
    start = jnp.sum((document[:, None] < document[None, :]).astype(jnp.int32), axis=0)
    first_key = start[::QUERY_BLOCK] // QUERY_BLOCK
    start = start[None, :]
    steps = jnp.arange(HEAD_SIZE // 2, dtype=f32)
    frequency = jnp.power(THETA, -2.0 * steps / HEAD_SIZE)
    angle_a = (jnp.arange(length // 64, dtype=f32) * 64.0)[:, None] * frequency[None, :]
    angle_b = jnp.arange(64, dtype=f32)[:, None] * frequency[None, :]
    coarse = jnp.tile(jnp.stack([jnp.cos(angle_a), jnp.sin(angle_a)]), (1, 1, 4))
    fine = jnp.tile(jnp.stack([jnp.cos(angle_b), jnp.sin(angle_b)]), (1, 1, 4))
    storage = jnp.arange(blocks, dtype=jnp.int32)
    held = (((storage // 2) % 2) ^ idd) * (blocks // 2) + (storage // 4) * 2 + storage % 2
    h_place = jnp.sum(jnp.where(place[:, None] == storage[None, :], held[None, :], 0), axis=1)
    storage = jnp.arange(blocks, dtype=jnp.int32)
    held = (((storage // 2) % 2) ^ idd) * (blocks // 2) + (storage // 4) * 2 + storage % 2
    h_place = jnp.sum(jnp.where(place[:, None] == storage[None, :], held[None, :], 0), axis=1)
    head_weight, out_part, other_gain_two, other_router, query_key_value_weight = together(
        head_weight, out_part, other_gain_two, other_router, query_key_value_weight
    )
    weight_part = share_swap(query_key_value_weight)
    query, key, value, mixed, attended_head = whole_call(
        attention_forward,
        3,
        [
            jax.ShapeDtypeStruct((length, 128), bf16),
            jax.ShapeDtypeStruct((length, 128), bf16),
            jax.ShapeDtypeStruct((length, 128), bf16),
            jax.ShapeDtypeStruct((72, length), f32),
            jax.ShapeDtypeStruct((length, 64), bf16),
        ],
        [pltpu.VMEM((128, length), bf16)],
        32 << 20,
    )(
        place, h_place, first_key, low_own, high_own, low_next, high_next, head_weight, fine,
        coarse, start,
    )

    def to_tokens(value_heads):
        return lax.all_to_all(
            value_heads.reshape(16, rows, -1), CTX, split_axis=0, concat_axis=0, tiled=True
        )

    pick_mine = picks(row_of)
    pick_other = picks(other_row_of)
    grad_rows = jnp.concatenate(
        [build_rows(pick_mine, cotangent[0]), build_rows(pick_other, other_cotangent)], 1
    )
    out_full = share_join(w_out, out_part)
    gain_two_f = in_order(ffn_gain, other_gain_two, "f", 0).astype(f32)
    router_full = in_order(w_router, other_router, "f", 0)
    attended_head, expert_weights, grad_rows, out_full, weight_part, counts = together(
        attended_head, expert_weights, grad_rows, out_full, weight_part, counts
    )
    attended = to_tokens(attended_head)
    weight_full = share_join(query_key_value_weight, weight_part)
    attended, grad_rows = together(attended, grad_rows)
    grad_rows = exchange(grad_rows)
    attended = attended.transpose(1, 0, 2).reshape(rows, 1024)
    middle_state = inputs + jnp.dot(attended, out_full, preferred_element_type=f32)
    scale_two = rms_scale(middle_state)
    norm_two = middle_state * scale_two
    h_two = (norm_two * gain_two_f).astype(bf16)
    logits = jnp.dot(h_two, router_full, preferred_element_type=f32)
    top = jnp.max(jnp.where(named, logits, MASK_FILL_VALUE), axis=-1, keepdims=True)
    weights = jnp.where(named, jnp.exp(logits - top), 0.0)
    gates = weights / jnp.sum(weights, axis=-1, keepdims=True)
    passed = (jnp.arange(16)[:, None] < mine).astype(f32)
    offset = jnp.sum(counts.reshape(16, E) * passed, axis=0, keepdims=True)
    kept = (named & (rank + offset < capacity)).astype(f32)
    extended = jnp.concatenate(
        [h_two] + two_parts(gates * kept) + [jnp.zeros((rows, 2 * E), bf16)], 1
    )
    other_extended = swap(extended, "a")
    rows_mine = build_rows(pick_mine, extended)
    rows_mine, grad_rows, weight_full, other_extended = together(
        rows_mine, grad_rows, weight_full, other_extended
    )
    rows_mine = exchange(rows_mine)
    up_weight = expert_weights[:, :64].reshape(width, 2 * F)
    down_weight = expert_weights[:, 64:].reshape(F, width)
    grad_rows = grad_rows.reshape(16, 2, MOST, width)
    rows_other = build_rows(pick_other, other_extended)
    rows_mine, rows_other, up_weight, down_weight = together(
        rows_mine, rows_other, up_weight, down_weight
    )
    rows_other = exchange(rows_other)
    rows_mine = rows_mine.reshape(16 * MOST, width + EXTRA)
    number = expert.astype(jnp.int32)[None]
    copy_mine, result_mine, act_mine, pair_mine, pre_mine = expert_call(
        0, number, rows_mine, grad_rows, up_weight, down_weight
    )
    rows_other, copy_mine = together(rows_other, copy_mine)
    rows_other = rows_other.reshape(16 * MOST, width + EXTRA)
    copy_other, result_other, act_other, pair_other, pre_other = expert_call(
        1, number, rows_other, grad_rows, up_weight, down_weight
    )

    def sum_rows(choice, got):
        return lax.dot_general(
            choice, got, (((0, 1), (0, 1)), ((), ())), preferred_element_type=f32
        )

    away = exchange(copy_other.reshape(16, MOST, width + EXTRA))
    away, copy_mine = together(away, copy_mine)
    home = exchange(copy_mine.reshape(16, MOST, width + EXTRA))
    grad_up_weight = contract_rows(rows_mine[:, :width], pre_mine) + contract_rows(
        rows_other[:, :width], pre_other
    )
    grad_down = contract_rows(act_mine, pair_mine) + contract_rows(act_other, pair_other)
    expert_grads = jnp.concatenate(
        [
            grad_up_weight.astype(bf16).reshape(16, 64, 2 * F),
            grad_down.astype(bf16).reshape(16, 32, width),
        ],
        1,
    )
    away_sum = swap(sum_rows(pick_other, away).astype(bf16), "a")
    home, away_sum, expert_grads = together(home, away_sum, expert_grads)
    back = sum_rows(pick_mine, home) + away_sum.astype(f32)

    gate_grads = (back[:, width : width + E] + back[:, width + E : width + 2 * E]) * kept
    grad_logits = gates * (gate_grads - jnp.sum(gates * gate_grads, axis=-1, keepdims=True))
    grad_h_two = back[:, :width] + lax.dot_general(
        grad_logits, router_full.astype(f32), (((1,), (1,)), ((), ())), precision=HIGHEST
    )
    grad_out = cotangent[0].astype(f32)
    scaled_two = grad_h_two * gain_two_f
    grad_mid = grad_out + scale_two * (
        scaled_two - norm_two * jnp.mean(scaled_two * norm_two, axis=-1, keepdims=True)
    )
    grad_branch = grad_mid.astype(bf16)
    attended_gradient = contract_columns(grad_branch, out_full).astype(bf16)
    grad_heads = to_tokens(attended_gradient.reshape(rows, 16, 64).transpose(1, 0, 2))
    grad_heads = grad_heads.reshape(length, 64)

    by_core = attended.reshape(rows, 2, 2, 256)
    keep = lax.dynamic_slice_in_dim(by_core, idd, 1, 2).reshape(rows, 512)
    send = lax.dynamic_slice_in_dim(by_core, 1 - idd, 1, 2).reshape(rows, 512)
    out_sum = contract_rows(keep, grad_branch) + swap(
        contract_rows(send, grad_branch).astype(bf16), "d"
    ).astype(f32)

    def halve(total, axis):
        count = total.shape[0] // 2
        index = lax.axis_index(axis)
        keep = lax.dynamic_slice_in_dim(total, index * count, count, 0)
        send = lax.dynamic_slice_in_dim(total, (1 - index) * count, count, 0)
        return keep + swap(send.astype(bf16), axis).astype(f32)

    grad_router_part = lax.dot_general(
        grad_logits, h_two.astype(f32), (((0,), (0,)), ((), ())), precision=HIGHEST
    )
    grad_gain_two = jnp.sum(grad_h_two * norm_two, axis=0, keepdims=True)
    small = jnp.concatenate([grad_router_part, jnp.broadcast_to(grad_gain_two, (8, width))], 0)
    grad_heads, expert_grads = together(grad_heads, expert_grads)
    expert_grads = lax.all_to_all(expert_grads, CTX, split_axis=0, concat_axis=0, tiled=True)

    keep, send = whole_call(
        attention_backward,
        3,
        [jax.ShapeDtypeStruct((length, 128), f32), jax.ShapeDtypeStruct((length, 128), bf16)],
        [
            pltpu.VMEM((64, length), bf16),
            pltpu.VMEM((length, 128), f32),
            pltpu.VMEM((length, 128), f32),
        ],
        32 << 20,
    )(
        place, first_key, idd.astype(jnp.int32)[None], query, key, value, mixed, grad_heads,
        fine, coarse, start,
    )
    keep, send, out_sum, small = together(keep, send, out_sum, small)
    grad_columns = (keep + swap(send, "d").astype(f32)).astype(bf16)
    out_sum = halve(out_sum, "f")
    small = small + swap(small, "d")
    small = small + swap(small, "f")
    ready, expert_grads, out_sum = together(grad_columns, expert_grads, out_sum)
    grad_projected = to_tokens(ready)
    for axis in ("c", "b", "a"):
        out_sum = halve(out_sum, axis)
    out_rows = out_sum.reshape(32, 8, 128).transpose(1, 0, 2).reshape(256, 128).astype(bf16)

    by_core = grad_columns.reshape(8, 2, rows, 128)
    own = jnp.where(idd == 0, by_core[:, 0], by_core[:, 1]).reshape(length // 2, 128)
    following = jnp.where(idd == 0, by_core[:, 1], by_core[:, 0]).reshape(length // 2, 128)
    low_part = contract_rows(low_own, own) + contract_rows(low_next, following)
    high_part = contract_rows(high_own, own) + contract_rows(high_next, following)
    columns_grad = jnp.where(low_half, low_part, high_part) + swap(
        jnp.where(low_half, high_part, low_part), "f"
    )
    my_weight = jnp.concatenate(
        [my_columns[:, :64], jnp.where(idd == 0, my_columns[:, 64:128], my_columns[:, 128:192])], 1
    )
    gain_part = jnp.sum(columns_grad * my_weight.astype(f32), axis=1).reshape(4, 128)
    gain_part = jnp.concatenate([gain_part, jnp.zeros((4, 128), f32)], 0)
    columns_grad = jnp.concatenate(
        [columns_grad.astype(bf16), out_rows] + two_parts(gain_part), 0
    )
    gathered = gather_step(spread(columns_grad), "a")
    first = gather_step(gathered[..., :384, :], "b")
    second = gather_step(gathered[..., 384:, :], "c")
    first = gather_step(first, "c")
    second = gather_step(second, "b")
    results = jnp.concatenate(
        [result_mine.reshape(16, MOST, width), result_other.reshape(16, MOST, width)], 1
    )
    grad_expert_in = expert_grads[:, :64].astype(f32)
    grad_expert_out = expert_grads[:, 64:].astype(f32)
    grad_projected, results, small, grad_expert_in, grad_expert_out, first, second = together(
        grad_projected, results, small, grad_expert_in, grad_expert_out, first, second
    )
    results = exchange(results)
    first = gather_step(first, "d")
    second = gather_step(second, "d")
    for axis in ("c", "b", "a"):
        small = small + swap(small, axis)

    grad_projected = grad_projected.transpose(1, 0, 2)
    grad_kv = grad_projected[:, :, 64:].reshape(rows, 8, 2, 64)
    grad_projected = jnp.concatenate(
        [
            grad_projected[:, :, :64].reshape(rows, 1024),
            grad_kv[:, :, 0].reshape(rows, 512),
            grad_kv[:, :, 1].reshape(rows, 512),
        ],
        1,
    )
    grad_h_one = contract_columns(grad_projected, weight_full)
    scaled_one = grad_h_one * gain_one_f
    grad_inputs = grad_mid + scale_one * (
        scaled_one - norm_one * jnp.mean(scaled_one * norm_one, axis=-1, keepdims=True)
    )
    small = jnp.where(low_half, small[:, :512], small[:, 512:])
    share_router = small[:E].T
    share_two = small[E]
    share_qkv, share_out, gain_sum = whole_call(
        assemble,
        0,
        [
            jax.ShapeDtypeStruct((512, 2048), f32),
            jax.ShapeDtypeStruct((512, 1024), f32),
            jax.ShapeDtypeStruct((8, 128), f32),
        ],
        [],
        32 << 20,
    )(first.reshape(16, 384, 128), second.reshape(16, 400, 128))
    share_one = gain_sum[:4].reshape(512) / attn_gain.astype(f32)
    mixture = sum_rows(pick_mine, results[:, :MOST]) + swap(
        sum_rows(pick_other, results[:, MOST:]).astype(bf16), "a"
    ).astype(f32)
    hidden_out = (middle_state + mixture).astype(bf16)
    return (
        hidden_out[None],
        grad_inputs[None],
        share_one,
        share_qkv,
        share_out,
        share_two,
        share_router,
        grad_expert_in,
        grad_expert_out,
    )


def fast_solution(mesh):
    fine = Mesh(mesh.devices.reshape(2, 2, 2, 2, 2), EVERY)
    placed = (
        P("f", CTX, None),
        P("f", None),
        P("f", None),
        P("f", CTX, None),
        P("f"),
        P("f", None),
        P("f", None),
        P("f"),
        P("f", None),
        P("f", CTX, None),
        P("f", CTX, None),
        P("f", CTX, None),
    )
    return jax.shard_map(
        fast_shards,
        mesh=fine,
        in_specs=placed,
        out_specs=(
            P("f", CTX, None),
            P("f", CTX, None),
            P("f"),
            P("f", None),
            P("f", None),
            P("f"),
            P("f", None),
            P("f", CTX, None),
            P("f", CTX, None),
        ),
        check_vma=False,
    )


def solution(mesh):
    if mesh.shape["ctx"] == QUERY_HEADS and mesh.shape["fsdp"] * mesh.shape["ctx"] == E:
        return fast_solution(mesh)
    return general_solution(mesh)
```

```python
import math

import jax
import jax.numpy as jnp
from jax import lax
from jax.experimental import pallas as pl
from jax.experimental.pallas import tpu as pltpu
from jax.sharding import Mesh
from jax.sharding import PartitionSpec as P

QUERY_HEADS = 16
KEY_VALUE_HEADS = 8
HEAD_SIZE = 64
E = 32
TOPK = 8
F = 512
MOST = 48


EPSILON = 1e-06
THETA = 10000.0
MASK_FILL_VALUE = -1e30
HIGHEST = lax.Precision.HIGHEST


def carried_in(value, axis, combine, identity):
    length, mine = (lax.axis_size(axis), lax.axis_index(axis))
    everything = lax.all_gather(value, axis)
    start = jnp.broadcast_to(jnp.asarray(identity, value.dtype), value.shape)

    def turn(k, before):
        reached = k < mine
        new = combine(before, everything[k])
        return jnp.where(reached, new, before)

    return lax.fori_loop(0, length, turn, start)


def rms_scale(value_rows):
    return lax.rsqrt(jnp.mean(value_rows * value_rows, axis=-1, keepdims=True) + EPSILON)


def rotate(value_rows):
    middle = value_rows.shape[-1] // 2
    return jnp.concatenate([-value_rows[..., middle:], value_rows[..., :middle]], axis=-1)


def rotate_back(value_rows):
    middle = value_rows.shape[-1] // 2
    return jnp.concatenate([value_rows[..., middle:], -value_rows[..., :middle]], axis=-1)


def rope_tables(position):
    steps = jnp.arange(HEAD_SIZE // 2, dtype=jnp.float32)
    frequency = jnp.power(THETA, -2.0 * steps / HEAD_SIZE)
    angle = position.astype(jnp.float32)[:, None] * frequency[None, :]
    angle = jnp.concatenate([angle, angle], axis=-1)
    return (jnp.cos(angle), jnp.sin(angle))


def contract_rows(left, right):
    return lax.dot_general(
        left, right, (((0,), (0,)), ((), ())), preferred_element_type=jnp.float32
    )


def contract_columns(left, right):
    return lax.dot_general(
        left, right, (((1,), (1,)), ((), ())), preferred_element_type=jnp.float32
    )


def own_rows(total, rank, count):
    share = total.shape[0] // count
    return lax.dynamic_slice_in_dim(total, rank * share, share, 0)


def general_shards(
    hidden_in,
    block_order,
    segment_ids,
    cotangent,
    attn_gain,
    query_key_value_weight,
    w_out,
    ffn_gain,
    w_router,
    routes,
    expert_in,
    expert_out,
):
    count_of_rows = hidden_in.shape[1]
    width = hidden_in.shape[2]
    ctx_count = lax.axis_size("ctx")
    fsdp_count = lax.axis_size("fsdp")
    sequence_length = count_of_rows * ctx_count
    half_block = count_of_rows // 2
    capacity = sequence_length * TOPK * 9 // (8 * E)
    query_total_width = QUERY_HEADS * HEAD_SIZE
    key_total_width = KEY_VALUE_HEADS * HEAD_SIZE
    query_group = QUERY_HEADS // KEY_VALUE_HEADS
    scale = 1.0 / math.sqrt(HEAD_SIZE)
    key_block_rows = min(1024, sequence_length)
    block_count = sequence_length // key_block_rows
    pair_count = count_of_rows * TOPK
    gain_one, qkv_full, out_full, gain_two, router_full = (
        lax.all_gather(attn_gain, "fsdp", axis=0, tiled=True),
        lax.all_gather(query_key_value_weight, "fsdp", axis=0, tiled=True),
        lax.all_gather(w_out, "fsdp", axis=0, tiled=True),
        lax.all_gather(ffn_gain, "fsdp", axis=0, tiled=True),
        lax.all_gather(w_router, "fsdp", axis=0, tiled=True),
    )
    up_full, down_full = (
        lax.all_gather(expert_in, "ctx", axis=1, tiled=True),
        lax.all_gather(expert_out, "ctx", axis=1, tiled=True),
    )
    key_position = (
        block_order[0][:, None] * half_block + jnp.arange(half_block, dtype=jnp.int32)[None, :]
    ).reshape(-1)
    key_document = segment_ids[0][key_position]
    first_row = lax.axis_index("ctx") * count_of_rows
    query_position = lax.dynamic_slice_in_dim(key_position, first_row, count_of_rows, 0)
    query_document = lax.dynamic_slice_in_dim(key_document, first_row, count_of_rows, 0)
    inputs = hidden_in[0].astype(jnp.float32)
    grad_out = cotangent[0].astype(jnp.float32)
    scale_one = rms_scale(inputs)
    norm_one = inputs * scale_one
    gain_one_f = gain_one.astype(jnp.float32)
    h_one = (norm_one * gain_one_f).astype(jnp.bfloat16)
    projected_rows = jnp.dot(h_one, qkv_full, preferred_element_type=jnp.float32)
    cosine, sine = rope_tables(query_position)
    query_raw = projected_rows[:, :query_total_width].reshape(count_of_rows, QUERY_HEADS, HEAD_SIZE)
    unrotated_key = projected_rows[
        :, query_total_width : query_total_width + key_total_width
    ].reshape(count_of_rows, KEY_VALUE_HEADS, HEAD_SIZE)
    query_matrix = (query_raw * cosine[:, None, :] + rotate(query_raw) * sine[:, None, :]).astype(
        jnp.bfloat16
    )
    key_rows = (
        unrotated_key * cosine[:, None, :] + rotate(unrotated_key) * sine[:, None, :]
    ).astype(jnp.bfloat16)
    value_rows = projected_rows[:, query_total_width + key_total_width :].astype(jnp.bfloat16)
    key_value_local = jnp.concatenate(
        [key_rows.reshape(count_of_rows, key_total_width), value_rows], axis=1
    )
    key_value_all = lax.all_gather(key_value_local, "ctx", axis=0, tiled=True)
    grouped_queries = query_matrix.reshape(count_of_rows, KEY_VALUE_HEADS, query_group, HEAD_SIZE)
    block_number = jnp.arange(block_count, dtype=jnp.int32)

    def block_keys(source, index):
        current_rows = lax.dynamic_slice_in_dim(source, index * key_block_rows, key_block_rows, 0)
        block_key_rows = current_rows[:, :key_total_width].reshape(
            key_block_rows, KEY_VALUE_HEADS, HEAD_SIZE
        )
        block_value_rows = current_rows[:, key_total_width:].reshape(
            key_block_rows, KEY_VALUE_HEADS, HEAD_SIZE
        )
        block_position = lax.dynamic_slice_in_dim(
            key_position, index * key_block_rows, key_block_rows, 0
        )
        block_document = lax.dynamic_slice_in_dim(
            key_document, index * key_block_rows, key_block_rows, 0
        )
        allowed = (query_document[:, None] == block_document[None, :]) & (
            block_position[None, :] <= query_position[:, None]
        )
        return (block_key_rows, block_value_rows, allowed)

    def scores_of(block_key_rows, allowed):
        scores = (
            jnp.einsum(
                "qhgd,khd->hgqk",
                grouped_queries,
                block_key_rows,
                preferred_element_type=jnp.float32,
            )
            * scale
        )
        return jnp.where(allowed[None, None], scores, MASK_FILL_VALUE)

    def max_sum(carry, index):
        top, total = carry
        block_key_rows, block_value_rows, allowed = block_keys(key_value_all, index)
        scores = scores_of(block_key_rows, allowed)
        new_top = jnp.maximum(top, jnp.max(scores, axis=-1))
        weights = jnp.where(allowed[None, None], jnp.exp(scores - new_top[..., None]), 0.0)
        total = total * jnp.exp(top - new_top) + jnp.sum(weights, axis=-1)
        return ((new_top, total), None)

    upper_start = jnp.full(
        (KEY_VALUE_HEADS, query_group, count_of_rows), MASK_FILL_VALUE, jnp.float32
    )
    overall_start = jnp.zeros((KEY_VALUE_HEADS, query_group, count_of_rows), jnp.float32)
    (top, total), unused = lax.scan(max_sum, (upper_start, overall_start), block_number)
    log_total = top + jnp.log(total)

    def weighted_values(accum, index):
        block_key_rows, block_value_rows, allowed = block_keys(key_value_all, index)
        scores = scores_of(block_key_rows, allowed)
        probs = jnp.where(allowed[None, None], jnp.exp(scores - log_total[..., None]), 0.0).astype(
            jnp.bfloat16
        )
        return (
            accum
            + jnp.einsum(
                "hgqk,khd->qhgd", probs, block_value_rows, preferred_element_type=jnp.float32
            ),
            None,
        )

    attended_f, unused = lax.scan(
        weighted_values,
        jnp.zeros((count_of_rows, KEY_VALUE_HEADS, query_group, HEAD_SIZE), jnp.float32),
        block_number,
    )
    attended = attended_f.reshape(count_of_rows, query_total_width).astype(jnp.bfloat16)
    middle_state = inputs + jnp.dot(attended, out_full, preferred_element_type=jnp.float32)
    scale_two = rms_scale(middle_state)
    norm_two = middle_state * scale_two
    gain_two_f = gain_two.astype(jnp.float32)
    h_two = (norm_two * gain_two_f).astype(jnp.bfloat16)
    logits = jnp.dot(h_two, router_full, preferred_element_type=jnp.float32)
    route = routes[0]
    gates = jax.nn.softmax(jnp.take_along_axis(logits, route, axis=1), axis=-1)
    flat = route.reshape(-1)
    onehot = (flat[:, None] == jnp.arange(E, dtype=jnp.int32)[None, :]).astype(jnp.int32)
    rank = jnp.sum((jnp.cumsum(onehot, axis=0) - onehot) * onehot, axis=1)
    counts = jnp.sum(onehot, axis=0)

    def add_counts(earlier, later):
        return earlier + later

    offsets = carried_in(counts, "ctx", add_counts, jnp.zeros((E,), jnp.int32))
    slot = jnp.sum(onehot * offsets[None, :], axis=1) + rank
    kept = slot < capacity
    target = jnp.where(kept, flat * MOST + rank, E * MOST)
    safe_target = jnp.minimum(target, E * MOST - 1)
    keep_float = kept.astype(jnp.float32)[:, None]
    token = jnp.arange(pair_count, dtype=jnp.int32) // TOPK
    send_rows = (
        jnp.zeros((E * MOST, width), jnp.bfloat16)
        .at[target]
        .set(h_two[token], mode="drop")
        .reshape(E, MOST, width)
    )
    received = lax.all_to_all(send_rows, "fsdp", split_axis=0, concat_axis=1, tiled=True)
    before = jnp.einsum("erd,edf->erf", received, up_full, preferred_element_type=jnp.float32)
    gate_pre = before[..., :F]
    up_pre = before[..., F:]
    sigma = jax.nn.sigmoid(gate_pre)
    activation = (gate_pre * sigma * up_pre).astype(jnp.bfloat16)
    expert_result = jnp.einsum(
        "erf,efd->erd", activation, down_full, preferred_element_type=jnp.float32
    ).astype(jnp.bfloat16)
    returned = lax.all_to_all(
        expert_result, "fsdp", split_axis=1, concat_axis=0, tiled=True
    ).reshape(E * MOST, width)
    pair_result = (returned[safe_target].astype(jnp.float32) * keep_float).reshape(
        count_of_rows, TOPK, width
    )
    mixture = jnp.sum(gates[..., None] * pair_result, axis=1)
    hidden_out = (middle_state + mixture).astype(jnp.bfloat16)
    grad_pair = (
        (gates[..., None] * grad_out[:, None, :]).reshape(pair_count, width) * keep_float
    ).astype(jnp.bfloat16)
    grad_gates = jnp.sum(grad_out[:, None, :] * pair_result, axis=-1)
    grad_chosen = gates * (grad_gates - jnp.sum(gates * grad_gates, axis=-1, keepdims=True))
    chosen_table = (route[..., None] == jnp.arange(E, dtype=jnp.int32)[None, None, :]).astype(
        jnp.float32
    )
    grad_logits = jnp.sum(grad_chosen[..., None] * chosen_table, axis=1)
    grad_router_part = lax.dot_general(
        h_two.astype(jnp.float32), grad_logits, (((0,), (0,)), ((), ())), precision=HIGHEST
    )
    grad_h_two = lax.dot_general(
        grad_logits, router_full.astype(jnp.float32), (((1,), (1,)), ((), ())), precision=HIGHEST
    )
    send_grads = (
        jnp.zeros((E * MOST, width), jnp.bfloat16)
        .at[target]
        .set(grad_pair, mode="drop")
        .reshape(E, MOST, width)
    )
    grad_received = lax.all_to_all(send_grads, "fsdp", split_axis=0, concat_axis=1, tiled=True)
    grad_activation = jnp.einsum(
        "erd,efd->erf", grad_received, down_full, preferred_element_type=jnp.float32
    )
    grad_down = jnp.einsum(
        "erf,erd->efd", activation, grad_received, preferred_element_type=jnp.float32
    )
    grad_gate = grad_activation * up_pre * sigma * (1.0 + gate_pre * (1.0 - sigma))
    grad_up = grad_activation * gate_pre * sigma
    grad_pre = jnp.concatenate([grad_gate, grad_up], axis=-1).astype(jnp.bfloat16)
    grad_up_weight = jnp.einsum(
        "erd,erf->edf", received, grad_pre, preferred_element_type=jnp.float32
    )
    grad_copy = jnp.einsum(
        "erf,edf->erd", grad_pre, up_full, preferred_element_type=jnp.float32
    ).astype(jnp.bfloat16)
    grad_returned = lax.all_to_all(
        grad_copy, "fsdp", split_axis=1, concat_axis=0, tiled=True
    ).reshape(E * MOST, width)
    grad_h_two = grad_h_two + jnp.sum(
        (grad_returned[safe_target].astype(jnp.float32) * keep_float).reshape(
            count_of_rows, TOPK, width
        ),
        axis=1,
    )
    grad_expert_in, grad_expert_out = (
        lax.psum_scatter(
            grad_up_weight.astype(jnp.bfloat16), "ctx", scatter_dimension=1, tiled=True
        ).astype(jnp.float32),
        lax.psum_scatter(
            grad_down.astype(jnp.bfloat16), "ctx", scatter_dimension=1, tiled=True
        ).astype(jnp.float32),
    )
    grad_gain_two = jnp.sum(grad_h_two * norm_two, axis=0)
    scaled_two = grad_h_two * gain_two_f
    grad_mid = grad_out + scale_two * (
        scaled_two - norm_two * jnp.mean(scaled_two * norm_two, axis=-1, keepdims=True)
    )
    grad_branch = grad_mid.astype(jnp.bfloat16)
    grad_out_weight = contract_rows(attended, grad_branch)
    attended_gradient = contract_columns(grad_branch, out_full).astype(jnp.bfloat16)
    grouped_gradient = attended_gradient.reshape(
        count_of_rows, KEY_VALUE_HEADS, query_group, HEAD_SIZE
    )
    delta = jnp.transpose(
        jnp.sum(grouped_gradient.astype(jnp.float32) * attended_f, axis=-1), (1, 2, 0)
    )

    def block_gradients(query_accum, index):
        block_key_rows, block_value_rows, allowed = block_keys(key_value_all, index)
        scores = scores_of(block_key_rows, allowed)
        probs = jnp.where(allowed[None, None], jnp.exp(scores - log_total[..., None]), 0.0)
        grad_probs = jnp.einsum(
            "qhgd,khd->hgqk", grouped_gradient, block_value_rows, preferred_element_type=jnp.float32
        )
        grad_scores = (probs * (grad_probs - delta[..., None])).astype(jnp.bfloat16)
        query_accum = query_accum + jnp.einsum(
            "hgqk,khd->qhgd", grad_scores, block_key_rows, preferred_element_type=jnp.float32
        )
        grad_keys = (
            jnp.einsum(
                "hgqk,qhgd->khd", grad_scores, grouped_queries, preferred_element_type=jnp.float32
            )
            * scale
        )
        grad_values = jnp.einsum(
            "hgqk,qhgd->khd",
            probs.astype(jnp.bfloat16),
            grouped_gradient,
            preferred_element_type=jnp.float32,
        )
        joined = jnp.concatenate(
            [
                grad_keys.reshape(key_block_rows, key_total_width),
                grad_values.reshape(key_block_rows, key_total_width),
            ],
            axis=1,
        )
        return (query_accum, joined)

    grad_queries, grad_blocks = lax.scan(
        block_gradients,
        jnp.zeros((count_of_rows, KEY_VALUE_HEADS, query_group, HEAD_SIZE), jnp.float32),
        block_number,
    )
    key_value_gradient = lax.psum_scatter(
        grad_blocks.reshape(sequence_length, 2 * key_total_width).astype(jnp.bfloat16),
        "ctx",
        scatter_dimension=0,
        tiled=True,
    ).astype(jnp.float32)
    grad_queries = (grad_queries * scale).reshape(count_of_rows, QUERY_HEADS, HEAD_SIZE)
    local_key_gradient = key_value_gradient[:, :key_total_width].reshape(
        count_of_rows, KEY_VALUE_HEADS, HEAD_SIZE
    )
    grad_values_mine = key_value_gradient[:, key_total_width:]
    grad_query_pre = grad_queries * cosine[:, None, :] + rotate_back(
        grad_queries * sine[:, None, :]
    )
    grad_key_pre = local_key_gradient * cosine[:, None, :] + rotate_back(
        local_key_gradient * sine[:, None, :]
    )
    grad_projected = jnp.concatenate(
        [
            grad_query_pre.reshape(count_of_rows, query_total_width),
            grad_key_pre.reshape(count_of_rows, key_total_width),
            grad_values_mine,
        ],
        axis=1,
    ).astype(jnp.bfloat16)
    grad_qkv_weight = contract_rows(h_one, grad_projected)
    grad_h_one = contract_columns(grad_projected, qkv_full)
    grad_gain_one = jnp.sum(grad_h_one * norm_one, axis=0)
    scaled_one = grad_h_one * gain_one_f
    grad_inputs = grad_mid + scale_one * (
        scaled_one - norm_one * jnp.mean(scaled_one * norm_one, axis=-1, keepdims=True)
    )
    total_one, total_qkv, total_out, total_two, total_router = lax.psum(
        (grad_gain_one, grad_qkv_weight, grad_out_weight, grad_gain_two, grad_router_part),
        ("ctx", "fsdp"),
    )
    fsdp_rank = lax.axis_index("fsdp")
    share_one = own_rows(total_one, fsdp_rank, fsdp_count)
    share_qkv = own_rows(total_qkv, fsdp_rank, fsdp_count)
    share_out = own_rows(total_out, fsdp_rank, fsdp_count)
    share_two = own_rows(total_two, fsdp_rank, fsdp_count)
    share_router = own_rows(total_router, fsdp_rank, fsdp_count)
    return (
        hidden_out[None],
        grad_inputs[None],
        share_one,
        share_qkv,
        share_out,
        share_two,
        share_router,
        grad_expert_in,
        grad_expert_out,
    )


def general_solution(mesh):
    placed = (
        P("fsdp", "ctx", None),
        P("fsdp", None),
        P("fsdp", None),
        P("fsdp", "ctx", None),
        P("fsdp"),
        P("fsdp", None),
        P("fsdp", None),
        P("fsdp"),
        P("fsdp", None),
        P("fsdp", "ctx", None),
        P("fsdp", "ctx", None),
        P("fsdp", "ctx", None),
    )
    return jax.shard_map(
        general_shards,
        mesh=mesh,
        in_specs=placed,
        out_specs=(
            P("fsdp", "ctx", None),
            P("fsdp", "ctx", None),
            P("fsdp"),
            P("fsdp", None),
            P("fsdp", None),
            P("fsdp"),
            P("fsdp", None),
            P("fsdp", "ctx", None),
            P("fsdp", "ctx", None),
        ),
        check_vma=False,
    )


CTX = ("a", "b", "c", "d")
HALF = ("b", "c", "d", "f")
EVERY = ("a", "b", "c", "d", "f")
QUERY_BLOCK = 256
EXTRA = 128


def swap(value, axis):
    return lax.ppermute(value, axis, [(0, 1), (1, 0)])


def in_order(mine, other, axis, dim):
    first = lax.axis_index(axis) == 0
    return jnp.where(
        first, jnp.concatenate([mine, other], dim), jnp.concatenate([other, mine], dim)
    )


def join(value, axis, dim=0):
    return in_order(value, swap(value, axis), axis, dim)


def spread(value):
    return value[(None,) * 4]


def gather_step(held, axis):
    return in_order(held, swap(held, axis), axis, CTX.index(axis))


def share_swap(value):
    half = value.shape[0] // 2
    part = swap(jnp.where(lax.axis_index("d") == 0, value[:half], value[half:]), "f")
    return part


def share_join(value, part):
    return in_order(value, join(part, "d"), "f", 0)


def sum_everywhere(value):
    for axis in ("d", "f", "c", "b", "a"):
        value = value + swap(value, axis)
    return value


def together(*values):
    return lax.optimization_barrier(values)


def two_parts(value):
    high = lax.reduce_precision(value, 8, 7)
    return [high.astype(jnp.bfloat16), (value - high).astype(jnp.bfloat16)]


def angles(number, fine, coarse):
    cos_b, sin_b = fine[0], fine[1]
    cos_a = coarse[0, pl.ds(number, 1), :]
    sin_a = coarse[1, pl.ds(number, 1), :]
    return cos_a * cos_b - sin_a * sin_b, sin_a * cos_b + cos_a * sin_b


def block_angles(chunk, pieces, fine, coarse):
    pairs = [angles(chunk * pieces + n, fine, coarse) for n in range(pieces)]
    return (
        jnp.concatenate([one[0] for one in pairs], 0),
        jnp.concatenate([one[1] for one in pairs], 0),
    )


def lane_of(shape):
    return lax.broadcasted_iota(jnp.int32, shape, 1)


def attention_forward(
    place, h_place, first_key, low_own, high_own, low_next, high_next, weight, fine, coarse,
    start, query_out, key_out, value_out, mixed_out, attended_out, value_t,
):
    rows = query_out.shape[0]
    block = QUERY_BLOCK
    pieces = block // 64

    def project(chunk, carry):
        def rows_of(own, following):
            found = []
            for n in range(pieces):
                spot = h_place[chunk * pieces + n]
                at = pl.ds(pl.multiple_of((spot % 16) * 64, 64), 64)
                found.append(jnp.where(spot < 16, own[at, :], following[at, :]))
            return jnp.concatenate(found, 0)

        low = rows_of(low_own, low_next)
        high = rows_of(high_own, high_next)
        here = pl.ds(pl.multiple_of(chunk * block, block), block)
        both = jnp.dot(low, weight[:512, :], preferred_element_type=jnp.float32) + jnp.dot(
            high, weight[512:, :], preferred_element_type=jnp.float32
        )
        pair = both[:, :128]
        values = both[:, 128:].astype(jnp.bfloat16)
        lane = lane_of((block, 128))
        turned = jnp.where(
            lane % 64 < 32, -pltpu.roll(pair, 96, 1), pltpu.roll(pair, 32, 1)
        )
        cosine, sine = block_angles(chunk, pieces, fine, coarse)
        pair = pair * cosine + turned * sine
        pair = pair.astype(jnp.bfloat16).astype(jnp.float32)
        key_out[here, :] = jnp.where(lane >= 64, pair, 0.0).astype(jnp.bfloat16)
        query_out[here, :] = jnp.where(
            lane >= 64, pltpu.roll(pair, 64, 1) * (1.0 / math.sqrt(HEAD_SIZE)), 0.0
        ).astype(jnp.bfloat16)
        value_out[here, :] = values
        turned_values = jnp.transpose(values.astype(jnp.float32))
        ones = lax.broadcasted_iota(jnp.int32, (128, block), 0) == 64
        value_t[:, here] = jnp.where(ones, 1.0, turned_values).astype(jnp.bfloat16)
        return carry

    lax.fori_loop(0, rows // block, project, 0)

    def attend(number, carry):
        here = pl.ds(pl.multiple_of(number * block, block), block)
        queries = query_out[here, :]
        begin = start[:, here]
        query_at = lax.broadcasted_iota(jnp.int32, (block, block), 1) + number * block

        def turn(key_number, state):
            top, total = state
            there = pl.ds(pl.multiple_of(key_number * block, block), block)
            scores = lax.dot_general(
                key_out[there, :], queries, (((1,), (1,)), ((), ())),
                preferred_element_type=jnp.float32,
            )
            key_at = lax.broadcasted_iota(jnp.int32, (block, block), 0) + key_number * block
            allowed = (key_at >= begin) & (key_at <= query_at)
            scores = jnp.where(allowed, scores, MASK_FILL_VALUE)
            new_top = jnp.maximum(top, jnp.max(scores, axis=0, keepdims=True))
            weights = jnp.exp(scores - new_top).astype(jnp.bfloat16)
            total = total * jnp.exp(top - new_top) + jnp.dot(
                value_t[:, there], weights, preferred_element_type=jnp.float32
            )
            return new_top, total

        top, total = lax.fori_loop(
            first_key[number],
            number + 1,
            turn,
            (
                jnp.full((1, block), MASK_FILL_VALUE, jnp.float32),
                jnp.zeros((128, block), jnp.float32),
            ),
        )
        weight_sum = total[64:65, :]
        mixed = total * (1.0 / weight_sum)
        log_total = top + jnp.log(weight_sum)
        mixed_out[:64, here] = mixed[:64, :]
        mixed_out[64:72, here] = jnp.broadcast_to(log_total, (8, block))
        upright = jnp.transpose(mixed)[:, :64].astype(jnp.bfloat16)
        for n in range(pieces):
            rows_there = pl.ds(pl.multiple_of(place[number * pieces + n] * 64, 64), 64)
            attended_out[rows_there, :] = upright[n * 64 : (n + 1) * 64, :]
        return carry

    lax.fori_loop(0, rows // block, attend, 0)


def attention_backward(
    place, first_key, core, query, key, value, mixed, grad, fine, coarse, start,
    keep_out, send_out, key_t, pair_sum, value_sum,
):
    rows = query.shape[0]
    block = QUERY_BLOCK
    pieces = block // 64
    scale = 1.0 / math.sqrt(HEAD_SIZE)

    def prepare(chunk, carry):
        here = pl.ds(pl.multiple_of(chunk * block, block), block)
        turned = jnp.transpose(key[here, :].astype(jnp.float32))
        key_t[:, here] = turned[64:, :].astype(jnp.bfloat16)
        pair_sum[here, :] = jnp.zeros((block, 128), jnp.float32)
        value_sum[here, :] = jnp.zeros((block, 128), jnp.float32)
        return carry

    lax.fori_loop(0, rows // block, prepare, 0)

    def storage(number):
        return [
            pl.ds(pl.multiple_of(place[number * pieces + n] * 64, 64), 64) for n in range(pieces)
        ]

    def attend(number, carry):
        here = pl.ds(pl.multiple_of(number * block, block), block)
        queries = query[here, :]
        incoming = jnp.concatenate([grad[one, :] for one in storage(number)], 0)
        nothing = jnp.zeros((block, 64), jnp.bfloat16)
        padded = jnp.concatenate([incoming, nothing], 1)
        upper = jnp.concatenate([nothing, incoming], 1)
        incoming_t = jnp.transpose(padded.astype(jnp.float32))[:64, :]
        log_total = mixed[64:65, here]
        delta = jnp.sum(incoming_t * mixed[:64, here], axis=0, keepdims=True)
        begin = start[:, here]
        query_at = lax.broadcasted_iota(jnp.int32, (block, block), 1) + number * block

        def turn(key_number, total):
            there = pl.ds(pl.multiple_of(key_number * block, block), block)
            scores = lax.dot_general(
                key[there, :], queries, (((1,), (1,)), ((), ())),
                preferred_element_type=jnp.float32,
            )
            key_at = lax.broadcasted_iota(jnp.int32, (block, block), 0) + key_number * block
            allowed = (key_at >= begin) & (key_at <= query_at)
            probs = jnp.where(allowed, jnp.exp(scores - log_total), 0.0)
            grad_probs = lax.dot_general(
                value[there, :], padded, (((1,), (1,)), ((), ())),
                preferred_element_type=jnp.float32,
            )
            grad_scores = (probs * (grad_probs - delta)).astype(jnp.bfloat16)
            value_sum[there, :] += jnp.dot(
                probs.astype(jnp.bfloat16), upper, preferred_element_type=jnp.float32
            )
            pair_sum[there, :] += jnp.dot(
                grad_scores, queries, preferred_element_type=jnp.float32
            )
            return total + jnp.dot(
                key_t[:, there], grad_scores, preferred_element_type=jnp.float32
            )

        total = lax.fori_loop(
            first_key[number], number + 1, turn, jnp.zeros((64, block), jnp.float32)
        )
        tall = jnp.concatenate([total * scale, jnp.zeros((64, block), jnp.float32)], 0)
        pair_sum[here, :] += jnp.transpose(tall)
        return carry

    lax.fori_loop(0, rows // block, attend, 0)

    def finish(number, carry):
        here = pl.ds(pl.multiple_of(number * block, block), block)
        pair = pair_sum[here, :]
        lane = lane_of((block, 128))
        cosine, sine = block_angles(number, pieces, fine, coarse)
        across = pair * sine
        turned = jnp.where(
            lane % 64 < 32, pltpu.roll(across, 96, 1), -pltpu.roll(across, 32, 1)
        )
        pair = pair * cosine + turned
        values = value_sum[here, :]
        keys_stay = core[0] == 0
        keep = jnp.where((lane < 64) | keys_stay, pair, values)
        send = jnp.where(lane < 64, 0.0, jnp.where(keys_stay, values, pair)).astype(jnp.bfloat16)
        for n, one in enumerate(storage(number)):
            keep_out[one, :] = keep[n * 64 : (n + 1) * 64, :]
            send_out[one, :] = send[n * 64 : (n + 1) * 64, :]
        return carry

    lax.fori_loop(0, rows // block, finish, 0)


def expert_rows(
    where, rows, grad, up_weight, down_weight,
    copy_out, result_out, activation_out, pair_out, pre_out,
):
    f32, bf16 = jnp.float32, jnp.bfloat16
    width = grad.shape[3]
    count = rows.shape[0]
    expert = where[0]
    extra = rows[:, width:].astype(f32)
    lane = lane_of((count, EXTRA))
    gate = jnp.sum(
        jnp.where((lane == expert) | (lane == expert + E), extra, 0.0), axis=1, keepdims=True
    )
    before = jnp.dot(rows[:, :width], up_weight[...], preferred_element_type=f32)
    gate_pre = before[:, :F]
    up_pre = before[:, F:]
    sigma = jax.nn.sigmoid(gate_pre)
    swish = gate_pre * sigma
    activation = (swish * up_pre).astype(bf16)
    activation_out[...] = activation
    result = jnp.dot(activation, down_weight[...], preferred_element_type=f32).astype(bf16)
    result = result.astype(f32)
    grads = grad[...].reshape(count, width).astype(f32)
    grad_gate = jnp.sum(grads * result, axis=1, keepdims=True)
    result_out[...] = (gate * result).astype(bf16)
    pair = (gate * grads).astype(bf16)
    pair_out[...] = pair
    grad_activation = lax.dot_general(
        pair, down_weight[...], (((1,), (1,)), ((), ())), preferred_element_type=f32
    )
    pre_out[:, :F] = (
        grad_activation * up_pre * sigma * (1.0 + gate_pre * (1.0 - sigma))
    ).astype(bf16)
    pre_out[:, F:] = (grad_activation * swish).astype(bf16)
    copy_out[:, :width] = lax.dot_general(
        pre_out[...], up_weight[...], (((1,), (1,)), ((), ())), preferred_element_type=f32
    ).astype(bf16)
    high = grad_gate.astype(bf16).astype(f32)
    copy_out[:, width:] = jnp.where(
        lane == expert, high, jnp.where(lane == expert + E, grad_gate - high, 0.0)
    ).astype(bf16)


def expert_call(half, where, rows, grads, up_weight, down_weight):
    count, full = rows.shape
    width = grads.shape[3]
    steps = 2
    block = count // steps
    bf16 = jnp.bfloat16
    row_spec = lambda columns: pl.BlockSpec((block, columns), lambda i, w: (i, 0))
    whole = lambda a: pl.BlockSpec(a.shape, lambda i, w: (0, 0), pipeline_mode=pl.Buffered(1))
    columns = (full, width, F, width, 2 * F)
    return pl.pallas_call(
        expert_rows,
        out_shape=[jax.ShapeDtypeStruct((count, n), bf16) for n in columns],
        grid_spec=pltpu.PrefetchScalarGridSpec(
            num_scalar_prefetch=1,
            grid=(steps,),
            in_specs=[
                row_spec(full),
                pl.BlockSpec((16 // steps, 1, MOST, width), lambda i, w: (i, half, 0, 0)),
                whole(up_weight),
                whole(down_weight),
            ],
            out_specs=[row_spec(n) for n in columns],
        ),
        compiler_params=pltpu.CompilerParams(vmem_limit_bytes=48 << 20),
    )(where, rows, grads, up_weight, down_weight)


def assemble(first, second, qkv_out, out_out, beside_out, gain_out):
    f32 = jnp.float32
    for pair in range(8):
        for source, rows, at in ((first, 400, 0), (second, 112, 400)):
            left = source[2 * pair, :rows, :].astype(f32)
            right = source[2 * pair + 1, :rows, :].astype(f32)
            here = slice(at, at + rows)
            qkv_out[here, pair * 128 : (pair + 1) * 128] = jnp.concatenate(
                [left[:, :64], right[:, :64]], 1
            )
            qkv_out[here, 1024 + pair * 64 : 1024 + (pair + 1) * 64] = left[:, 64:]
            qkv_out[here, 1536 + pair * 64 : 1536 + (pair + 1) * 64] = right[:, 64:]
    total = jnp.zeros((16, 128), f32)
    for device in range(16):
        bits = [(device >> n) & 1 for n in range(4)]
        at = bits[0] * 256 + bits[1] * 128 + bits[2] * 64 + bits[3] * 32
        for part in range(8):
            out_out[at : at + 32, part * 128 : (part + 1) * 128] = second[
                device, 112 + part * 32 : 144 + part * 32, :
            ].astype(f32)
        beside_out[at : at + 32, :] = second[device, 368:400, :].astype(f32)
        total = total + second[device, 400:416, :].astype(f32)
    gain_out[...] = total[:8, :] + total[8:, :]


def whole_call(kernel, scalars, outs, scratch, vmem):
    def run(*operands):
        spec = pl.BlockSpec(memory_space=pltpu.VMEM)
        return pl.pallas_call(
            kernel,
            out_shape=outs,
            grid_spec=pltpu.PrefetchScalarGridSpec(
                num_scalar_prefetch=scalars,
                grid=(),
                in_specs=[spec] * (len(operands) - scalars),
                out_specs=[spec] * len(outs),
                scratch_shapes=scratch,
            ),
            compiler_params=pltpu.CompilerParams(vmem_limit_bytes=vmem),
        )(*operands)

    return run


def fast_shards(
    hidden_in, block_order, segment_ids, cotangent, attn_gain, query_key_value_weight,
    w_out, ffn_gain, w_router, routes, expert_in, expert_out,
):
    bf16, f32 = jnp.bfloat16, jnp.float32
    rows = hidden_in.shape[1]
    width = hidden_in.shape[2]
    length = rows * 16
    capacity = length * TOPK * 9 // (8 * E)
    ia, ib, ic, idd, jf = (lax.axis_index(name) for name in EVERY)
    mine = ia * 8 + ib * 4 + ic * 2 + idd
    expert = jf * 16 + mine
    low_half = jf == 0

    inputs = hidden_in[0].astype(f32)
    scale_one = rms_scale(inputs)
    norm_one = inputs * scale_one
    gain_one_f = join(attn_gain, "f").astype(f32)
    h_one = (norm_one * gain_one_f).astype(bf16)

    (
        h_one, block_order, segment_ids, query_key_value_weight, w_out, ffn_gain, w_router,
        expert_in, expert_out,
    ) = together(
        h_one, block_order, segment_ids, query_key_value_weight, w_out, ffn_gain, w_router,
        expert_in, expert_out,
    )
    both = gather_step(spread(h_one), "a")

    def columns_of(start, number, low_first):
        pair = lax.dynamic_slice_in_dim(query_key_value_weight, start + number * 128, 128, 1)
        return jnp.where(low_first, pair[:, :64], pair[:, 64:])

    my_columns = jnp.concatenate(
        [
            columns_of(0, mine // 2, idd == 0),
            columns_of(1024, mine // 4, ic == 0),
            columns_of(1536, mine // 4, ic == 0),
            jnp.zeros((512, 64), bf16),
        ],
        1,
    )
    other_columns = swap(my_columns, "f")

    route = routes[0]
    named = jnp.any(route[:, :, None] == jnp.arange(E, dtype=jnp.int32)[None, None, :], axis=1)
    counts = spread(jnp.sum(named.astype(f32), axis=0, keepdims=True))
    named_b = named.astype(bf16)
    earlier = (jnp.arange(rows)[:, None] > jnp.arange(rows)[None, :]).astype(bf16)
    rank = jnp.dot(earlier, named_b, preferred_element_type=f32)
    row_of = jnp.where(named, rank, -1.0)
    counts = gather_step(counts, "a")
    expert_weights = jnp.concatenate([expert_in, expert_out], 1)
    both, row_of, cotangent, counts, expert_weights = together(
        both, row_of, cotangent, counts, expert_weights
    )
    low = gather_step(both[..., :512], "b")
    high = gather_step(both[..., 512:], "c")
    other_row_of = swap(row_of, "a")
    other_cotangent = swap(cotangent[0], "a")
    counts = gather_step(counts, "c")

    def picks(rows_of):
        half = rows_of.reshape(rows, 2, 2, 8)
        half = jnp.where(ia == 0, half[:, :, 0], half[:, :, 1])
        half = half.transpose(2, 1, 0).reshape(16, 1, rows)
        return (half == jnp.arange(MOST, dtype=f32)[None, :, None]).astype(bf16)

    def build_rows(choice, tokens):
        return lax.dot_general(
            choice, tokens, (((2,), (0,)), ((), ())), preferred_element_type=f32
        ).astype(bf16)

    def exchange(sent):
        return lax.all_to_all(sent, HALF, split_axis=0, concat_axis=0, tiled=True)

    low, high, other_columns, counts = together(low, high, other_columns, counts)
    low = gather_step(low, "c")
    high = gather_step(high, "b")
    counts = gather_step(counts, "b")
    out_part = share_swap(w_out)
    other_gain_two = swap(ffn_gain, "f")
    other_router = swap(w_router, "f")
    low, high, other_cotangent, other_row_of, counts, expert_weights, out_part = together(
        low, high, other_cotangent, other_row_of, counts, expert_weights, out_part
    )
    low_own = low.reshape(length // 2, 512)
    high_own = high.reshape(length // 2, 512)
    low_next = swap(low_own, "d")
    high_next = swap(high_own, "d")
    expert_weights = lax.all_to_all(
        expert_weights, CTX, split_axis=0, concat_axis=0, tiled=True
    )
    counts = gather_step(counts, "d")
    head_weight = in_order(my_columns, other_columns, "f", 0)

    order = block_order[0]
    blocks = order.shape[0]
    place = jnp.sum(
        jnp.where(order[None, :] == jnp.arange(blocks, dtype=jnp.int32)[:, None],
                  jnp.arange(blocks, dtype=jnp.int32)[None, :], 0),
        axis=1,
    )
    document = segment_ids[0]
    start = jnp.sum((document[:, None] < document[None, :]).astype(jnp.int32), axis=0)
    first_key = start[::QUERY_BLOCK] // QUERY_BLOCK
    start = start[None, :]
    steps = jnp.arange(HEAD_SIZE // 2, dtype=f32)
    frequency = jnp.power(THETA, -2.0 * steps / HEAD_SIZE)
    angle_a = (jnp.arange(length // 64, dtype=f32) * 64.0)[:, None] * frequency[None, :]
    angle_b = jnp.arange(64, dtype=f32)[:, None] * frequency[None, :]
    coarse = jnp.tile(jnp.stack([jnp.cos(angle_a), jnp.sin(angle_a)]), (1, 1, 4))
    fine = jnp.tile(jnp.stack([jnp.cos(angle_b), jnp.sin(angle_b)]), (1, 1, 4))
    storage = jnp.arange(blocks, dtype=jnp.int32)
    held = (((storage // 2) % 2) ^ idd) * (blocks // 2) + (storage // 4) * 2 + storage % 2
    h_place = jnp.sum(jnp.where(place[:, None] == storage[None, :], held[None, :], 0), axis=1)
    storage = jnp.arange(blocks, dtype=jnp.int32)
    held = (((storage // 2) % 2) ^ idd) * (blocks // 2) + (storage // 4) * 2 + storage % 2
    h_place = jnp.sum(jnp.where(place[:, None] == storage[None, :], held[None, :], 0), axis=1)
    head_weight, out_part, other_gain_two, other_router, query_key_value_weight = together(
        head_weight, out_part, other_gain_two, other_router, query_key_value_weight
    )
    weight_part = share_swap(query_key_value_weight)
    query, key, value, mixed, attended_head = whole_call(
        attention_forward,
        3,
        [
            jax.ShapeDtypeStruct((length, 128), bf16),
            jax.ShapeDtypeStruct((length, 128), bf16),
            jax.ShapeDtypeStruct((length, 128), bf16),
            jax.ShapeDtypeStruct((72, length), f32),
            jax.ShapeDtypeStruct((length, 64), bf16),
        ],
        [pltpu.VMEM((128, length), bf16)],
        32 << 20,
    )(
        place, h_place, first_key, low_own, high_own, low_next, high_next, head_weight, fine,
        coarse, start,
    )

    def to_tokens(value_heads):
        return lax.all_to_all(
            value_heads.reshape(16, rows, -1), CTX, split_axis=0, concat_axis=0, tiled=True
        )

    pick_mine = picks(row_of)
    pick_other = picks(other_row_of)
    grad_rows = jnp.concatenate(
        [build_rows(pick_mine, cotangent[0]), build_rows(pick_other, other_cotangent)], 1
    )
    out_full = share_join(w_out, out_part)
    gain_two_f = in_order(ffn_gain, other_gain_two, "f", 0).astype(f32)
    router_full = in_order(w_router, other_router, "f", 0)
    attended_head, expert_weights, grad_rows, out_full, weight_part, counts = together(
        attended_head, expert_weights, grad_rows, out_full, weight_part, counts
    )
    attended = to_tokens(attended_head)
    weight_full = share_join(query_key_value_weight, weight_part)
    attended, grad_rows = together(attended, grad_rows)
    grad_rows = exchange(grad_rows)
    attended = attended.transpose(1, 0, 2).reshape(rows, 1024)
    middle_state = inputs + jnp.dot(attended, out_full, preferred_element_type=f32)
    scale_two = rms_scale(middle_state)
    norm_two = middle_state * scale_two
    h_two = (norm_two * gain_two_f).astype(bf16)
    logits = jnp.dot(h_two, router_full, preferred_element_type=f32)
    top = jnp.max(jnp.where(named, logits, MASK_FILL_VALUE), axis=-1, keepdims=True)
    weights = jnp.where(named, jnp.exp(logits - top), 0.0)
    gates = weights / jnp.sum(weights, axis=-1, keepdims=True)
    passed = (jnp.arange(16)[:, None] < mine).astype(f32)
    offset = jnp.sum(counts.reshape(16, E) * passed, axis=0, keepdims=True)
    kept = (named & (rank + offset < capacity)).astype(f32)
    extended = jnp.concatenate(
        [h_two] + two_parts(gates * kept) + [jnp.zeros((rows, 2 * E), bf16)], 1
    )
    other_extended = swap(extended, "a")
    rows_mine = build_rows(pick_mine, extended)
    rows_mine, grad_rows, weight_full, other_extended = together(
        rows_mine, grad_rows, weight_full, other_extended
    )
    rows_mine = exchange(rows_mine)
    up_weight = expert_weights[:, :64].reshape(width, 2 * F)
    down_weight = expert_weights[:, 64:].reshape(F, width)
    grad_rows = grad_rows.reshape(16, 2, MOST, width)
    rows_other = build_rows(pick_other, other_extended)
    rows_mine, rows_other, up_weight, down_weight = together(
        rows_mine, rows_other, up_weight, down_weight
    )
    rows_other = exchange(rows_other)
    rows_mine = rows_mine.reshape(16 * MOST, width + EXTRA)
    number = expert.astype(jnp.int32)[None]
    copy_mine, result_mine, act_mine, pair_mine, pre_mine = expert_call(
        0, number, rows_mine, grad_rows, up_weight, down_weight
    )
    rows_other, copy_mine = together(rows_other, copy_mine)
    rows_other = rows_other.reshape(16 * MOST, width + EXTRA)
    copy_other, result_other, act_other, pair_other, pre_other = expert_call(
        1, number, rows_other, grad_rows, up_weight, down_weight
    )

    def sum_rows(choice, got):
        return lax.dot_general(
            choice, got, (((0, 1), (0, 1)), ((), ())), preferred_element_type=f32
        )

    away = exchange(copy_other.reshape(16, MOST, width + EXTRA))
    away, copy_mine = together(away, copy_mine)
    home = exchange(copy_mine.reshape(16, MOST, width + EXTRA))
    grad_up_weight = contract_rows(rows_mine[:, :width], pre_mine) + contract_rows(
        rows_other[:, :width], pre_other
    )
    grad_down = contract_rows(act_mine, pair_mine) + contract_rows(act_other, pair_other)
    expert_grads = jnp.concatenate(
        [
            grad_up_weight.astype(bf16).reshape(16, 64, 2 * F),
            grad_down.astype(bf16).reshape(16, 32, width),
        ],
        1,
    )
    away_sum = swap(sum_rows(pick_other, away).astype(bf16), "a")
    home, away_sum, expert_grads = together(home, away_sum, expert_grads)
    back = sum_rows(pick_mine, home) + away_sum.astype(f32)

    gate_grads = (back[:, width : width + E] + back[:, width + E : width + 2 * E]) * kept
    grad_logits = gates * (gate_grads - jnp.sum(gates * gate_grads, axis=-1, keepdims=True))
    grad_h_two = back[:, :width] + lax.dot_general(
        grad_logits, router_full.astype(f32), (((1,), (1,)), ((), ())), precision=HIGHEST
    )
    grad_out = cotangent[0].astype(f32)
    scaled_two = grad_h_two * gain_two_f
    grad_mid = grad_out + scale_two * (
        scaled_two - norm_two * jnp.mean(scaled_two * norm_two, axis=-1, keepdims=True)
    )
    grad_branch = grad_mid.astype(bf16)
    attended_gradient = contract_columns(grad_branch, out_full).astype(bf16)
    grad_heads = to_tokens(attended_gradient.reshape(rows, 16, 64).transpose(1, 0, 2))
    grad_heads = grad_heads.reshape(length, 64)

    grad_router_part = lax.dot_general(
        h_two.astype(f32), grad_logits, (((0,), (0,)), ((), ())), precision=HIGHEST
    )
    grad_gain_two = jnp.sum(grad_h_two * norm_two, axis=0)
    beside = jnp.concatenate(
        [grad_router_part, grad_gain_two[:, None], jnp.zeros((width, 128 - E - 1), f32)], 1
    ).reshape(2, 2, 256, 128)
    by_core = attended.reshape(rows, 2, 2, 256)

    def rows_at(core):
        columns = lax.dynamic_slice_in_dim(by_core, core, 1, 2).reshape(rows, 512)
        others = lax.dynamic_slice_in_dim(beside, core, 1, 1).reshape(512, 128)
        return jnp.concatenate([contract_rows(columns, grad_branch), others], 1)

    out_sum = rows_at(idd)
    leaving = rows_at(1 - idd).astype(bf16)

    def halve(total, axis):
        count = total.shape[0] // 2
        index = lax.axis_index(axis)
        keep = lax.dynamic_slice_in_dim(total, index * count, count, 0)
        send = lax.dynamic_slice_in_dim(total, (1 - index) * count, count, 0)
        return keep + swap(send.astype(bf16), axis).astype(f32)

    results = jnp.concatenate(
        [result_mine.reshape(16, MOST, width), result_other.reshape(16, MOST, width)], 1
    )
    grad_heads, results = together(grad_heads, results)
    results = exchange(results)

    keep, send = whole_call(
        attention_backward,
        3,
        [jax.ShapeDtypeStruct((length, 128), f32), jax.ShapeDtypeStruct((length, 128), bf16)],
        [
            pltpu.VMEM((64, length), bf16),
            pltpu.VMEM((length, 128), f32),
            pltpu.VMEM((length, 128), f32),
        ],
        32 << 20,
    )(
        place, first_key, idd.astype(jnp.int32)[None], query, key, value, mixed, grad_heads,
        fine, coarse, start,
    )
    keep, send, out_sum, leaving = together(keep, send, out_sum, leaving)
    out_sum = out_sum + swap(leaving, "d").astype(f32)
    grad_columns = (keep + swap(send, "d").astype(f32)).astype(bf16)
    out_sum = halve(out_sum, "f")
    results, expert_grads = together(results, expert_grads)
    expert_grads = lax.all_to_all(expert_grads, CTX, split_axis=0, concat_axis=0, tiled=True)
    for axis in ("c", "b", "a"):
        out_sum = halve(out_sum, axis)
    out_rows = out_sum.reshape(32, 9, 128).transpose(1, 0, 2).reshape(288, 128).astype(bf16)

    by_core = grad_columns.reshape(8, 2, rows, 128)
    own = jnp.where(idd == 0, by_core[:, 0], by_core[:, 1]).reshape(length // 2, 128)
    following = jnp.where(idd == 0, by_core[:, 1], by_core[:, 0]).reshape(length // 2, 128)
    low_part = contract_rows(low_own, own) + contract_rows(low_next, following)
    high_part = contract_rows(high_own, own) + contract_rows(high_next, following)
    columns_grad = jnp.where(low_half, low_part, high_part) + swap(
        jnp.where(low_half, high_part, low_part), "f"
    )
    my_weight = jnp.concatenate(
        [my_columns[:, :64], jnp.where(idd == 0, my_columns[:, 64:128], my_columns[:, 128:192])], 1
    )
    gain_part = jnp.sum(columns_grad * my_weight.astype(f32), axis=1).reshape(4, 128)
    gain_part = jnp.concatenate([gain_part, jnp.zeros((4, 128), f32)], 0)
    columns_grad = jnp.concatenate(
        [columns_grad.astype(bf16), out_rows] + two_parts(gain_part), 0
    )
    gathered = gather_step(spread(columns_grad), "a")
    first = gather_step(gathered[..., :400, :], "b")
    second = gather_step(gathered[..., 400:, :], "c")
    first = gather_step(first, "c")
    second = gather_step(second, "b")
    ready, expert_grads = together(grad_columns, expert_grads)
    grad_projected = to_tokens(ready)
    grad_expert_in = expert_grads[:, :64].astype(f32)
    grad_expert_out = expert_grads[:, 64:].astype(f32)
    first, second, grad_projected = together(first, second, grad_projected)
    first = gather_step(first, "d")
    second = gather_step(second, "d")

    grad_projected = grad_projected.transpose(1, 0, 2)
    grad_kv = grad_projected[:, :, 64:].reshape(rows, 8, 2, 64)
    grad_projected = jnp.concatenate(
        [
            grad_projected[:, :, :64].reshape(rows, 1024),
            grad_kv[:, :, 0].reshape(rows, 512),
            grad_kv[:, :, 1].reshape(rows, 512),
        ],
        1,
    )
    grad_h_one = contract_columns(grad_projected, weight_full)
    scaled_one = grad_h_one * gain_one_f
    grad_inputs = grad_mid + scale_one * (
        scaled_one - norm_one * jnp.mean(scaled_one * norm_one, axis=-1, keepdims=True)
    )
    share_qkv, share_out, beside, gain_sum = whole_call(
        assemble,
        0,
        [
            jax.ShapeDtypeStruct((512, 2048), f32),
            jax.ShapeDtypeStruct((512, 1024), f32),
            jax.ShapeDtypeStruct((512, 128), f32),
            jax.ShapeDtypeStruct((8, 128), f32),
        ],
        [],
        32 << 20,
    )(first.reshape(16, 400, 128), second.reshape(16, 416, 128))
    share_router = beside[:, :E]
    share_two = beside[:, E]
    share_one = gain_sum[:4].reshape(512) / attn_gain.astype(f32)
    mixture = sum_rows(pick_mine, results[:, :MOST]) + swap(
        sum_rows(pick_other, results[:, MOST:]).astype(bf16), "a"
    ).astype(f32)
    hidden_out = (middle_state + mixture).astype(bf16)
    return (
        hidden_out[None],
        grad_inputs[None],
        share_one,
        share_qkv,
        share_out,
        share_two,
        share_router,
        grad_expert_in,
        grad_expert_out,
    )


def fast_solution(mesh):
    fine = Mesh(mesh.devices.reshape(2, 2, 2, 2, 2), EVERY)
    placed = (
        P("f", CTX, None),
        P("f", None),
        P("f", None),
        P("f", CTX, None),
        P("f"),
        P("f", None),
        P("f", None),
        P("f"),
        P("f", None),
        P("f", CTX, None),
        P("f", CTX, None),
        P("f", CTX, None),
    )
    return jax.shard_map(
        fast_shards,
        mesh=fine,
        in_specs=placed,
        out_specs=(
            P("f", CTX, None),
            P("f", CTX, None),
            P("f"),
            P("f", None),
            P("f", None),
            P("f"),
            P("f", None),
            P("f", CTX, None),
            P("f", CTX, None),
        ),
        check_vma=False,
    )


def solution(mesh):
    if mesh.shape["ctx"] == QUERY_HEADS and mesh.shape["fsdp"] * mesh.shape["ctx"] == E:
        return fast_solution(mesh)
    return general_solution(mesh)
```

```python
import math

import jax
import jax.numpy as jnp
from jax import lax
from jax.experimental import pallas as pl
from jax.experimental.pallas import tpu as pltpu
from jax.sharding import Mesh
from jax.sharding import PartitionSpec as P

QUERY_HEADS = 16
KEY_VALUE_HEADS = 8
HEAD_SIZE = 64
E = 32
TOPK = 8
F = 512
MOST = 48


EPSILON = 1e-06
THETA = 10000.0
MASK_FILL_VALUE = -1e30
HIGHEST = lax.Precision.HIGHEST


def carried_in(value, axis, combine, identity):
    length, mine = (lax.axis_size(axis), lax.axis_index(axis))
    everything = lax.all_gather(value, axis)
    start = jnp.broadcast_to(jnp.asarray(identity, value.dtype), value.shape)

    def turn(k, before):
        reached = k < mine
        new = combine(before, everything[k])
        return jnp.where(reached, new, before)

    return lax.fori_loop(0, length, turn, start)


def rms_scale(value_rows):
    return lax.rsqrt(jnp.mean(value_rows * value_rows, axis=-1, keepdims=True) + EPSILON)


def rotate(value_rows):
    middle = value_rows.shape[-1] // 2
    return jnp.concatenate([-value_rows[..., middle:], value_rows[..., :middle]], axis=-1)


def rotate_back(value_rows):
    middle = value_rows.shape[-1] // 2
    return jnp.concatenate([value_rows[..., middle:], -value_rows[..., :middle]], axis=-1)


def rope_tables(position):
    steps = jnp.arange(HEAD_SIZE // 2, dtype=jnp.float32)
    frequency = jnp.power(THETA, -2.0 * steps / HEAD_SIZE)
    angle = position.astype(jnp.float32)[:, None] * frequency[None, :]
    angle = jnp.concatenate([angle, angle], axis=-1)
    return (jnp.cos(angle), jnp.sin(angle))


def contract_rows(left, right):
    return lax.dot_general(
        left, right, (((0,), (0,)), ((), ())), preferred_element_type=jnp.float32
    )


def contract_columns(left, right):
    return lax.dot_general(
        left, right, (((1,), (1,)), ((), ())), preferred_element_type=jnp.float32
    )


def own_rows(total, rank, count):
    share = total.shape[0] // count
    return lax.dynamic_slice_in_dim(total, rank * share, share, 0)


def general_shards(
    hidden_in,
    block_order,
    segment_ids,
    cotangent,
    attn_gain,
    query_key_value_weight,
    w_out,
    ffn_gain,
    w_router,
    routes,
    expert_in,
    expert_out,
):
    count_of_rows = hidden_in.shape[1]
    width = hidden_in.shape[2]
    ctx_count = lax.axis_size("ctx")
    fsdp_count = lax.axis_size("fsdp")
    sequence_length = count_of_rows * ctx_count
    half_block = count_of_rows // 2
    capacity = sequence_length * TOPK * 9 // (8 * E)
    query_total_width = QUERY_HEADS * HEAD_SIZE
    key_total_width = KEY_VALUE_HEADS * HEAD_SIZE
    query_group = QUERY_HEADS // KEY_VALUE_HEADS
    scale = 1.0 / math.sqrt(HEAD_SIZE)
    key_block_rows = min(1024, sequence_length)
    block_count = sequence_length // key_block_rows
    pair_count = count_of_rows * TOPK
    gain_one, qkv_full, out_full, gain_two, router_full = (
        lax.all_gather(attn_gain, "fsdp", axis=0, tiled=True),
        lax.all_gather(query_key_value_weight, "fsdp", axis=0, tiled=True),
        lax.all_gather(w_out, "fsdp", axis=0, tiled=True),
        lax.all_gather(ffn_gain, "fsdp", axis=0, tiled=True),
        lax.all_gather(w_router, "fsdp", axis=0, tiled=True),
    )
    up_full, down_full = (
        lax.all_gather(expert_in, "ctx", axis=1, tiled=True),
        lax.all_gather(expert_out, "ctx", axis=1, tiled=True),
    )
    key_position = (
        block_order[0][:, None] * half_block + jnp.arange(half_block, dtype=jnp.int32)[None, :]
    ).reshape(-1)
    key_document = segment_ids[0][key_position]
    first_row = lax.axis_index("ctx") * count_of_rows
    query_position = lax.dynamic_slice_in_dim(key_position, first_row, count_of_rows, 0)
    query_document = lax.dynamic_slice_in_dim(key_document, first_row, count_of_rows, 0)
    inputs = hidden_in[0].astype(jnp.float32)
    grad_out = cotangent[0].astype(jnp.float32)
    scale_one = rms_scale(inputs)
    norm_one = inputs * scale_one
    gain_one_f = gain_one.astype(jnp.float32)
    h_one = (norm_one * gain_one_f).astype(jnp.bfloat16)
    projected_rows = jnp.dot(h_one, qkv_full, preferred_element_type=jnp.float32)
    cosine, sine = rope_tables(query_position)
    query_raw = projected_rows[:, :query_total_width].reshape(count_of_rows, QUERY_HEADS, HEAD_SIZE)
    unrotated_key = projected_rows[
        :, query_total_width : query_total_width + key_total_width
    ].reshape(count_of_rows, KEY_VALUE_HEADS, HEAD_SIZE)
    query_matrix = (query_raw * cosine[:, None, :] + rotate(query_raw) * sine[:, None, :]).astype(
        jnp.bfloat16
    )
    key_rows = (
        unrotated_key * cosine[:, None, :] + rotate(unrotated_key) * sine[:, None, :]
    ).astype(jnp.bfloat16)
    value_rows = projected_rows[:, query_total_width + key_total_width :].astype(jnp.bfloat16)
    key_value_local = jnp.concatenate(
        [key_rows.reshape(count_of_rows, key_total_width), value_rows], axis=1
    )
    key_value_all = lax.all_gather(key_value_local, "ctx", axis=0, tiled=True)
    grouped_queries = query_matrix.reshape(count_of_rows, KEY_VALUE_HEADS, query_group, HEAD_SIZE)
    block_number = jnp.arange(block_count, dtype=jnp.int32)

    def block_keys(source, index):
        current_rows = lax.dynamic_slice_in_dim(source, index * key_block_rows, key_block_rows, 0)
        block_key_rows = current_rows[:, :key_total_width].reshape(
            key_block_rows, KEY_VALUE_HEADS, HEAD_SIZE
        )
        block_value_rows = current_rows[:, key_total_width:].reshape(
            key_block_rows, KEY_VALUE_HEADS, HEAD_SIZE
        )
        block_position = lax.dynamic_slice_in_dim(
            key_position, index * key_block_rows, key_block_rows, 0
        )
        block_document = lax.dynamic_slice_in_dim(
            key_document, index * key_block_rows, key_block_rows, 0
        )
        allowed = (query_document[:, None] == block_document[None, :]) & (
            block_position[None, :] <= query_position[:, None]
        )
        return (block_key_rows, block_value_rows, allowed)

    def scores_of(block_key_rows, allowed):
        scores = (
            jnp.einsum(
                "qhgd,khd->hgqk",
                grouped_queries,
                block_key_rows,
                preferred_element_type=jnp.float32,
            )
            * scale
        )
        return jnp.where(allowed[None, None], scores, MASK_FILL_VALUE)

    def max_sum(carry, index):
        top, total = carry
        block_key_rows, block_value_rows, allowed = block_keys(key_value_all, index)
        scores = scores_of(block_key_rows, allowed)
        new_top = jnp.maximum(top, jnp.max(scores, axis=-1))
        weights = jnp.where(allowed[None, None], jnp.exp(scores - new_top[..., None]), 0.0)
        total = total * jnp.exp(top - new_top) + jnp.sum(weights, axis=-1)
        return ((new_top, total), None)

    upper_start = jnp.full(
        (KEY_VALUE_HEADS, query_group, count_of_rows), MASK_FILL_VALUE, jnp.float32
    )
    overall_start = jnp.zeros((KEY_VALUE_HEADS, query_group, count_of_rows), jnp.float32)
    (top, total), unused = lax.scan(max_sum, (upper_start, overall_start), block_number)
    log_total = top + jnp.log(total)

    def weighted_values(accum, index):
        block_key_rows, block_value_rows, allowed = block_keys(key_value_all, index)
        scores = scores_of(block_key_rows, allowed)
        probs = jnp.where(allowed[None, None], jnp.exp(scores - log_total[..., None]), 0.0).astype(
            jnp.bfloat16
        )
        return (
            accum
            + jnp.einsum(
                "hgqk,khd->qhgd", probs, block_value_rows, preferred_element_type=jnp.float32
            ),
            None,
        )

    attended_f, unused = lax.scan(
        weighted_values,
        jnp.zeros((count_of_rows, KEY_VALUE_HEADS, query_group, HEAD_SIZE), jnp.float32),
        block_number,
    )
    attended = attended_f.reshape(count_of_rows, query_total_width).astype(jnp.bfloat16)
    middle_state = inputs + jnp.dot(attended, out_full, preferred_element_type=jnp.float32)
    scale_two = rms_scale(middle_state)
    norm_two = middle_state * scale_two
    gain_two_f = gain_two.astype(jnp.float32)
    h_two = (norm_two * gain_two_f).astype(jnp.bfloat16)
    logits = jnp.dot(h_two, router_full, preferred_element_type=jnp.float32)
    route = routes[0]
    gates = jax.nn.softmax(jnp.take_along_axis(logits, route, axis=1), axis=-1)
    flat = route.reshape(-1)
    onehot = (flat[:, None] == jnp.arange(E, dtype=jnp.int32)[None, :]).astype(jnp.int32)
    rank = jnp.sum((jnp.cumsum(onehot, axis=0) - onehot) * onehot, axis=1)
    counts = jnp.sum(onehot, axis=0)

    def add_counts(earlier, later):
        return earlier + later

    offsets = carried_in(counts, "ctx", add_counts, jnp.zeros((E,), jnp.int32))
    slot = jnp.sum(onehot * offsets[None, :], axis=1) + rank
    kept = slot < capacity
    target = jnp.where(kept, flat * MOST + rank, E * MOST)
    safe_target = jnp.minimum(target, E * MOST - 1)
    keep_float = kept.astype(jnp.float32)[:, None]
    token = jnp.arange(pair_count, dtype=jnp.int32) // TOPK
    send_rows = (
        jnp.zeros((E * MOST, width), jnp.bfloat16)
        .at[target]
        .set(h_two[token], mode="drop")
        .reshape(E, MOST, width)
    )
    received = lax.all_to_all(send_rows, "fsdp", split_axis=0, concat_axis=1, tiled=True)
    before = jnp.einsum("erd,edf->erf", received, up_full, preferred_element_type=jnp.float32)
    gate_pre = before[..., :F]
    up_pre = before[..., F:]
    sigma = jax.nn.sigmoid(gate_pre)
    activation = (gate_pre * sigma * up_pre).astype(jnp.bfloat16)
    expert_result = jnp.einsum(
        "erf,efd->erd", activation, down_full, preferred_element_type=jnp.float32
    ).astype(jnp.bfloat16)
    returned = lax.all_to_all(
        expert_result, "fsdp", split_axis=1, concat_axis=0, tiled=True
    ).reshape(E * MOST, width)
    pair_result = (returned[safe_target].astype(jnp.float32) * keep_float).reshape(
        count_of_rows, TOPK, width
    )
    mixture = jnp.sum(gates[..., None] * pair_result, axis=1)
    hidden_out = (middle_state + mixture).astype(jnp.bfloat16)
    grad_pair = (
        (gates[..., None] * grad_out[:, None, :]).reshape(pair_count, width) * keep_float
    ).astype(jnp.bfloat16)
    grad_gates = jnp.sum(grad_out[:, None, :] * pair_result, axis=-1)
    grad_chosen = gates * (grad_gates - jnp.sum(gates * grad_gates, axis=-1, keepdims=True))
    chosen_table = (route[..., None] == jnp.arange(E, dtype=jnp.int32)[None, None, :]).astype(
        jnp.float32
    )
    grad_logits = jnp.sum(grad_chosen[..., None] * chosen_table, axis=1)
    grad_router_part = lax.dot_general(
        h_two.astype(jnp.float32), grad_logits, (((0,), (0,)), ((), ())), precision=HIGHEST
    )
    grad_h_two = lax.dot_general(
        grad_logits, router_full.astype(jnp.float32), (((1,), (1,)), ((), ())), precision=HIGHEST
    )
    send_grads = (
        jnp.zeros((E * MOST, width), jnp.bfloat16)
        .at[target]
        .set(grad_pair, mode="drop")
        .reshape(E, MOST, width)
    )
    grad_received = lax.all_to_all(send_grads, "fsdp", split_axis=0, concat_axis=1, tiled=True)
    grad_activation = jnp.einsum(
        "erd,efd->erf", grad_received, down_full, preferred_element_type=jnp.float32
    )
    grad_down = jnp.einsum(
        "erf,erd->efd", activation, grad_received, preferred_element_type=jnp.float32
    )
    grad_gate = grad_activation * up_pre * sigma * (1.0 + gate_pre * (1.0 - sigma))
    grad_up = grad_activation * gate_pre * sigma
    grad_pre = jnp.concatenate([grad_gate, grad_up], axis=-1).astype(jnp.bfloat16)
    grad_up_weight = jnp.einsum(
        "erd,erf->edf", received, grad_pre, preferred_element_type=jnp.float32
    )
    grad_copy = jnp.einsum(
        "erf,edf->erd", grad_pre, up_full, preferred_element_type=jnp.float32
    ).astype(jnp.bfloat16)
    grad_returned = lax.all_to_all(
        grad_copy, "fsdp", split_axis=1, concat_axis=0, tiled=True
    ).reshape(E * MOST, width)
    grad_h_two = grad_h_two + jnp.sum(
        (grad_returned[safe_target].astype(jnp.float32) * keep_float).reshape(
            count_of_rows, TOPK, width
        ),
        axis=1,
    )
    grad_expert_in, grad_expert_out = (
        lax.psum_scatter(
            grad_up_weight.astype(jnp.bfloat16), "ctx", scatter_dimension=1, tiled=True
        ).astype(jnp.float32),
        lax.psum_scatter(
            grad_down.astype(jnp.bfloat16), "ctx", scatter_dimension=1, tiled=True
        ).astype(jnp.float32),
    )
    grad_gain_two = jnp.sum(grad_h_two * norm_two, axis=0)
    scaled_two = grad_h_two * gain_two_f
    grad_mid = grad_out + scale_two * (
        scaled_two - norm_two * jnp.mean(scaled_two * norm_two, axis=-1, keepdims=True)
    )
    grad_branch = grad_mid.astype(jnp.bfloat16)
    grad_out_weight = contract_rows(attended, grad_branch)
    attended_gradient = contract_columns(grad_branch, out_full).astype(jnp.bfloat16)
    grouped_gradient = attended_gradient.reshape(
        count_of_rows, KEY_VALUE_HEADS, query_group, HEAD_SIZE
    )
    delta = jnp.transpose(
        jnp.sum(grouped_gradient.astype(jnp.float32) * attended_f, axis=-1), (1, 2, 0)
    )

    def block_gradients(query_accum, index):
        block_key_rows, block_value_rows, allowed = block_keys(key_value_all, index)
        scores = scores_of(block_key_rows, allowed)
        probs = jnp.where(allowed[None, None], jnp.exp(scores - log_total[..., None]), 0.0)
        grad_probs = jnp.einsum(
            "qhgd,khd->hgqk", grouped_gradient, block_value_rows, preferred_element_type=jnp.float32
        )
        grad_scores = (probs * (grad_probs - delta[..., None])).astype(jnp.bfloat16)
        query_accum = query_accum + jnp.einsum(
            "hgqk,khd->qhgd", grad_scores, block_key_rows, preferred_element_type=jnp.float32
        )
        grad_keys = (
            jnp.einsum(
                "hgqk,qhgd->khd", grad_scores, grouped_queries, preferred_element_type=jnp.float32
            )
            * scale
        )
        grad_values = jnp.einsum(
            "hgqk,qhgd->khd",
            probs.astype(jnp.bfloat16),
            grouped_gradient,
            preferred_element_type=jnp.float32,
        )
        joined = jnp.concatenate(
            [
                grad_keys.reshape(key_block_rows, key_total_width),
                grad_values.reshape(key_block_rows, key_total_width),
            ],
            axis=1,
        )
        return (query_accum, joined)

    grad_queries, grad_blocks = lax.scan(
        block_gradients,
        jnp.zeros((count_of_rows, KEY_VALUE_HEADS, query_group, HEAD_SIZE), jnp.float32),
        block_number,
    )
    key_value_gradient = lax.psum_scatter(
        grad_blocks.reshape(sequence_length, 2 * key_total_width).astype(jnp.bfloat16),
        "ctx",
        scatter_dimension=0,
        tiled=True,
    ).astype(jnp.float32)
    grad_queries = (grad_queries * scale).reshape(count_of_rows, QUERY_HEADS, HEAD_SIZE)
    local_key_gradient = key_value_gradient[:, :key_total_width].reshape(
        count_of_rows, KEY_VALUE_HEADS, HEAD_SIZE
    )
    grad_values_mine = key_value_gradient[:, key_total_width:]
    grad_query_pre = grad_queries * cosine[:, None, :] + rotate_back(
        grad_queries * sine[:, None, :]
    )
    grad_key_pre = local_key_gradient * cosine[:, None, :] + rotate_back(
        local_key_gradient * sine[:, None, :]
    )
    grad_projected = jnp.concatenate(
        [
            grad_query_pre.reshape(count_of_rows, query_total_width),
            grad_key_pre.reshape(count_of_rows, key_total_width),
            grad_values_mine,
        ],
        axis=1,
    ).astype(jnp.bfloat16)
    grad_qkv_weight = contract_rows(h_one, grad_projected)
    grad_h_one = contract_columns(grad_projected, qkv_full)
    grad_gain_one = jnp.sum(grad_h_one * norm_one, axis=0)
    scaled_one = grad_h_one * gain_one_f
    grad_inputs = grad_mid + scale_one * (
        scaled_one - norm_one * jnp.mean(scaled_one * norm_one, axis=-1, keepdims=True)
    )
    total_one, total_qkv, total_out, total_two, total_router = lax.psum(
        (grad_gain_one, grad_qkv_weight, grad_out_weight, grad_gain_two, grad_router_part),
        ("ctx", "fsdp"),
    )
    fsdp_rank = lax.axis_index("fsdp")
    share_one = own_rows(total_one, fsdp_rank, fsdp_count)
    share_qkv = own_rows(total_qkv, fsdp_rank, fsdp_count)
    share_out = own_rows(total_out, fsdp_rank, fsdp_count)
    share_two = own_rows(total_two, fsdp_rank, fsdp_count)
    share_router = own_rows(total_router, fsdp_rank, fsdp_count)
    return (
        hidden_out[None],
        grad_inputs[None],
        share_one,
        share_qkv,
        share_out,
        share_two,
        share_router,
        grad_expert_in,
        grad_expert_out,
    )


def general_solution(mesh):
    placed = (
        P("fsdp", "ctx", None),
        P("fsdp", None),
        P("fsdp", None),
        P("fsdp", "ctx", None),
        P("fsdp"),
        P("fsdp", None),
        P("fsdp", None),
        P("fsdp"),
        P("fsdp", None),
        P("fsdp", "ctx", None),
        P("fsdp", "ctx", None),
        P("fsdp", "ctx", None),
    )
    return jax.shard_map(
        general_shards,
        mesh=mesh,
        in_specs=placed,
        out_specs=(
            P("fsdp", "ctx", None),
            P("fsdp", "ctx", None),
            P("fsdp"),
            P("fsdp", None),
            P("fsdp", None),
            P("fsdp"),
            P("fsdp", None),
            P("fsdp", "ctx", None),
            P("fsdp", "ctx", None),
        ),
        check_vma=False,
    )


CTX = ("a", "b", "c", "d")
HALF = ("b", "c", "d", "f")
EVERY = ("a", "b", "c", "d", "f")
QUERY_BLOCK = 256
EXTRA = 128


def swap(value, axis):
    return lax.ppermute(value, axis, [(0, 1), (1, 0)])


def in_order(mine, other, axis, dim):
    first = lax.axis_index(axis) == 0
    return jnp.where(
        first, jnp.concatenate([mine, other], dim), jnp.concatenate([other, mine], dim)
    )


def join(value, axis, dim=0):
    return in_order(value, swap(value, axis), axis, dim)


def spread(value):
    return value[(None,) * 4]


def gather_step(held, axis):
    return in_order(held, swap(held, axis), axis, CTX.index(axis))


def share_swap(value):
    half = value.shape[0] // 2
    part = swap(jnp.where(lax.axis_index("d") == 0, value[:half], value[half:]), "f")
    return part


def share_join(value, part):
    return in_order(value, join(part, "d"), "f", 0)


def sum_everywhere(value):
    for axis in ("d", "f", "c", "b", "a"):
        value = value + swap(value, axis)
    return value


def together(*values):
    return lax.optimization_barrier(values)


def two_parts(value):
    high = lax.reduce_precision(value, 8, 7)
    return [high.astype(jnp.bfloat16), (value - high).astype(jnp.bfloat16)]


def angles(number, fine, coarse):
    cos_b, sin_b = fine[0], fine[1]
    cos_a = coarse[0, pl.ds(number, 1), :]
    sin_a = coarse[1, pl.ds(number, 1), :]
    return cos_a * cos_b - sin_a * sin_b, sin_a * cos_b + cos_a * sin_b


def block_angles(chunk, pieces, fine, coarse):
    pairs = [angles(chunk * pieces + n, fine, coarse) for n in range(pieces)]
    return (
        jnp.concatenate([one[0] for one in pairs], 0),
        jnp.concatenate([one[1] for one in pairs], 0),
    )


def lane_of(shape):
    return lax.broadcasted_iota(jnp.int32, shape, 1)


def attention_forward(
    place, h_place, first_key, low_own, high_own, low_next, high_next, weight, fine, coarse,
    start, query_out, key_out, value_out, mixed_out, attended_out, value_t,
):
    rows = query_out.shape[0]
    block = QUERY_BLOCK
    pieces = block // 64

    def project(chunk, carry):
        def rows_of(own, following):
            found = []
            for n in range(pieces):
                spot = h_place[chunk * pieces + n]
                at = pl.ds(pl.multiple_of((spot % 16) * 64, 64), 64)
                found.append(jnp.where(spot < 16, own[at, :], following[at, :]))
            return jnp.concatenate(found, 0)

        low = rows_of(low_own, low_next)
        high = rows_of(high_own, high_next)
        here = pl.ds(pl.multiple_of(chunk * block, block), block)
        both = jnp.dot(low, weight[:512, :], preferred_element_type=jnp.float32) + jnp.dot(
            high, weight[512:, :], preferred_element_type=jnp.float32
        )
        pair = both[:, :128]
        values = both[:, 128:].astype(jnp.bfloat16)
        lane = lane_of((block, 128))
        turned = jnp.where(
            lane % 64 < 32, -pltpu.roll(pair, 96, 1), pltpu.roll(pair, 32, 1)
        )
        cosine, sine = block_angles(chunk, pieces, fine, coarse)
        pair = pair * cosine + turned * sine
        pair = pair.astype(jnp.bfloat16).astype(jnp.float32)
        key_out[here, :] = jnp.where(lane >= 64, pair, 0.0).astype(jnp.bfloat16)
        query_out[here, :] = jnp.where(
            lane >= 64, pltpu.roll(pair, 64, 1) * (1.0 / math.sqrt(HEAD_SIZE)), 0.0
        ).astype(jnp.bfloat16)
        value_out[here, :] = values
        turned_values = jnp.transpose(values.astype(jnp.float32))
        ones = lax.broadcasted_iota(jnp.int32, (128, block), 0) == 64
        value_t[:, here] = jnp.where(ones, 1.0, turned_values).astype(jnp.bfloat16)
        return carry

    lax.fori_loop(0, rows // block, project, 0)

    def attend(number, carry):
        here = pl.ds(pl.multiple_of(number * block, block), block)
        queries = query_out[here, :]
        begin = start[:, here]
        query_at = lax.broadcasted_iota(jnp.int32, (block, block), 1) + number * block

        def turn(key_number, state):
            top, total = state
            there = pl.ds(pl.multiple_of(key_number * block, block), block)
            scores = lax.dot_general(
                key_out[there, :], queries, (((1,), (1,)), ((), ())),
                preferred_element_type=jnp.float32,
            )
            key_at = lax.broadcasted_iota(jnp.int32, (block, block), 0) + key_number * block
            allowed = (key_at >= begin) & (key_at <= query_at)
            scores = jnp.where(allowed, scores, MASK_FILL_VALUE)
            new_top = jnp.maximum(top, jnp.max(scores, axis=0, keepdims=True))
            weights = jnp.exp(scores - new_top).astype(jnp.bfloat16)
            total = total * jnp.exp(top - new_top) + jnp.dot(
                value_t[:, there], weights, preferred_element_type=jnp.float32
            )
            return new_top, total

        top, total = lax.fori_loop(
            first_key[number],
            number + 1,
            turn,
            (
                jnp.full((1, block), MASK_FILL_VALUE, jnp.float32),
                jnp.zeros((128, block), jnp.float32),
            ),
        )
        weight_sum = total[64:65, :]
        mixed = total * (1.0 / weight_sum)
        log_total = top + jnp.log(weight_sum)
        mixed_out[:64, here] = mixed[:64, :]
        mixed_out[64:72, here] = jnp.broadcast_to(log_total, (8, block))
        upright = jnp.transpose(mixed)[:, :64].astype(jnp.bfloat16)
        for n in range(pieces):
            rows_there = pl.ds(pl.multiple_of(place[number * pieces + n] * 64, 64), 64)
            attended_out[rows_there, :] = upright[n * 64 : (n + 1) * 64, :]
        return carry

    lax.fori_loop(0, rows // block, attend, 0)


def attention_backward(
    place, first_key, core, query, key, value, mixed, grad, fine, coarse, start,
    keep_out, send_out, key_t, pair_sum, value_sum,
):
    rows = query.shape[0]
    block = QUERY_BLOCK
    pieces = block // 64
    scale = 1.0 / math.sqrt(HEAD_SIZE)

    def prepare(chunk, carry):
        here = pl.ds(pl.multiple_of(chunk * block, block), block)
        turned = jnp.transpose(key[here, :].astype(jnp.float32))
        key_t[:, here] = turned[64:, :].astype(jnp.bfloat16)
        pair_sum[here, :] = jnp.zeros((block, 128), jnp.float32)
        value_sum[here, :] = jnp.zeros((block, 128), jnp.float32)
        return carry

    lax.fori_loop(0, rows // block, prepare, 0)

    def storage(number):
        return [
            pl.ds(pl.multiple_of(place[number * pieces + n] * 64, 64), 64) for n in range(pieces)
        ]

    def attend(number, carry):
        here = pl.ds(pl.multiple_of(number * block, block), block)
        queries = query[here, :]
        incoming = jnp.concatenate([grad[one, :] for one in storage(number)], 0)
        nothing = jnp.zeros((block, 64), jnp.bfloat16)
        padded = jnp.concatenate([incoming, nothing], 1)
        upper = jnp.concatenate([nothing, incoming], 1)
        incoming_t = jnp.transpose(padded.astype(jnp.float32))[:64, :]
        log_total = mixed[64:65, here]
        delta = jnp.sum(incoming_t * mixed[:64, here], axis=0, keepdims=True)
        begin = start[:, here]
        query_at = lax.broadcasted_iota(jnp.int32, (block, block), 1) + number * block

        def turn(key_number, total):
            there = pl.ds(pl.multiple_of(key_number * block, block), block)
            scores = lax.dot_general(
                key[there, :], queries, (((1,), (1,)), ((), ())),
                preferred_element_type=jnp.float32,
            )
            key_at = lax.broadcasted_iota(jnp.int32, (block, block), 0) + key_number * block
            allowed = (key_at >= begin) & (key_at <= query_at)
            probs = jnp.where(allowed, jnp.exp(scores - log_total), 0.0)
            grad_probs = lax.dot_general(
                value[there, :], padded, (((1,), (1,)), ((), ())),
                preferred_element_type=jnp.float32,
            )
            grad_scores = (probs * (grad_probs - delta)).astype(jnp.bfloat16)
            value_sum[there, :] += jnp.dot(
                probs.astype(jnp.bfloat16), upper, preferred_element_type=jnp.float32
            )
            pair_sum[there, :] += jnp.dot(
                grad_scores, queries, preferred_element_type=jnp.float32
            )
            return total + jnp.dot(
                key_t[:, there], grad_scores, preferred_element_type=jnp.float32
            )

        total = lax.fori_loop(
            first_key[number], number + 1, turn, jnp.zeros((64, block), jnp.float32)
        )
        tall = jnp.concatenate([total * scale, jnp.zeros((64, block), jnp.float32)], 0)
        pair_sum[here, :] += jnp.transpose(tall)
        return carry

    lax.fori_loop(0, rows // block, attend, 0)

    def finish(number, carry):
        here = pl.ds(pl.multiple_of(number * block, block), block)
        pair = pair_sum[here, :]
        lane = lane_of((block, 128))
        cosine, sine = block_angles(number, pieces, fine, coarse)
        across = pair * sine
        turned = jnp.where(
            lane % 64 < 32, pltpu.roll(across, 96, 1), -pltpu.roll(across, 32, 1)
        )
        pair = pair * cosine + turned
        values = value_sum[here, :]
        keys_stay = core[0] == 0
        keep = jnp.where((lane < 64) | keys_stay, pair, values)
        send = jnp.where(lane < 64, 0.0, jnp.where(keys_stay, values, pair)).astype(jnp.bfloat16)
        for n, one in enumerate(storage(number)):
            keep_out[one, :] = keep[n * 64 : (n + 1) * 64, :]
            send_out[one, :] = send[n * 64 : (n + 1) * 64, :]
        return carry

    lax.fori_loop(0, rows // block, finish, 0)


def expert_rows(
    where, rows, grad, up_weight, down_weight,
    copy_out, result_out, activation_out, pair_out, pre_out,
):
    f32, bf16 = jnp.float32, jnp.bfloat16
    width = grad.shape[3]
    count = rows.shape[0]
    expert = where[0]
    extra = rows[:, width:].astype(f32)
    lane = lane_of((count, EXTRA))
    gate = jnp.sum(
        jnp.where((lane == expert) | (lane == expert + E), extra, 0.0), axis=1, keepdims=True
    )
    before = jnp.dot(rows[:, :width], up_weight[...], preferred_element_type=f32)
    gate_pre = before[:, :F]
    up_pre = before[:, F:]
    sigma = jax.nn.sigmoid(gate_pre)
    swish = gate_pre * sigma
    activation = (swish * up_pre).astype(bf16)
    activation_out[...] = activation
    result = jnp.dot(activation, down_weight[...], preferred_element_type=f32).astype(bf16)
    result = result.astype(f32)
    grads = grad[...].reshape(count, width).astype(f32)
    grad_gate = jnp.sum(grads * result, axis=1, keepdims=True)
    result_out[...] = (gate * result).astype(bf16)
    pair = (gate * grads).astype(bf16)
    pair_out[...] = pair
    grad_activation = lax.dot_general(
        pair, down_weight[...], (((1,), (1,)), ((), ())), preferred_element_type=f32
    )
    pre_out[:, :F] = (
        grad_activation * up_pre * sigma * (1.0 + gate_pre * (1.0 - sigma))
    ).astype(bf16)
    pre_out[:, F:] = (grad_activation * swish).astype(bf16)
    copy_out[:, :width] = lax.dot_general(
        pre_out[...], up_weight[...], (((1,), (1,)), ((), ())), preferred_element_type=f32
    ).astype(bf16)
    high = grad_gate.astype(bf16).astype(f32)
    copy_out[:, width:] = jnp.where(
        lane == expert, high, jnp.where(lane == expert + E, grad_gate - high, 0.0)
    ).astype(bf16)


def expert_call(half, where, rows, grads, up_weight, down_weight):
    count, full = rows.shape
    width = grads.shape[3]
    steps = 2
    block = count // steps
    bf16 = jnp.bfloat16
    row_spec = lambda columns: pl.BlockSpec((block, columns), lambda i, w: (i, 0))
    whole = lambda a: pl.BlockSpec(a.shape, lambda i, w: (0, 0), pipeline_mode=pl.Buffered(1))
    columns = (full, width, F, width, 2 * F)
    return pl.pallas_call(
        expert_rows,
        out_shape=[jax.ShapeDtypeStruct((count, n), bf16) for n in columns],
        grid_spec=pltpu.PrefetchScalarGridSpec(
            num_scalar_prefetch=1,
            grid=(steps,),
            in_specs=[
                row_spec(full),
                pl.BlockSpec((16 // steps, 1, MOST, width), lambda i, w: (i, half, 0, 0)),
                whole(up_weight),
                whole(down_weight),
            ],
            out_specs=[row_spec(n) for n in columns],
        ),
        compiler_params=pltpu.CompilerParams(vmem_limit_bytes=60 << 20),
    )(where, rows, grads, up_weight, down_weight)


def assemble(first, second, qkv_out, out_out, beside_out, gain_out):
    f32 = jnp.float32
    for pair in range(8):
        for source, rows, at in ((first, 400, 0), (second, 112, 400)):
            left = source[2 * pair, :rows, :].astype(f32)
            right = source[2 * pair + 1, :rows, :].astype(f32)
            here = slice(at, at + rows)
            qkv_out[here, pair * 128 : (pair + 1) * 128] = jnp.concatenate(
                [left[:, :64], right[:, :64]], 1
            )
            qkv_out[here, 1024 + pair * 64 : 1024 + (pair + 1) * 64] = left[:, 64:]
            qkv_out[here, 1536 + pair * 64 : 1536 + (pair + 1) * 64] = right[:, 64:]
    total = jnp.zeros((16, 128), f32)
    for device in range(16):
        bits = [(device >> n) & 1 for n in range(4)]
        at = bits[0] * 256 + bits[1] * 128 + bits[2] * 64 + bits[3] * 32
        for part in range(8):
            out_out[at : at + 32, part * 128 : (part + 1) * 128] = second[
                device, 112 + part * 32 : 144 + part * 32, :
            ].astype(f32)
        beside_out[at : at + 32, :] = second[device, 368:400, :].astype(f32)
        total = total + second[device, 400:416, :].astype(f32)
    gain_out[...] = total[:8, :] + total[8:, :]


def whole_call(kernel, scalars, outs, scratch, vmem):
    def run(*operands):
        spec = pl.BlockSpec(memory_space=pltpu.VMEM)
        return pl.pallas_call(
            kernel,
            out_shape=outs,
            grid_spec=pltpu.PrefetchScalarGridSpec(
                num_scalar_prefetch=scalars,
                grid=(),
                in_specs=[spec] * (len(operands) - scalars),
                out_specs=[spec] * len(outs),
                scratch_shapes=scratch,
            ),
            compiler_params=pltpu.CompilerParams(vmem_limit_bytes=vmem),
        )(*operands)

    return run


def fast_shards(
    hidden_in, block_order, segment_ids, cotangent, attn_gain, query_key_value_weight,
    w_out, ffn_gain, w_router, routes, expert_in, expert_out,
):
    bf16, f32 = jnp.bfloat16, jnp.float32
    rows = hidden_in.shape[1]
    width = hidden_in.shape[2]
    length = rows * 16
    capacity = length * TOPK * 9 // (8 * E)
    ia, ib, ic, idd, jf = (lax.axis_index(name) for name in EVERY)
    mine = ia * 8 + ib * 4 + ic * 2 + idd
    expert = jf * 16 + mine
    low_half = jf == 0

    inputs = hidden_in[0].astype(f32)
    scale_one = rms_scale(inputs)
    norm_one = inputs * scale_one
    gain_one_f = join(attn_gain, "f").astype(f32)
    h_one = (norm_one * gain_one_f).astype(bf16)

    (
        h_one, block_order, segment_ids, query_key_value_weight, w_out, ffn_gain, w_router,
        expert_in, expert_out,
    ) = together(
        h_one, block_order, segment_ids, query_key_value_weight, w_out, ffn_gain, w_router,
        expert_in, expert_out,
    )
    both = gather_step(spread(h_one), "a")

    def columns_of(start, number, low_first):
        pair = lax.dynamic_slice_in_dim(query_key_value_weight, start + number * 128, 128, 1)
        return jnp.where(low_first, pair[:, :64], pair[:, 64:])

    my_columns = jnp.concatenate(
        [
            columns_of(0, mine // 2, idd == 0),
            columns_of(1024, mine // 4, ic == 0),
            columns_of(1536, mine // 4, ic == 0),
            jnp.zeros((512, 64), bf16),
        ],
        1,
    )
    other_columns = swap(my_columns, "f")

    route = routes[0]
    named = jnp.any(route[:, :, None] == jnp.arange(E, dtype=jnp.int32)[None, None, :], axis=1)
    counts = spread(jnp.sum(named.astype(f32), axis=0, keepdims=True))
    named_b = named.astype(bf16)
    earlier = (jnp.arange(rows)[:, None] > jnp.arange(rows)[None, :]).astype(bf16)
    rank = jnp.dot(earlier, named_b, preferred_element_type=f32)
    row_of = jnp.where(named, rank, -1.0)
    counts = gather_step(counts, "a")
    expert_weights = jnp.concatenate([expert_in, expert_out], 1)
    both, row_of, cotangent, counts, expert_weights = together(
        both, row_of, cotangent, counts, expert_weights
    )
    low = gather_step(both[..., :512], "b")
    high = gather_step(both[..., 512:], "c")
    other_row_of = swap(row_of, "a")
    other_cotangent = swap(cotangent[0], "a")
    counts = gather_step(counts, "c")

    def picks(rows_of):
        half = rows_of.reshape(rows, 2, 2, 8)
        half = jnp.where(ia == 0, half[:, :, 0], half[:, :, 1])
        half = half.transpose(2, 1, 0).reshape(16, 1, rows)
        return (half == jnp.arange(MOST, dtype=f32)[None, :, None]).astype(bf16)

    def build_rows(choice, tokens):
        return lax.dot_general(
            choice, tokens, (((2,), (0,)), ((), ())), preferred_element_type=f32
        ).astype(bf16)

    def exchange(sent):
        return lax.all_to_all(sent, HALF, split_axis=0, concat_axis=0, tiled=True)

    low, high, other_columns, counts = together(low, high, other_columns, counts)
    low = gather_step(low, "c")
    high = gather_step(high, "b")
    out_part = share_swap(w_out)
    other_gain_two = swap(ffn_gain, "f")
    other_router = swap(w_router, "f")
    low, high, other_cotangent, other_row_of, expert_weights, out_part = together(
        low, high, other_cotangent, other_row_of, expert_weights, out_part
    )
    low_own = low.reshape(length // 2, 512)
    high_own = high.reshape(length // 2, 512)
    low_next = swap(low_own, "d")
    high_next = swap(high_own, "d")
    expert_weights = lax.all_to_all(
        expert_weights, CTX, split_axis=0, concat_axis=0, tiled=True
    )
    counts = gather_step(gather_step(counts, "d"), "b")
    head_weight = in_order(my_columns, other_columns, "f", 0)

    order = block_order[0]
    blocks = order.shape[0]
    place = jnp.sum(
        jnp.where(order[None, :] == jnp.arange(blocks, dtype=jnp.int32)[:, None],
                  jnp.arange(blocks, dtype=jnp.int32)[None, :], 0),
        axis=1,
    )
    document = segment_ids[0]
    start = jnp.sum((document[:, None] < document[None, :]).astype(jnp.int32), axis=0)
    first_key = start[::QUERY_BLOCK] // QUERY_BLOCK
    start = start[None, :]
    steps = jnp.arange(HEAD_SIZE // 2, dtype=f32)
    frequency = jnp.power(THETA, -2.0 * steps / HEAD_SIZE)
    angle_a = (jnp.arange(length // 64, dtype=f32) * 64.0)[:, None] * frequency[None, :]
    angle_b = jnp.arange(64, dtype=f32)[:, None] * frequency[None, :]
    coarse = jnp.tile(jnp.stack([jnp.cos(angle_a), jnp.sin(angle_a)]), (1, 1, 4))
    fine = jnp.tile(jnp.stack([jnp.cos(angle_b), jnp.sin(angle_b)]), (1, 1, 4))
    storage = jnp.arange(blocks, dtype=jnp.int32)
    held = (((storage // 2) % 2) ^ idd) * (blocks // 2) + (storage // 4) * 2 + storage % 2
    h_place = jnp.sum(jnp.where(place[:, None] == storage[None, :], held[None, :], 0), axis=1)
    storage = jnp.arange(blocks, dtype=jnp.int32)
    held = (((storage // 2) % 2) ^ idd) * (blocks // 2) + (storage // 4) * 2 + storage % 2
    h_place = jnp.sum(jnp.where(place[:, None] == storage[None, :], held[None, :], 0), axis=1)
    head_weight, out_part, other_gain_two, other_router, query_key_value_weight = together(
        head_weight, out_part, other_gain_two, other_router, query_key_value_weight
    )
    weight_part = share_swap(query_key_value_weight)
    query, key, value, mixed, attended_head = whole_call(
        attention_forward,
        3,
        [
            jax.ShapeDtypeStruct((length, 128), bf16),
            jax.ShapeDtypeStruct((length, 128), bf16),
            jax.ShapeDtypeStruct((length, 128), bf16),
            jax.ShapeDtypeStruct((72, length), f32),
            jax.ShapeDtypeStruct((length, 64), bf16),
        ],
        [pltpu.VMEM((128, length), bf16)],
        60 << 20,
    )(
        place, h_place, first_key, low_own, high_own, low_next, high_next, head_weight, fine,
        coarse, start,
    )

    def to_tokens(value_heads):
        return lax.all_to_all(
            value_heads.reshape(16, rows, -1), CTX, split_axis=0, concat_axis=0, tiled=True
        )

    pick_mine = picks(row_of)
    pick_other = picks(other_row_of)
    grad_rows = jnp.concatenate(
        [build_rows(pick_mine, cotangent[0]), build_rows(pick_other, other_cotangent)], 1
    )
    out_full = share_join(w_out, out_part)
    gain_two_f = in_order(ffn_gain, other_gain_two, "f", 0).astype(f32)
    router_full = in_order(w_router, other_router, "f", 0)
    attended_head, expert_weights, grad_rows, out_full, weight_part = together(
        attended_head, expert_weights, grad_rows, out_full, weight_part
    )
    attended = to_tokens(attended_head)
    weight_full = share_join(query_key_value_weight, weight_part)
    attended, grad_rows, counts = together(attended, grad_rows, counts)
    grad_rows = exchange(grad_rows)
    attended = attended.transpose(1, 0, 2).reshape(rows, 1024)
    middle_state = inputs + jnp.dot(attended, out_full, preferred_element_type=f32)
    scale_two = rms_scale(middle_state)
    norm_two = middle_state * scale_two
    h_two = (norm_two * gain_two_f).astype(bf16)
    logits = jnp.dot(h_two, router_full, preferred_element_type=f32)
    top = jnp.max(jnp.where(named, logits, MASK_FILL_VALUE), axis=-1, keepdims=True)
    weights = jnp.where(named, jnp.exp(logits - top), 0.0)
    gates = weights / jnp.sum(weights, axis=-1, keepdims=True)
    passed = (jnp.arange(16)[:, None] < mine).astype(f32)
    offset = jnp.sum(counts.reshape(16, E) * passed, axis=0, keepdims=True)
    kept = (named & (rank + offset < capacity)).astype(f32)
    extended = jnp.concatenate(
        [h_two] + two_parts(gates * kept) + [jnp.zeros((rows, 2 * E), bf16)], 1
    )
    other_extended = swap(extended, "a")
    rows_mine = build_rows(pick_mine, extended)
    rows_mine, grad_rows, weight_full, other_extended = together(
        rows_mine, grad_rows, weight_full, other_extended
    )
    rows_mine = exchange(rows_mine)
    up_weight = expert_weights[:, :64].reshape(width, 2 * F)
    down_weight = expert_weights[:, 64:].reshape(F, width)
    grad_rows = grad_rows.reshape(16, 2, MOST, width)
    rows_other = build_rows(pick_other, other_extended)
    rows_mine, rows_other, up_weight, down_weight = together(
        rows_mine, rows_other, up_weight, down_weight
    )
    rows_other = exchange(rows_other)
    rows_mine = rows_mine.reshape(16 * MOST, width + EXTRA)
    number = expert.astype(jnp.int32)[None]
    copy_mine, result_mine, act_mine, pair_mine, pre_mine = expert_call(
        0, number, rows_mine, grad_rows, up_weight, down_weight
    )
    rows_other, copy_mine = together(rows_other, copy_mine)
    rows_other = rows_other.reshape(16 * MOST, width + EXTRA)
    copy_other, result_other, act_other, pair_other, pre_other = expert_call(
        1, number, rows_other, grad_rows, up_weight, down_weight
    )

    def sum_rows(choice, got):
        return lax.dot_general(
            choice, got, (((0, 1), (0, 1)), ((), ())), preferred_element_type=f32
        )

    away = exchange(copy_other.reshape(16, MOST, width + EXTRA))
    away, copy_mine = together(away, copy_mine)
    home = exchange(copy_mine.reshape(16, MOST, width + EXTRA))
    grad_up_weight = contract_rows(rows_mine[:, :width], pre_mine) + contract_rows(
        rows_other[:, :width], pre_other
    )
    grad_down = contract_rows(act_mine, pair_mine) + contract_rows(act_other, pair_other)
    expert_grads = jnp.concatenate(
        [
            grad_up_weight.astype(bf16).reshape(16, 64, 2 * F),
            grad_down.astype(bf16).reshape(16, 32, width),
        ],
        1,
    )
    away_sum = swap(sum_rows(pick_other, away).astype(bf16), "a")
    home, away_sum, expert_grads = together(home, away_sum, expert_grads)
    back = sum_rows(pick_mine, home) + away_sum.astype(f32)

    gate_grads = (back[:, width : width + E] + back[:, width + E : width + 2 * E]) * kept
    grad_logits = gates * (gate_grads - jnp.sum(gates * gate_grads, axis=-1, keepdims=True))
    grad_h_two = back[:, :width] + lax.dot_general(
        grad_logits, router_full.astype(f32), (((1,), (1,)), ((), ())), precision=HIGHEST
    )
    grad_out = cotangent[0].astype(f32)
    scaled_two = grad_h_two * gain_two_f
    grad_mid = grad_out + scale_two * (
        scaled_two - norm_two * jnp.mean(scaled_two * norm_two, axis=-1, keepdims=True)
    )
    grad_branch = grad_mid.astype(bf16)
    attended_gradient = contract_columns(grad_branch, out_full).astype(bf16)
    grad_heads = to_tokens(attended_gradient.reshape(rows, 16, 64).transpose(1, 0, 2))
    grad_heads = grad_heads.reshape(length, 64)

    grad_router_part = lax.dot_general(
        h_two.astype(f32), grad_logits, (((0,), (0,)), ((), ())), precision=HIGHEST
    )
    grad_gain_two = jnp.sum(grad_h_two * norm_two, axis=0)
    beside = jnp.concatenate(
        [grad_router_part, grad_gain_two[:, None], jnp.zeros((width, 128 - E - 1), f32)], 1
    ).reshape(2, 2, 256, 128)
    by_core = attended.reshape(rows, 2, 2, 256)

    def rows_at(core):
        columns = lax.dynamic_slice_in_dim(by_core, core, 1, 2).reshape(rows, 512)
        others = lax.dynamic_slice_in_dim(beside, core, 1, 1).reshape(512, 128)
        return jnp.concatenate([contract_rows(columns, grad_branch), others], 1)

    out_sum = rows_at(idd)
    leaving = rows_at(1 - idd).astype(bf16)

    def halve(total, axis):
        count = total.shape[0] // 2
        index = lax.axis_index(axis)
        keep = lax.dynamic_slice_in_dim(total, index * count, count, 0)
        send = lax.dynamic_slice_in_dim(total, (1 - index) * count, count, 0)
        return keep + swap(send.astype(bf16), axis).astype(f32)

    results = jnp.concatenate(
        [result_mine.reshape(16, MOST, width), result_other.reshape(16, MOST, width)], 1
    )
    grad_heads, results = together(grad_heads, results)
    results = exchange(results)

    keep, send = whole_call(
        attention_backward,
        3,
        [jax.ShapeDtypeStruct((length, 128), f32), jax.ShapeDtypeStruct((length, 128), bf16)],
        [
            pltpu.VMEM((64, length), bf16),
            pltpu.VMEM((length, 128), f32),
            pltpu.VMEM((length, 128), f32),
        ],
        60 << 20,
    )(
        place, first_key, idd.astype(jnp.int32)[None], query, key, value, mixed, grad_heads,
        fine, coarse, start,
    )
    keep, send, out_sum, leaving = together(keep, send, out_sum, leaving)
    out_sum = out_sum + swap(leaving, "d").astype(f32)
    grad_columns = (keep + swap(send, "d").astype(f32)).astype(bf16)
    out_sum = halve(out_sum, "f")
    results, expert_grads = together(results, expert_grads)
    expert_grads = lax.all_to_all(expert_grads, CTX, split_axis=0, concat_axis=0, tiled=True)
    for axis in ("c", "b", "a"):
        out_sum = halve(out_sum, axis)
    out_rows = out_sum.reshape(32, 9, 128).transpose(1, 0, 2).reshape(288, 128).astype(bf16)

    by_core = grad_columns.reshape(8, 2, rows, 128)
    own = jnp.where(idd == 0, by_core[:, 0], by_core[:, 1]).reshape(length // 2, 128)
    following = jnp.where(idd == 0, by_core[:, 1], by_core[:, 0]).reshape(length // 2, 128)
    low_part = contract_rows(low_own, own) + contract_rows(low_next, following)
    high_part = contract_rows(high_own, own) + contract_rows(high_next, following)
    columns_grad = jnp.where(low_half, low_part, high_part) + swap(
        jnp.where(low_half, high_part, low_part), "f"
    )
    my_weight = jnp.concatenate(
        [my_columns[:, :64], jnp.where(idd == 0, my_columns[:, 64:128], my_columns[:, 128:192])], 1
    )
    gain_part = jnp.sum(columns_grad * my_weight.astype(f32), axis=1).reshape(4, 128)
    gain_part = jnp.concatenate([gain_part, jnp.zeros((4, 128), f32)], 0)
    columns_grad = jnp.concatenate(
        [columns_grad.astype(bf16), out_rows] + two_parts(gain_part), 0
    )
    gathered = gather_step(spread(columns_grad), "a")
    first = gather_step(gathered[..., :400, :], "b")
    second = gather_step(gathered[..., 400:, :], "c")
    first = gather_step(first, "c")
    second = gather_step(second, "b")
    ready, expert_grads = together(grad_columns, expert_grads)
    grad_projected = to_tokens(ready)
    grad_expert_in = expert_grads[:, :64].astype(f32)
    grad_expert_out = expert_grads[:, 64:].astype(f32)
    first, second, grad_projected = together(first, second, grad_projected)
    first = gather_step(first, "d")
    second = gather_step(second, "d")

    grad_projected = grad_projected.transpose(1, 0, 2)
    grad_kv = grad_projected[:, :, 64:].reshape(rows, 8, 2, 64)
    grad_projected = jnp.concatenate(
        [
            grad_projected[:, :, :64].reshape(rows, 1024),
            grad_kv[:, :, 0].reshape(rows, 512),
            grad_kv[:, :, 1].reshape(rows, 512),
        ],
        1,
    )
    grad_h_one = contract_columns(grad_projected, weight_full)
    scaled_one = grad_h_one * gain_one_f
    grad_inputs = grad_mid + scale_one * (
        scaled_one - norm_one * jnp.mean(scaled_one * norm_one, axis=-1, keepdims=True)
    )
    share_qkv, share_out, beside, gain_sum = whole_call(
        assemble,
        0,
        [
            jax.ShapeDtypeStruct((512, 2048), f32),
            jax.ShapeDtypeStruct((512, 1024), f32),
            jax.ShapeDtypeStruct((512, 128), f32),
            jax.ShapeDtypeStruct((8, 128), f32),
        ],
        [],
        32 << 20,
    )(first.reshape(16, 400, 128), second.reshape(16, 416, 128))
    share_router = beside[:, :E]
    share_two = beside[:, E]
    share_one = gain_sum[:4].reshape(512) / attn_gain.astype(f32)
    mixture = sum_rows(pick_mine, results[:, :MOST]) + swap(
        sum_rows(pick_other, results[:, MOST:]).astype(bf16), "a"
    ).astype(f32)
    hidden_out = (middle_state + mixture).astype(bf16)
    return (
        hidden_out[None],
        grad_inputs[None],
        share_one,
        share_qkv,
        share_out,
        share_two,
        share_router,
        grad_expert_in,
        grad_expert_out,
    )


def fast_solution(mesh):
    fine = Mesh(mesh.devices.reshape(2, 2, 2, 2, 2), EVERY)
    placed = (
        P("f", CTX, None),
        P("f", None),
        P("f", None),
        P("f", CTX, None),
        P("f"),
        P("f", None),
        P("f", None),
        P("f"),
        P("f", None),
        P("f", CTX, None),
        P("f", CTX, None),
        P("f", CTX, None),
    )
    return jax.shard_map(
        fast_shards,
        mesh=fine,
        in_specs=placed,
        out_specs=(
            P("f", CTX, None),
            P("f", CTX, None),
            P("f"),
            P("f", None),
            P("f", None),
            P("f"),
            P("f", None),
            P("f", CTX, None),
            P("f", CTX, None),
        ),
        check_vma=False,
    )


def solution(mesh):
    if mesh.shape["ctx"] == QUERY_HEADS and mesh.shape["fsdp"] * mesh.shape["ctx"] == E:
        return fast_solution(mesh)
    return general_solution(mesh)
```

```python
import math

import jax
import jax.numpy as jnp
from jax import lax
from jax.experimental import pallas as pl
from jax.experimental.pallas import tpu as pltpu
from jax.sharding import Mesh
from jax.sharding import PartitionSpec as P

QUERY_HEADS = 16
KEY_VALUE_HEADS = 8
HEAD_SIZE = 64
E = 32
TOPK = 8
F = 512
MOST = 48


EPSILON = 1e-06
THETA = 10000.0
MASK_FILL_VALUE = -1e30
HIGHEST = lax.Precision.HIGHEST


def carried_in(value, axis, combine, identity):
    length, mine = (lax.axis_size(axis), lax.axis_index(axis))
    everything = lax.all_gather(value, axis)
    start = jnp.broadcast_to(jnp.asarray(identity, value.dtype), value.shape)

    def turn(k, before):
        reached = k < mine
        new = combine(before, everything[k])
        return jnp.where(reached, new, before)

    return lax.fori_loop(0, length, turn, start)


def rms_scale(value_rows):
    return lax.rsqrt(jnp.mean(value_rows * value_rows, axis=-1, keepdims=True) + EPSILON)


def rotate(value_rows):
    middle = value_rows.shape[-1] // 2
    return jnp.concatenate([-value_rows[..., middle:], value_rows[..., :middle]], axis=-1)


def rotate_back(value_rows):
    middle = value_rows.shape[-1] // 2
    return jnp.concatenate([value_rows[..., middle:], -value_rows[..., :middle]], axis=-1)


def rope_tables(position):
    steps = jnp.arange(HEAD_SIZE // 2, dtype=jnp.float32)
    frequency = jnp.power(THETA, -2.0 * steps / HEAD_SIZE)
    angle = position.astype(jnp.float32)[:, None] * frequency[None, :]
    angle = jnp.concatenate([angle, angle], axis=-1)
    return (jnp.cos(angle), jnp.sin(angle))


def contract_rows(left, right):
    return lax.dot_general(
        left, right, (((0,), (0,)), ((), ())), preferred_element_type=jnp.float32
    )


def contract_columns(left, right):
    return lax.dot_general(
        left, right, (((1,), (1,)), ((), ())), preferred_element_type=jnp.float32
    )


def own_rows(total, rank, count):
    share = total.shape[0] // count
    return lax.dynamic_slice_in_dim(total, rank * share, share, 0)


def general_shards(
    hidden_in,
    block_order,
    segment_ids,
    cotangent,
    attn_gain,
    query_key_value_weight,
    w_out,
    ffn_gain,
    w_router,
    routes,
    expert_in,
    expert_out,
):
    count_of_rows = hidden_in.shape[1]
    width = hidden_in.shape[2]
    ctx_count = lax.axis_size("ctx")
    fsdp_count = lax.axis_size("fsdp")
    sequence_length = count_of_rows * ctx_count
    half_block = count_of_rows // 2
    capacity = sequence_length * TOPK * 9 // (8 * E)
    query_total_width = QUERY_HEADS * HEAD_SIZE
    key_total_width = KEY_VALUE_HEADS * HEAD_SIZE
    query_group = QUERY_HEADS // KEY_VALUE_HEADS
    scale = 1.0 / math.sqrt(HEAD_SIZE)
    key_block_rows = min(1024, sequence_length)
    block_count = sequence_length // key_block_rows
    pair_count = count_of_rows * TOPK
    gain_one, qkv_full, out_full, gain_two, router_full = (
        lax.all_gather(attn_gain, "fsdp", axis=0, tiled=True),
        lax.all_gather(query_key_value_weight, "fsdp", axis=0, tiled=True),
        lax.all_gather(w_out, "fsdp", axis=0, tiled=True),
        lax.all_gather(ffn_gain, "fsdp", axis=0, tiled=True),
        lax.all_gather(w_router, "fsdp", axis=0, tiled=True),
    )
    up_full, down_full = (
        lax.all_gather(expert_in, "ctx", axis=1, tiled=True),
        lax.all_gather(expert_out, "ctx", axis=1, tiled=True),
    )
    key_position = (
        block_order[0][:, None] * half_block + jnp.arange(half_block, dtype=jnp.int32)[None, :]
    ).reshape(-1)
    key_document = segment_ids[0][key_position]
    first_row = lax.axis_index("ctx") * count_of_rows
    query_position = lax.dynamic_slice_in_dim(key_position, first_row, count_of_rows, 0)
    query_document = lax.dynamic_slice_in_dim(key_document, first_row, count_of_rows, 0)
    inputs = hidden_in[0].astype(jnp.float32)
    grad_out = cotangent[0].astype(jnp.float32)
    scale_one = rms_scale(inputs)
    norm_one = inputs * scale_one
    gain_one_f = gain_one.astype(jnp.float32)
    h_one = (norm_one * gain_one_f).astype(jnp.bfloat16)
    projected_rows = jnp.dot(h_one, qkv_full, preferred_element_type=jnp.float32)
    cosine, sine = rope_tables(query_position)
    query_raw = projected_rows[:, :query_total_width].reshape(count_of_rows, QUERY_HEADS, HEAD_SIZE)
    unrotated_key = projected_rows[
        :, query_total_width : query_total_width + key_total_width
    ].reshape(count_of_rows, KEY_VALUE_HEADS, HEAD_SIZE)
    query_matrix = (query_raw * cosine[:, None, :] + rotate(query_raw) * sine[:, None, :]).astype(
        jnp.bfloat16
    )
    key_rows = (
        unrotated_key * cosine[:, None, :] + rotate(unrotated_key) * sine[:, None, :]
    ).astype(jnp.bfloat16)
    value_rows = projected_rows[:, query_total_width + key_total_width :].astype(jnp.bfloat16)
    key_value_local = jnp.concatenate(
        [key_rows.reshape(count_of_rows, key_total_width), value_rows], axis=1
    )
    key_value_all = lax.all_gather(key_value_local, "ctx", axis=0, tiled=True)
    grouped_queries = query_matrix.reshape(count_of_rows, KEY_VALUE_HEADS, query_group, HEAD_SIZE)
    block_number = jnp.arange(block_count, dtype=jnp.int32)

    def block_keys(source, index):
        current_rows = lax.dynamic_slice_in_dim(source, index * key_block_rows, key_block_rows, 0)
        block_key_rows = current_rows[:, :key_total_width].reshape(
            key_block_rows, KEY_VALUE_HEADS, HEAD_SIZE
        )
        block_value_rows = current_rows[:, key_total_width:].reshape(
            key_block_rows, KEY_VALUE_HEADS, HEAD_SIZE
        )
        block_position = lax.dynamic_slice_in_dim(
            key_position, index * key_block_rows, key_block_rows, 0
        )
        block_document = lax.dynamic_slice_in_dim(
            key_document, index * key_block_rows, key_block_rows, 0
        )
        allowed = (query_document[:, None] == block_document[None, :]) & (
            block_position[None, :] <= query_position[:, None]
        )
        return (block_key_rows, block_value_rows, allowed)

    def scores_of(block_key_rows, allowed):
        scores = (
            jnp.einsum(
                "qhgd,khd->hgqk",
                grouped_queries,
                block_key_rows,
                preferred_element_type=jnp.float32,
            )
            * scale
        )
        return jnp.where(allowed[None, None], scores, MASK_FILL_VALUE)

    def max_sum(carry, index):
        top, total = carry
        block_key_rows, block_value_rows, allowed = block_keys(key_value_all, index)
        scores = scores_of(block_key_rows, allowed)
        new_top = jnp.maximum(top, jnp.max(scores, axis=-1))
        weights = jnp.where(allowed[None, None], jnp.exp(scores - new_top[..., None]), 0.0)
        total = total * jnp.exp(top - new_top) + jnp.sum(weights, axis=-1)
        return ((new_top, total), None)

    upper_start = jnp.full(
        (KEY_VALUE_HEADS, query_group, count_of_rows), MASK_FILL_VALUE, jnp.float32
    )
    overall_start = jnp.zeros((KEY_VALUE_HEADS, query_group, count_of_rows), jnp.float32)
    (top, total), unused = lax.scan(max_sum, (upper_start, overall_start), block_number)
    log_total = top + jnp.log(total)

    def weighted_values(accum, index):
        block_key_rows, block_value_rows, allowed = block_keys(key_value_all, index)
        scores = scores_of(block_key_rows, allowed)
        probs = jnp.where(allowed[None, None], jnp.exp(scores - log_total[..., None]), 0.0).astype(
            jnp.bfloat16
        )
        return (
            accum
            + jnp.einsum(
                "hgqk,khd->qhgd", probs, block_value_rows, preferred_element_type=jnp.float32
            ),
            None,
        )

    attended_f, unused = lax.scan(
        weighted_values,
        jnp.zeros((count_of_rows, KEY_VALUE_HEADS, query_group, HEAD_SIZE), jnp.float32),
        block_number,
    )
    attended = attended_f.reshape(count_of_rows, query_total_width).astype(jnp.bfloat16)
    middle_state = inputs + jnp.dot(attended, out_full, preferred_element_type=jnp.float32)
    scale_two = rms_scale(middle_state)
    norm_two = middle_state * scale_two
    gain_two_f = gain_two.astype(jnp.float32)
    h_two = (norm_two * gain_two_f).astype(jnp.bfloat16)
    logits = jnp.dot(h_two, router_full, preferred_element_type=jnp.float32)
    route = routes[0]
    gates = jax.nn.softmax(jnp.take_along_axis(logits, route, axis=1), axis=-1)
    flat = route.reshape(-1)
    onehot = (flat[:, None] == jnp.arange(E, dtype=jnp.int32)[None, :]).astype(jnp.int32)
    rank = jnp.sum((jnp.cumsum(onehot, axis=0) - onehot) * onehot, axis=1)
    counts = jnp.sum(onehot, axis=0)

    def add_counts(earlier, later):
        return earlier + later

    offsets = carried_in(counts, "ctx", add_counts, jnp.zeros((E,), jnp.int32))
    slot = jnp.sum(onehot * offsets[None, :], axis=1) + rank
    kept = slot < capacity
    target = jnp.where(kept, flat * MOST + rank, E * MOST)
    safe_target = jnp.minimum(target, E * MOST - 1)
    keep_float = kept.astype(jnp.float32)[:, None]
    token = jnp.arange(pair_count, dtype=jnp.int32) // TOPK
    send_rows = (
        jnp.zeros((E * MOST, width), jnp.bfloat16)
        .at[target]
        .set(h_two[token], mode="drop")
        .reshape(E, MOST, width)
    )
    received = lax.all_to_all(send_rows, "fsdp", split_axis=0, concat_axis=1, tiled=True)
    before = jnp.einsum("erd,edf->erf", received, up_full, preferred_element_type=jnp.float32)
    gate_pre = before[..., :F]
    up_pre = before[..., F:]
    sigma = jax.nn.sigmoid(gate_pre)
    activation = (gate_pre * sigma * up_pre).astype(jnp.bfloat16)
    expert_result = jnp.einsum(
        "erf,efd->erd", activation, down_full, preferred_element_type=jnp.float32
    ).astype(jnp.bfloat16)
    returned = lax.all_to_all(
        expert_result, "fsdp", split_axis=1, concat_axis=0, tiled=True
    ).reshape(E * MOST, width)
    pair_result = (returned[safe_target].astype(jnp.float32) * keep_float).reshape(
        count_of_rows, TOPK, width
    )
    mixture = jnp.sum(gates[..., None] * pair_result, axis=1)
    hidden_out = (middle_state + mixture).astype(jnp.bfloat16)
    grad_pair = (
        (gates[..., None] * grad_out[:, None, :]).reshape(pair_count, width) * keep_float
    ).astype(jnp.bfloat16)
    grad_gates = jnp.sum(grad_out[:, None, :] * pair_result, axis=-1)
    grad_chosen = gates * (grad_gates - jnp.sum(gates * grad_gates, axis=-1, keepdims=True))
    chosen_table = (route[..., None] == jnp.arange(E, dtype=jnp.int32)[None, None, :]).astype(
        jnp.float32
    )
    grad_logits = jnp.sum(grad_chosen[..., None] * chosen_table, axis=1)
    grad_router_part = lax.dot_general(
        h_two.astype(jnp.float32), grad_logits, (((0,), (0,)), ((), ())), precision=HIGHEST
    )
    grad_h_two = lax.dot_general(
        grad_logits, router_full.astype(jnp.float32), (((1,), (1,)), ((), ())), precision=HIGHEST
    )
    send_grads = (
        jnp.zeros((E * MOST, width), jnp.bfloat16)
        .at[target]
        .set(grad_pair, mode="drop")
        .reshape(E, MOST, width)
    )
    grad_received = lax.all_to_all(send_grads, "fsdp", split_axis=0, concat_axis=1, tiled=True)
    grad_activation = jnp.einsum(
        "erd,efd->erf", grad_received, down_full, preferred_element_type=jnp.float32
    )
    grad_down = jnp.einsum(
        "erf,erd->efd", activation, grad_received, preferred_element_type=jnp.float32
    )
    grad_gate = grad_activation * up_pre * sigma * (1.0 + gate_pre * (1.0 - sigma))
    grad_up = grad_activation * gate_pre * sigma
    grad_pre = jnp.concatenate([grad_gate, grad_up], axis=-1).astype(jnp.bfloat16)
    grad_up_weight = jnp.einsum(
        "erd,erf->edf", received, grad_pre, preferred_element_type=jnp.float32
    )
    grad_copy = jnp.einsum(
        "erf,edf->erd", grad_pre, up_full, preferred_element_type=jnp.float32
    ).astype(jnp.bfloat16)
    grad_returned = lax.all_to_all(
        grad_copy, "fsdp", split_axis=1, concat_axis=0, tiled=True
    ).reshape(E * MOST, width)
    grad_h_two = grad_h_two + jnp.sum(
        (grad_returned[safe_target].astype(jnp.float32) * keep_float).reshape(
            count_of_rows, TOPK, width
        ),
        axis=1,
    )
    grad_expert_in, grad_expert_out = (
        lax.psum_scatter(
            grad_up_weight.astype(jnp.bfloat16), "ctx", scatter_dimension=1, tiled=True
        ).astype(jnp.float32),
        lax.psum_scatter(
            grad_down.astype(jnp.bfloat16), "ctx", scatter_dimension=1, tiled=True
        ).astype(jnp.float32),
    )
    grad_gain_two = jnp.sum(grad_h_two * norm_two, axis=0)
    scaled_two = grad_h_two * gain_two_f
    grad_mid = grad_out + scale_two * (
        scaled_two - norm_two * jnp.mean(scaled_two * norm_two, axis=-1, keepdims=True)
    )
    grad_branch = grad_mid.astype(jnp.bfloat16)
    grad_out_weight = contract_rows(attended, grad_branch)
    attended_gradient = contract_columns(grad_branch, out_full).astype(jnp.bfloat16)
    grouped_gradient = attended_gradient.reshape(
        count_of_rows, KEY_VALUE_HEADS, query_group, HEAD_SIZE
    )
    delta = jnp.transpose(
        jnp.sum(grouped_gradient.astype(jnp.float32) * attended_f, axis=-1), (1, 2, 0)
    )

    def block_gradients(query_accum, index):
        block_key_rows, block_value_rows, allowed = block_keys(key_value_all, index)
        scores = scores_of(block_key_rows, allowed)
        probs = jnp.where(allowed[None, None], jnp.exp(scores - log_total[..., None]), 0.0)
        grad_probs = jnp.einsum(
            "qhgd,khd->hgqk", grouped_gradient, block_value_rows, preferred_element_type=jnp.float32
        )
        grad_scores = (probs * (grad_probs - delta[..., None])).astype(jnp.bfloat16)
        query_accum = query_accum + jnp.einsum(
            "hgqk,khd->qhgd", grad_scores, block_key_rows, preferred_element_type=jnp.float32
        )
        grad_keys = (
            jnp.einsum(
                "hgqk,qhgd->khd", grad_scores, grouped_queries, preferred_element_type=jnp.float32
            )
            * scale
        )
        grad_values = jnp.einsum(
            "hgqk,qhgd->khd",
            probs.astype(jnp.bfloat16),
            grouped_gradient,
            preferred_element_type=jnp.float32,
        )
        joined = jnp.concatenate(
            [
                grad_keys.reshape(key_block_rows, key_total_width),
                grad_values.reshape(key_block_rows, key_total_width),
            ],
            axis=1,
        )
        return (query_accum, joined)

    grad_queries, grad_blocks = lax.scan(
        block_gradients,
        jnp.zeros((count_of_rows, KEY_VALUE_HEADS, query_group, HEAD_SIZE), jnp.float32),
        block_number,
    )
    key_value_gradient = lax.psum_scatter(
        grad_blocks.reshape(sequence_length, 2 * key_total_width).astype(jnp.bfloat16),
        "ctx",
        scatter_dimension=0,
        tiled=True,
    ).astype(jnp.float32)
    grad_queries = (grad_queries * scale).reshape(count_of_rows, QUERY_HEADS, HEAD_SIZE)
    local_key_gradient = key_value_gradient[:, :key_total_width].reshape(
        count_of_rows, KEY_VALUE_HEADS, HEAD_SIZE
    )
    grad_values_mine = key_value_gradient[:, key_total_width:]
    grad_query_pre = grad_queries * cosine[:, None, :] + rotate_back(
        grad_queries * sine[:, None, :]
    )
    grad_key_pre = local_key_gradient * cosine[:, None, :] + rotate_back(
        local_key_gradient * sine[:, None, :]
    )
    grad_projected = jnp.concatenate(
        [
            grad_query_pre.reshape(count_of_rows, query_total_width),
            grad_key_pre.reshape(count_of_rows, key_total_width),
            grad_values_mine,
        ],
        axis=1,
    ).astype(jnp.bfloat16)
    grad_qkv_weight = contract_rows(h_one, grad_projected)
    grad_h_one = contract_columns(grad_projected, qkv_full)
    grad_gain_one = jnp.sum(grad_h_one * norm_one, axis=0)
    scaled_one = grad_h_one * gain_one_f
    grad_inputs = grad_mid + scale_one * (
        scaled_one - norm_one * jnp.mean(scaled_one * norm_one, axis=-1, keepdims=True)
    )
    total_one, total_qkv, total_out, total_two, total_router = lax.psum(
        (grad_gain_one, grad_qkv_weight, grad_out_weight, grad_gain_two, grad_router_part),
        ("ctx", "fsdp"),
    )
    fsdp_rank = lax.axis_index("fsdp")
    share_one = own_rows(total_one, fsdp_rank, fsdp_count)
    share_qkv = own_rows(total_qkv, fsdp_rank, fsdp_count)
    share_out = own_rows(total_out, fsdp_rank, fsdp_count)
    share_two = own_rows(total_two, fsdp_rank, fsdp_count)
    share_router = own_rows(total_router, fsdp_rank, fsdp_count)
    return (
        hidden_out[None],
        grad_inputs[None],
        share_one,
        share_qkv,
        share_out,
        share_two,
        share_router,
        grad_expert_in,
        grad_expert_out,
    )


def general_solution(mesh):
    placed = (
        P("fsdp", "ctx", None),
        P("fsdp", None),
        P("fsdp", None),
        P("fsdp", "ctx", None),
        P("fsdp"),
        P("fsdp", None),
        P("fsdp", None),
        P("fsdp"),
        P("fsdp", None),
        P("fsdp", "ctx", None),
        P("fsdp", "ctx", None),
        P("fsdp", "ctx", None),
    )
    return jax.shard_map(
        general_shards,
        mesh=mesh,
        in_specs=placed,
        out_specs=(
            P("fsdp", "ctx", None),
            P("fsdp", "ctx", None),
            P("fsdp"),
            P("fsdp", None),
            P("fsdp", None),
            P("fsdp"),
            P("fsdp", None),
            P("fsdp", "ctx", None),
            P("fsdp", "ctx", None),
        ),
        check_vma=False,
    )


CTX = ("a", "b", "c", "d")
HALF = ("b", "c", "d", "f")
EVERY = ("a", "b", "c", "d", "f")
QUERY_BLOCK = 256
EXTRA = 128


def swap(value, axis):
    return lax.ppermute(value, axis, [(0, 1), (1, 0)])


def in_order(mine, other, axis, dim):
    first = lax.axis_index(axis) == 0
    return jnp.where(
        first, jnp.concatenate([mine, other], dim), jnp.concatenate([other, mine], dim)
    )


def join(value, axis, dim=0):
    return in_order(value, swap(value, axis), axis, dim)


def spread(value):
    return value[(None,) * 4]


def gather_step(held, axis):
    return in_order(held, swap(held, axis), axis, CTX.index(axis))


def share_swap(value):
    half = value.shape[0] // 2
    part = swap(jnp.where(lax.axis_index("d") == 0, value[:half], value[half:]), "f")
    return part


def share_join(value, part):
    return in_order(value, join(part, "d"), "f", 0)


def sum_everywhere(value):
    for axis in ("d", "f", "c", "b", "a"):
        value = value + swap(value, axis)
    return value


def together(*values):
    return lax.optimization_barrier(values)


def two_parts(value):
    high = lax.reduce_precision(value, 8, 7)
    return [high.astype(jnp.bfloat16), (value - high).astype(jnp.bfloat16)]


def angles(number, fine, coarse):
    cos_b, sin_b = fine[0], fine[1]
    cos_a = coarse[0, pl.ds(number, 1), :]
    sin_a = coarse[1, pl.ds(number, 1), :]
    return cos_a * cos_b - sin_a * sin_b, sin_a * cos_b + cos_a * sin_b


def block_angles(chunk, pieces, fine, coarse):
    pairs = [angles(chunk * pieces + n, fine, coarse) for n in range(pieces)]
    return (
        jnp.concatenate([one[0] for one in pairs], 0),
        jnp.concatenate([one[1] for one in pairs], 0),
    )


def lane_of(shape):
    return lax.broadcasted_iota(jnp.int32, shape, 1)


def attention_forward(
    place, h_place, first_key, low_own, high_own, low_next, high_next, weight, fine, coarse,
    start, query_out, key_out, value_out, mixed_out, attended_out, value_t,
):
    rows = query_out.shape[0]
    block = QUERY_BLOCK
    pieces = block // 64

    def project(chunk, carry):
        def rows_of(own, following):
            found = []
            for n in range(pieces):
                spot = h_place[chunk * pieces + n]
                at = pl.ds(pl.multiple_of((spot % 16) * 64, 64), 64)
                found.append(jnp.where(spot < 16, own[at, :], following[at, :]))
            return jnp.concatenate(found, 0)

        low = rows_of(low_own, low_next)
        high = rows_of(high_own, high_next)
        here = pl.ds(pl.multiple_of(chunk * block, block), block)
        both = jnp.dot(low, weight[:512, :], preferred_element_type=jnp.float32) + jnp.dot(
            high, weight[512:, :], preferred_element_type=jnp.float32
        )
        pair = both[:, :128]
        values = both[:, 128:].astype(jnp.bfloat16)
        lane = lane_of((block, 128))
        turned = jnp.where(
            lane % 64 < 32, -pltpu.roll(pair, 96, 1), pltpu.roll(pair, 32, 1)
        )
        cosine, sine = block_angles(chunk, pieces, fine, coarse)
        pair = pair * cosine + turned * sine
        pair = pair.astype(jnp.bfloat16).astype(jnp.float32)
        key_out[here, :] = jnp.where(lane >= 64, pair, 0.0).astype(jnp.bfloat16)
        query_out[here, :] = jnp.where(
            lane >= 64, pltpu.roll(pair, 64, 1) * (1.0 / math.sqrt(HEAD_SIZE)), 0.0
        ).astype(jnp.bfloat16)
        value_out[here, :] = values
        turned_values = jnp.transpose(values.astype(jnp.float32))
        ones = lax.broadcasted_iota(jnp.int32, (128, block), 0) == 64
        value_t[:, here] = jnp.where(ones, 1.0, turned_values).astype(jnp.bfloat16)
        return carry

    lax.fori_loop(0, rows // block, project, 0)

    def attend(number, carry):
        here = pl.ds(pl.multiple_of(number * block, block), block)
        queries = query_out[here, :]
        begin = start[:, here]
        query_at = lax.broadcasted_iota(jnp.int32, (block, block), 1) + number * block

        def turn(key_number, state):
            top, total = state
            there = pl.ds(pl.multiple_of(key_number * block, block), block)
            scores = lax.dot_general(
                key_out[there, :], queries, (((1,), (1,)), ((), ())),
                preferred_element_type=jnp.float32,
            )
            key_at = lax.broadcasted_iota(jnp.int32, (block, block), 0) + key_number * block
            allowed = (key_at >= begin) & (key_at <= query_at)
            scores = jnp.where(allowed, scores, MASK_FILL_VALUE)
            new_top = jnp.maximum(top, jnp.max(scores, axis=0, keepdims=True))
            weights = jnp.exp(scores - new_top).astype(jnp.bfloat16)
            total = total * jnp.exp(top - new_top) + jnp.dot(
                value_t[:, there], weights, preferred_element_type=jnp.float32
            )
            return new_top, total

        top, total = lax.fori_loop(
            first_key[number],
            number + 1,
            turn,
            (
                jnp.full((1, block), MASK_FILL_VALUE, jnp.float32),
                jnp.zeros((128, block), jnp.float32),
            ),
        )
        weight_sum = total[64:65, :]
        mixed = total * (1.0 / weight_sum)
        log_total = top + jnp.log(weight_sum)
        mixed_out[:64, here] = mixed[:64, :]
        mixed_out[64:72, here] = jnp.broadcast_to(log_total, (8, block))
        upright = jnp.transpose(mixed)[:, :64].astype(jnp.bfloat16)
        for n in range(pieces):
            rows_there = pl.ds(pl.multiple_of(place[number * pieces + n] * 64, 64), 64)
            attended_out[rows_there, :] = upright[n * 64 : (n + 1) * 64, :]
        return carry

    lax.fori_loop(0, rows // block, attend, 0)


def attention_backward(
    place, first_key, core, query, key, value, mixed, grad, fine, coarse, start,
    keep_out, send_out, key_t, pair_sum, value_sum,
):
    rows = query.shape[0]
    block = QUERY_BLOCK
    pieces = block // 64
    scale = 1.0 / math.sqrt(HEAD_SIZE)

    def prepare(chunk, carry):
        here = pl.ds(pl.multiple_of(chunk * block, block), block)
        turned = jnp.transpose(key[here, :].astype(jnp.float32))
        key_t[:, here] = turned[64:, :].astype(jnp.bfloat16)
        pair_sum[here, :] = jnp.zeros((block, 128), jnp.float32)
        value_sum[here, :] = jnp.zeros((block, 128), jnp.float32)
        return carry

    lax.fori_loop(0, rows // block, prepare, 0)

    def storage(number):
        return [
            pl.ds(pl.multiple_of(place[number * pieces + n] * 64, 64), 64) for n in range(pieces)
        ]

    def attend(number, carry):
        here = pl.ds(pl.multiple_of(number * block, block), block)
        queries = query[here, :]
        incoming = jnp.concatenate([grad[one, :] for one in storage(number)], 0)
        nothing = jnp.zeros((block, 64), jnp.bfloat16)
        padded = jnp.concatenate([incoming, nothing], 1)
        upper = jnp.concatenate([nothing, incoming], 1)
        incoming_t = jnp.transpose(padded.astype(jnp.float32))[:64, :]
        log_total = mixed[64:65, here]
        delta = jnp.sum(incoming_t * mixed[:64, here], axis=0, keepdims=True)
        begin = start[:, here]
        query_at = lax.broadcasted_iota(jnp.int32, (block, block), 1) + number * block

        def turn(key_number, total):
            there = pl.ds(pl.multiple_of(key_number * block, block), block)
            scores = lax.dot_general(
                key[there, :], queries, (((1,), (1,)), ((), ())),
                preferred_element_type=jnp.float32,
            )
            key_at = lax.broadcasted_iota(jnp.int32, (block, block), 0) + key_number * block
            allowed = (key_at >= begin) & (key_at <= query_at)
            probs = jnp.where(allowed, jnp.exp(scores - log_total), 0.0)
            grad_probs = lax.dot_general(
                value[there, :], padded, (((1,), (1,)), ((), ())),
                preferred_element_type=jnp.float32,
            )
            grad_scores = (probs * (grad_probs - delta)).astype(jnp.bfloat16)
            value_sum[there, :] += jnp.dot(
                probs.astype(jnp.bfloat16), upper, preferred_element_type=jnp.float32
            )
            pair_sum[there, :] += jnp.dot(
                grad_scores, queries, preferred_element_type=jnp.float32
            )
            return total + jnp.dot(
                key_t[:, there], grad_scores, preferred_element_type=jnp.float32
            )

        total = lax.fori_loop(
            first_key[number], number + 1, turn, jnp.zeros((64, block), jnp.float32)
        )
        tall = jnp.concatenate([total * scale, jnp.zeros((64, block), jnp.float32)], 0)
        pair_sum[here, :] += jnp.transpose(tall)
        return carry

    lax.fori_loop(0, rows // block, attend, 0)

    def finish(number, carry):
        here = pl.ds(pl.multiple_of(number * block, block), block)
        pair = pair_sum[here, :]
        lane = lane_of((block, 128))
        cosine, sine = block_angles(number, pieces, fine, coarse)
        across = pair * sine
        turned = jnp.where(
            lane % 64 < 32, pltpu.roll(across, 96, 1), -pltpu.roll(across, 32, 1)
        )
        pair = pair * cosine + turned
        values = value_sum[here, :]
        keys_stay = core[0] == 0
        keep = jnp.where((lane < 64) | keys_stay, pair, values)
        send = jnp.where(lane < 64, 0.0, jnp.where(keys_stay, values, pair)).astype(jnp.bfloat16)
        for n, one in enumerate(storage(number)):
            keep_out[one, :] = keep[n * 64 : (n + 1) * 64, :]
            send_out[one, :] = send[n * 64 : (n + 1) * 64, :]
        return carry

    lax.fori_loop(0, rows // block, finish, 0)


def expert_rows(
    where, rows, grad, up_weight, down_weight,
    copy_out, result_out, activation_out, pair_out, pre_out,
):
    f32, bf16 = jnp.float32, jnp.bfloat16
    width = grad.shape[3]
    count = rows.shape[0]
    expert = where[0]
    extra = rows[:, width:].astype(f32)
    lane = lane_of((count, EXTRA))
    gate = jnp.sum(
        jnp.where((lane == expert) | (lane == expert + E), extra, 0.0), axis=1, keepdims=True
    )
    before = jnp.dot(rows[:, :width], up_weight[...], preferred_element_type=f32)
    gate_pre = before[:, :F]
    up_pre = before[:, F:]
    sigma = jax.nn.sigmoid(gate_pre)
    swish = gate_pre * sigma
    activation = (swish * up_pre).astype(bf16)
    activation_out[...] = activation
    result = jnp.dot(activation, down_weight[...], preferred_element_type=f32).astype(bf16)
    result = result.astype(f32)
    grads = grad[...].reshape(count, width).astype(f32)
    grad_gate = jnp.sum(grads * result, axis=1, keepdims=True)
    result_out[...] = (gate * result).astype(bf16)
    pair = (gate * grads).astype(bf16)
    pair_out[...] = pair
    grad_activation = lax.dot_general(
        pair, down_weight[...], (((1,), (1,)), ((), ())), preferred_element_type=f32
    )
    pre_out[:, :F] = (
        grad_activation * up_pre * sigma * (1.0 + gate_pre * (1.0 - sigma))
    ).astype(bf16)
    pre_out[:, F:] = (grad_activation * swish).astype(bf16)
    copy_out[:, :width] = lax.dot_general(
        pre_out[...], up_weight[...], (((1,), (1,)), ((), ())), preferred_element_type=f32
    ).astype(bf16)
    high = grad_gate.astype(bf16).astype(f32)
    copy_out[:, width:] = jnp.where(
        lane == expert, high, jnp.where(lane == expert + E, grad_gate - high, 0.0)
    ).astype(bf16)


def expert_call(half, where, rows, grads, up_weight, down_weight):
    count, full = rows.shape
    width = grads.shape[3]
    steps = 2
    block = count // steps
    bf16 = jnp.bfloat16
    row_spec = lambda columns: pl.BlockSpec((block, columns), lambda i, w: (i, 0))
    whole = lambda a: pl.BlockSpec(a.shape, lambda i, w: (0, 0), pipeline_mode=pl.Buffered(1))
    columns = (full, width, F, width, 2 * F)
    return pl.pallas_call(
        expert_rows,
        out_shape=[jax.ShapeDtypeStruct((count, n), bf16) for n in columns],
        grid_spec=pltpu.PrefetchScalarGridSpec(
            num_scalar_prefetch=1,
            grid=(steps,),
            in_specs=[
                row_spec(full),
                pl.BlockSpec((16 // steps, 1, MOST, width), lambda i, w: (i, half, 0, 0)),
                whole(up_weight),
                whole(down_weight),
            ],
            out_specs=[row_spec(n) for n in columns],
        ),
        compiler_params=pltpu.CompilerParams(vmem_limit_bytes=60 << 20),
    )(where, rows, grads, up_weight, down_weight)


def assemble(
    core, first_own, first_next, second_own, second_next, qkv_out, out_out, beside_out, gain_out
):
    f32 = jnp.float32
    even_own = core[0] == 0
    total = jnp.zeros((16, 128), f32)
    for pair in range(8):
        for own, following, rows, at in (
            (first_own, first_next, 400, 0), (second_own, second_next, 112, 400),
        ):
            mine = own[pair, :rows, :].astype(f32)
            other = following[pair, :rows, :].astype(f32)
            left = jnp.where(even_own, mine, other)
            right = jnp.where(even_own, other, mine)
            here = slice(at, at + rows)
            qkv_out[here, pair * 128 : (pair + 1) * 128] = jnp.concatenate(
                [left[:, :64], right[:, :64]], 1
            )
            qkv_out[here, 1024 + pair * 64 : 1024 + (pair + 1) * 64] = left[:, 64:]
            qkv_out[here, 1536 + pair * 64 : 1536 + (pair + 1) * 64] = right[:, 64:]
        mine = second_own[pair, 112:, :].astype(f32)
        other = second_next[pair, 112:, :].astype(f32)
        for odd in range(2):
            rest = jnp.where(even_own == (odd == 0), mine, other)
            at = odd * 256 + (pair & 1) * 128 + ((pair >> 1) & 1) * 64 + (pair >> 2) * 32
            for part in range(8):
                out_out[at : at + 32, part * 128 : (part + 1) * 128] = rest[
                    part * 32 : part * 32 + 32, :
                ]
            beside_out[at : at + 32, :] = rest[256:288, :]
            total = total + rest[288:304, :]
    gain_out[...] = total[:8, :] + total[8:, :]


def whole_call(kernel, scalars, outs, scratch, vmem):
    def run(*operands):
        spec = pl.BlockSpec(memory_space=pltpu.VMEM)
        return pl.pallas_call(
            kernel,
            out_shape=outs,
            grid_spec=pltpu.PrefetchScalarGridSpec(
                num_scalar_prefetch=scalars,
                grid=(),
                in_specs=[spec] * (len(operands) - scalars),
                out_specs=[spec] * len(outs),
                scratch_shapes=scratch,
            ),
            compiler_params=pltpu.CompilerParams(vmem_limit_bytes=vmem),
        )(*operands)

    return run


def fast_shards(
    hidden_in, block_order, segment_ids, cotangent, attn_gain, query_key_value_weight,
    w_out, ffn_gain, w_router, routes, expert_in, expert_out,
):
    bf16, f32 = jnp.bfloat16, jnp.float32
    rows = hidden_in.shape[1]
    width = hidden_in.shape[2]
    length = rows * 16
    capacity = length * TOPK * 9 // (8 * E)
    ia, ib, ic, idd, jf = (lax.axis_index(name) for name in EVERY)
    mine = ia * 8 + ib * 4 + ic * 2 + idd
    expert = jf * 16 + mine
    low_half = jf == 0

    inputs = hidden_in[0].astype(f32)
    scale_one = rms_scale(inputs)
    norm_one = inputs * scale_one
    gain_one_f = join(attn_gain, "f").astype(f32)
    h_one = (norm_one * gain_one_f).astype(bf16)

    (
        h_one, block_order, segment_ids, query_key_value_weight, w_out, ffn_gain, w_router,
        expert_in, expert_out,
    ) = together(
        h_one, block_order, segment_ids, query_key_value_weight, w_out, ffn_gain, w_router,
        expert_in, expert_out,
    )
    both = gather_step(spread(h_one), "a")

    def columns_of(start, number, low_first):
        pair = lax.dynamic_slice_in_dim(query_key_value_weight, start + number * 128, 128, 1)
        return jnp.where(low_first, pair[:, :64], pair[:, 64:])

    my_columns = jnp.concatenate(
        [
            columns_of(0, mine // 2, idd == 0),
            columns_of(1024, mine // 4, ic == 0),
            columns_of(1536, mine // 4, ic == 0),
            jnp.zeros((512, 64), bf16),
        ],
        1,
    )
    other_columns = swap(my_columns, "f")

    route = routes[0]
    named = jnp.any(route[:, :, None] == jnp.arange(E, dtype=jnp.int32)[None, None, :], axis=1)
    counts = spread(jnp.sum(named.astype(f32), axis=0, keepdims=True))
    named_b = named.astype(bf16)
    earlier = (jnp.arange(rows)[:, None] > jnp.arange(rows)[None, :]).astype(bf16)
    rank = jnp.dot(earlier, named_b, preferred_element_type=f32)
    row_of = jnp.where(named, rank, -1.0)
    counts = gather_step(counts, "a")
    expert_weights = jnp.concatenate([expert_in, expert_out], 1)
    both, row_of, cotangent, counts, expert_weights = together(
        both, row_of, cotangent, counts, expert_weights
    )
    low = gather_step(both[..., :512], "b")
    high = gather_step(both[..., 512:], "c")
    other_row_of = swap(row_of, "a")
    other_cotangent = swap(cotangent[0], "a")
    counts = gather_step(counts, "c")

    def picks(rows_of):
        half = rows_of.reshape(rows, 2, 2, 8)
        half = jnp.where(ia == 0, half[:, :, 0], half[:, :, 1])
        half = half.transpose(2, 1, 0).reshape(16, 1, rows)
        return (half == jnp.arange(MOST, dtype=f32)[None, :, None]).astype(bf16)

    def build_rows(choice, tokens):
        return lax.dot_general(
            choice, tokens, (((2,), (0,)), ((), ())), preferred_element_type=f32
        ).astype(bf16)

    def exchange(sent):
        return lax.all_to_all(sent, HALF, split_axis=0, concat_axis=0, tiled=True)

    low, high, other_columns, counts = together(low, high, other_columns, counts)
    low = gather_step(low, "c")
    high = gather_step(high, "b")
    out_part = share_swap(w_out)
    other_gain_two = swap(ffn_gain, "f")
    other_router = swap(w_router, "f")
    low, high, other_cotangent, other_row_of, expert_weights, out_part = together(
        low, high, other_cotangent, other_row_of, expert_weights, out_part
    )
    low_own = low.reshape(length // 2, 512)
    high_own = high.reshape(length // 2, 512)
    low_next = swap(low_own, "d")
    high_next = swap(high_own, "d")
    expert_weights = lax.all_to_all(
        expert_weights, CTX, split_axis=0, concat_axis=0, tiled=True
    )
    counts = gather_step(gather_step(counts, "d"), "b")
    head_weight = in_order(my_columns, other_columns, "f", 0)

    order = block_order[0]
    blocks = order.shape[0]
    place = jnp.sum(
        jnp.where(order[None, :] == jnp.arange(blocks, dtype=jnp.int32)[:, None],
                  jnp.arange(blocks, dtype=jnp.int32)[None, :], 0),
        axis=1,
    )
    document = segment_ids[0]
    start = jnp.sum((document[:, None] < document[None, :]).astype(jnp.int32), axis=0)
    first_key = start[::QUERY_BLOCK] // QUERY_BLOCK
    start = start[None, :]
    steps = jnp.arange(HEAD_SIZE // 2, dtype=f32)
    frequency = jnp.power(THETA, -2.0 * steps / HEAD_SIZE)
    angle_a = (jnp.arange(length // 64, dtype=f32) * 64.0)[:, None] * frequency[None, :]
    angle_b = jnp.arange(64, dtype=f32)[:, None] * frequency[None, :]
    coarse = jnp.tile(jnp.stack([jnp.cos(angle_a), jnp.sin(angle_a)]), (1, 1, 4))
    fine = jnp.tile(jnp.stack([jnp.cos(angle_b), jnp.sin(angle_b)]), (1, 1, 4))
    storage = jnp.arange(blocks, dtype=jnp.int32)
    held = (((storage // 2) % 2) ^ idd) * (blocks // 2) + (storage // 4) * 2 + storage % 2
    h_place = jnp.sum(jnp.where(place[:, None] == storage[None, :], held[None, :], 0), axis=1)
    storage = jnp.arange(blocks, dtype=jnp.int32)
    held = (((storage // 2) % 2) ^ idd) * (blocks // 2) + (storage // 4) * 2 + storage % 2
    h_place = jnp.sum(jnp.where(place[:, None] == storage[None, :], held[None, :], 0), axis=1)
    head_weight, out_part, other_gain_two, other_router, query_key_value_weight = together(
        head_weight, out_part, other_gain_two, other_router, query_key_value_weight
    )
    weight_part = share_swap(query_key_value_weight)
    query, key, value, mixed, attended_head = whole_call(
        attention_forward,
        3,
        [
            jax.ShapeDtypeStruct((length, 128), bf16),
            jax.ShapeDtypeStruct((length, 128), bf16),
            jax.ShapeDtypeStruct((length, 128), bf16),
            jax.ShapeDtypeStruct((72, length), f32),
            jax.ShapeDtypeStruct((length, 64), bf16),
        ],
        [pltpu.VMEM((128, length), bf16)],
        60 << 20,
    )(
        place, h_place, first_key, low_own, high_own, low_next, high_next, head_weight, fine,
        coarse, start,
    )

    def to_tokens(value_heads):
        return lax.all_to_all(
            value_heads.reshape(16, rows, -1), CTX, split_axis=0, concat_axis=0, tiled=True
        )

    pick_mine = picks(row_of)
    pick_other = picks(other_row_of)
    grad_rows = jnp.concatenate(
        [build_rows(pick_mine, cotangent[0]), build_rows(pick_other, other_cotangent)], 1
    )
    out_full = share_join(w_out, out_part)
    gain_two_f = in_order(ffn_gain, other_gain_two, "f", 0).astype(f32)
    router_full = in_order(w_router, other_router, "f", 0)
    attended_head, expert_weights, grad_rows, out_full, weight_part = together(
        attended_head, expert_weights, grad_rows, out_full, weight_part
    )
    attended = to_tokens(attended_head)
    weight_full = share_join(query_key_value_weight, weight_part)
    attended, grad_rows, counts = together(attended, grad_rows, counts)
    grad_rows = exchange(grad_rows)
    attended = attended.transpose(1, 0, 2).reshape(rows, 1024)
    middle_state = inputs + jnp.dot(attended, out_full, preferred_element_type=f32)
    scale_two = rms_scale(middle_state)
    norm_two = middle_state * scale_two
    h_two = (norm_two * gain_two_f).astype(bf16)
    logits = jnp.dot(h_two, router_full, preferred_element_type=f32)
    top = jnp.max(jnp.where(named, logits, MASK_FILL_VALUE), axis=-1, keepdims=True)
    weights = jnp.where(named, jnp.exp(logits - top), 0.0)
    gates = weights / jnp.sum(weights, axis=-1, keepdims=True)
    passed = (jnp.arange(16)[:, None] < mine).astype(f32)
    offset = jnp.sum(counts.reshape(16, E) * passed, axis=0, keepdims=True)
    kept = (named & (rank + offset < capacity)).astype(f32)
    extended = jnp.concatenate(
        [h_two] + two_parts(gates * kept) + [jnp.zeros((rows, 2 * E), bf16)], 1
    )
    other_extended = swap(extended, "a")
    rows_mine = build_rows(pick_mine, extended)
    rows_mine, grad_rows, weight_full, other_extended = together(
        rows_mine, grad_rows, weight_full, other_extended
    )
    rows_mine = exchange(rows_mine)
    up_weight = expert_weights[:, :64].reshape(width, 2 * F)
    down_weight = expert_weights[:, 64:].reshape(F, width)
    grad_rows = grad_rows.reshape(16, 2, MOST, width)
    rows_other = build_rows(pick_other, other_extended)
    rows_mine, rows_other, up_weight, down_weight = together(
        rows_mine, rows_other, up_weight, down_weight
    )
    rows_other = exchange(rows_other)
    rows_mine = rows_mine.reshape(16 * MOST, width + EXTRA)
    number = expert.astype(jnp.int32)[None]
    copy_mine, result_mine, act_mine, pair_mine, pre_mine = expert_call(
        0, number, rows_mine, grad_rows, up_weight, down_weight
    )
    rows_other, copy_mine = together(rows_other, copy_mine)
    rows_other = rows_other.reshape(16 * MOST, width + EXTRA)
    copy_other, result_other, act_other, pair_other, pre_other = expert_call(
        1, number, rows_other, grad_rows, up_weight, down_weight
    )

    def sum_rows(choice, got):
        return lax.dot_general(
            choice, got, (((0, 1), (0, 1)), ((), ())), preferred_element_type=f32
        )

    away = exchange(copy_other.reshape(16, MOST, width + EXTRA))
    away, copy_mine = together(away, copy_mine)
    home = exchange(copy_mine.reshape(16, MOST, width + EXTRA))
    grad_up_weight = contract_rows(rows_mine[:, :width], pre_mine) + contract_rows(
        rows_other[:, :width], pre_other
    )
    grad_down = contract_rows(act_mine, pair_mine) + contract_rows(act_other, pair_other)
    expert_grads = jnp.concatenate(
        [
            grad_up_weight.astype(bf16).reshape(16, 64, 2 * F),
            grad_down.astype(bf16).reshape(16, 32, width),
        ],
        1,
    )
    away_sum = swap(sum_rows(pick_other, away).astype(bf16), "a")
    home, away_sum, expert_grads = together(home, away_sum, expert_grads)
    back = sum_rows(pick_mine, home) + away_sum.astype(f32)

    gate_grads = (back[:, width : width + E] + back[:, width + E : width + 2 * E]) * kept
    grad_logits = gates * (gate_grads - jnp.sum(gates * gate_grads, axis=-1, keepdims=True))
    grad_h_two = back[:, :width] + lax.dot_general(
        grad_logits, router_full.astype(f32), (((1,), (1,)), ((), ())), precision=HIGHEST
    )
    grad_out = cotangent[0].astype(f32)
    scaled_two = grad_h_two * gain_two_f
    grad_mid = grad_out + scale_two * (
        scaled_two - norm_two * jnp.mean(scaled_two * norm_two, axis=-1, keepdims=True)
    )
    grad_branch = grad_mid.astype(bf16)
    attended_gradient = contract_columns(grad_branch, out_full).astype(bf16)
    grad_heads = to_tokens(attended_gradient.reshape(rows, 16, 64).transpose(1, 0, 2))
    grad_heads = grad_heads.reshape(length, 64)

    grad_router_part = lax.dot_general(
        h_two.astype(f32), grad_logits, (((0,), (0,)), ((), ())), precision=HIGHEST
    )
    grad_gain_two = jnp.sum(grad_h_two * norm_two, axis=0)
    beside = jnp.concatenate(
        [grad_router_part, grad_gain_two[:, None], jnp.zeros((width, 128 - E - 1), f32)], 1
    ).reshape(2, 2, 256, 128)
    by_core = attended.reshape(rows, 2, 2, 256)

    def rows_at(core):
        columns = lax.dynamic_slice_in_dim(by_core, core, 1, 2).reshape(rows, 512)
        others = lax.dynamic_slice_in_dim(beside, core, 1, 1).reshape(512, 128)
        return jnp.concatenate([contract_rows(columns, grad_branch), others], 1)

    out_sum = rows_at(idd)
    leaving = rows_at(1 - idd).astype(bf16)

    def halve(total, axis):
        count = total.shape[0] // 2
        index = lax.axis_index(axis)
        keep = lax.dynamic_slice_in_dim(total, index * count, count, 0)
        send = lax.dynamic_slice_in_dim(total, (1 - index) * count, count, 0)
        return keep + swap(send.astype(bf16), axis).astype(f32)

    results = jnp.concatenate(
        [result_mine.reshape(16, MOST, width), result_other.reshape(16, MOST, width)], 1
    )
    grad_heads, results = together(grad_heads, results)
    results = exchange(results)

    keep, send = whole_call(
        attention_backward,
        3,
        [jax.ShapeDtypeStruct((length, 128), f32), jax.ShapeDtypeStruct((length, 128), bf16)],
        [
            pltpu.VMEM((64, length), bf16),
            pltpu.VMEM((length, 128), f32),
            pltpu.VMEM((length, 128), f32),
        ],
        60 << 20,
    )(
        place, first_key, idd.astype(jnp.int32)[None], query, key, value, mixed, grad_heads,
        fine, coarse, start,
    )
    keep, send, out_sum, leaving = together(keep, send, out_sum, leaving)
    out_sum = out_sum + swap(leaving, "d").astype(f32)
    grad_columns = (keep + swap(send, "d").astype(f32)).astype(bf16)
    out_sum = halve(out_sum, "f")
    results, expert_grads = together(results, expert_grads)
    expert_grads = lax.all_to_all(expert_grads, CTX, split_axis=0, concat_axis=0, tiled=True)
    for axis in ("c", "b", "a"):
        out_sum = halve(out_sum, axis)
    out_rows = out_sum.reshape(32, 9, 128).transpose(1, 0, 2).reshape(288, 128).astype(bf16)

    by_core = grad_columns.reshape(8, 2, rows, 128)
    own = jnp.where(idd == 0, by_core[:, 0], by_core[:, 1]).reshape(length // 2, 128)
    following = jnp.where(idd == 0, by_core[:, 1], by_core[:, 0]).reshape(length // 2, 128)
    low_part = contract_rows(low_own, own) + contract_rows(low_next, following)
    high_part = contract_rows(high_own, own) + contract_rows(high_next, following)
    columns_grad = jnp.where(low_half, low_part, high_part) + swap(
        jnp.where(low_half, high_part, low_part), "f"
    )
    my_weight = jnp.concatenate(
        [my_columns[:, :64], jnp.where(idd == 0, my_columns[:, 64:128], my_columns[:, 128:192])], 1
    )
    gain_part = jnp.sum(columns_grad * my_weight.astype(f32), axis=1).reshape(4, 128)
    gain_part = jnp.concatenate([gain_part, jnp.zeros((4, 128), f32)], 0)
    columns_grad = jnp.concatenate(
        [columns_grad.astype(bf16), out_rows] + two_parts(gain_part), 0
    )
    gathered = gather_step(spread(columns_grad), "a")
    first = gather_step(gathered[..., :400, :], "b")
    second = gather_step(gathered[..., 400:, :], "c")
    first = gather_step(first, "c")
    second = gather_step(second, "b")
    ready, expert_grads = together(grad_columns, expert_grads)
    grad_projected = to_tokens(ready)
    grad_expert_in = expert_grads[:, :64].astype(f32)
    grad_expert_out = expert_grads[:, 64:].astype(f32)
    first, second, grad_projected = together(first, second, grad_projected)
    first = first.reshape(8, 400, 128)
    second = second.reshape(8, 416, 128)
    first_next = swap(first, "d")
    second_next = swap(second, "d")

    grad_projected = grad_projected.transpose(1, 0, 2)
    grad_kv = grad_projected[:, :, 64:].reshape(rows, 8, 2, 64)
    grad_projected = jnp.concatenate(
        [
            grad_projected[:, :, :64].reshape(rows, 1024),
            grad_kv[:, :, 0].reshape(rows, 512),
            grad_kv[:, :, 1].reshape(rows, 512),
        ],
        1,
    )
    grad_h_one = contract_columns(grad_projected, weight_full)
    scaled_one = grad_h_one * gain_one_f
    grad_inputs = grad_mid + scale_one * (
        scaled_one - norm_one * jnp.mean(scaled_one * norm_one, axis=-1, keepdims=True)
    )
    share_qkv, share_out, beside, gain_sum = whole_call(
        assemble,
        1,
        [
            jax.ShapeDtypeStruct((512, 2048), f32),
            jax.ShapeDtypeStruct((512, 1024), f32),
            jax.ShapeDtypeStruct((512, 128), f32),
            jax.ShapeDtypeStruct((8, 128), f32),
        ],
        [],
        32 << 20,
    )(idd.astype(jnp.int32)[None], first, first_next, second, second_next)
    share_router = beside[:, :E]
    share_two = beside[:, E]
    share_one = gain_sum[:4].reshape(512) / attn_gain.astype(f32)
    mixture = sum_rows(pick_mine, results[:, :MOST]) + swap(
        sum_rows(pick_other, results[:, MOST:]).astype(bf16), "a"
    ).astype(f32)
    hidden_out = (middle_state + mixture).astype(bf16)
    return (
        hidden_out[None],
        grad_inputs[None],
        share_one,
        share_qkv,
        share_out,
        share_two,
        share_router,
        grad_expert_in,
        grad_expert_out,
    )


def fast_solution(mesh):
    fine = Mesh(mesh.devices.reshape(2, 2, 2, 2, 2), EVERY)
    placed = (
        P("f", CTX, None),
        P("f", None),
        P("f", None),
        P("f", CTX, None),
        P("f"),
        P("f", None),
        P("f", None),
        P("f"),
        P("f", None),
        P("f", CTX, None),
        P("f", CTX, None),
        P("f", CTX, None),
    )
    return jax.shard_map(
        fast_shards,
        mesh=fine,
        in_specs=placed,
        out_specs=(
            P("f", CTX, None),
            P("f", CTX, None),
            P("f"),
            P("f", None),
            P("f", None),
            P("f"),
            P("f", None),
            P("f", CTX, None),
            P("f", CTX, None),
        ),
        check_vma=False,
    )


def solution(mesh):
    if mesh.shape["ctx"] == QUERY_HEADS and mesh.shape["fsdp"] * mesh.shape["ctx"] == E:
        return fast_solution(mesh)
    return general_solution(mesh)
```
